32 devices in a mesh: dp: 4 (over x, core), context: 4 (over z), tensor: 2 (over y).
Axes of the slice: x: 2, y: 2, z: 4, core: 2. Of those that a mesh axis runs over, the one named last changes fastest.
Arguments:
- tokens: bfloat16 [8, 1024, 768], P('dp', 'context'), may hold values from -6 to 6
- lengths: int32 [8], P('dp'), may hold values from 256 to 1024, as said below
- ln1_gain: bfloat16 [768], replicated, may hold values from 0.099609375 to 1.8984375
- ln1_bias: bfloat16 [768], replicated, may hold values from -2 to 2
- w_query: bfloat16 [768, 768], P('dp', 'tensor'), may hold values from -0.21875 to 0.21875
- b_query: bfloat16 [768], P('tensor'), may hold values from -3 to 3
- w_key: bfloat16 [768, 768], P('dp', 'tensor'), may hold values from -0.21875 to 0.21875
- w_value: bfloat16 [768, 768], P('dp', 'tensor'), may hold values from -0.21875 to 0.21875
- b_value: bfloat16 [768], P('tensor'), may hold values from -0.29882812 to 0.29882812
- w_out: bfloat16 [768, 768], P('tensor', 'dp'), may hold values from -1.75 to 1.75
- b_out: bfloat16 [768], replicated, may hold values from -2 to 2
- ln2_gain: bfloat16 [768], replicated, may hold values from 0.099609375 to 1.8984375
- ln2_bias: bfloat16 [768], replicated, may hold values from -2 to 2
- w_up: bfloat16 [768, 3072], P('dp', 'tensor'), may hold values from -0.21875 to 0.21875
- b_up: bfloat16 [3072], P('tensor'), may hold values from -3 to 3
- w_down: bfloat16 [3072, 768], P('tensor', 'dp'), may hold values from -0.109375 to 0.109375
- b_down: bfloat16 [768], replicated, may hold values from -2 to 2
- cotangent: bfloat16 [8, 1024, 768], P('dp', 'context'), may hold values from -6 to 6
Outputs:
- output: bfloat16 [8, 1024, 768], P('dp', 'context')
- input_grad: bfloat16 [8, 1024, 768], P('dp', 'context')
- grad_ln1_gain: float32 [768], replicated
- grad_ln1_bias: float32 [768], replicated
- grad_w_query: float32 [768, 768], P('dp', 'tensor')
- grad_b_query: float32 [768], P('tensor')
- grad_w_key: float32 [768, 768], P('dp', 'tensor')
- grad_w_value: float32 [768, 768], P('dp', 'tensor')
- grad_b_value: float32 [768], P('tensor')
- grad_w_out: float32 [768, 768], P('tensor', 'dp')
- grad_b_out: float32 [768], replicated
- grad_ln2_gain: float32 [768], replicated
- grad_ln2_bias: float32 [768], replicated
- grad_w_up: float32 [768, 3072], P('dp', 'tensor')
- grad_b_up: float32 [3072], P('tensor')
- grad_w_down: float32 [3072, 768], P('tensor', 'dp')
- grad_b_down: float32 [768], replicated
The draws below stay inside these ranges and needn't reach their ends.
Inputs may be any that keep to these rules, and one draw needn't show every extreme that they name: Sequence n holds lengths[n] real patch rows at its start, the rest is padding; at least one sequence has 1024 real rows.
All inputs are finite; a program needn't handle non-finite values.
Results may differ from the reference program's by a relative error of at most 0.035.
Values may be sent and summed in bfloat16 or wider, within the bound.
No kernel may reach another device: no remote copies, remote signals or barrier semaphores. Data moves between devices by JAX's collectives and lax.ppermute only.
A program may use at most 192 MiB of HBM per device.

```python
from functools import partial
import jax
import jax.numpy as jnp
from jax import lax

D = 768
HEADS = 12
HEAD_DIM = 64
FF = 3072
LEN = 1024
NSEQ = 8


def draw_lengths(key, part):
    first, second = jax.random.split(key)
    drawn = jax.random.randint(first, (NSEQ,), LEN // 4, LEN + 1)
    chosen = jax.random.randint(second, (), 0, NSEQ)
    return jnp.where(jnp.arange(NSEQ) == chosen, LEN, drawn).astype(jnp.int32)


def block_scale(stream_key, shape, cuts, smallest, top_value):
    level = 1.0
    for dim, parts in cuts:
        steps = jax.random.uniform(jax.random.fold_in(jax.random.fold_in(stream_key, 6), dim), (parts,), jnp.float32, smallest / len(cuts), top_value / len(cuts))
        level = level * jnp.repeat(jnp.exp(steps), shape[dim] // parts).reshape((-1,) + (1,) * (len(shape) - 1 - dim))
    return level


def normal_values(stream_key, shape, scale, most, pieces=(), kind=jnp.bfloat16):
    values = scale * jax.random.normal(stream_key, shape, jnp.float32)
    if pieces:
        values = values * block_scale(stream_key, shape, pieces, -0.22, 0.18)
    return jnp.clip(values, -most, most).astype(kind)


def setup_inputs(seed: int = 0) -> dict:
    key_of = jax.random.split(jax.random.key(seed), 19)
    tokens = normal_values(key_of[0], (NSEQ, LEN, D), 1.0, 6.0, ((0, 4), (1, 4)))
    lengths = draw_lengths(jax.random.fold_in(key_of[18], 71), 0)
    ln1_gain = jnp.clip(1.0 + 0.18 * jax.random.normal(key_of[2], (D,), jnp.float32), 0.099609375, 1.8984375).astype(jnp.bfloat16)
    ln1_bias = normal_values(key_of[3], (D,), 0.3, 2.0)
    w_query = normal_values(key_of[4], (D, D), D ** -0.5, 0.21875, ((0, 4), (1, 2)))
    b_query = normal_values(key_of[5], (D,), 0.5, 3.0, ((0, 2),))
    w_key = normal_values(key_of[6], (D, D), D ** -0.5, 0.21875, ((0, 4), (1, 2)))
    w_value = normal_values(key_of[7], (D, D), D ** -0.5, 0.21875, ((0, 4), (1, 2)))
    b_value = normal_values(key_of[8], (D,), 0.05, 0.29882812, ((0, 2),))
    w_out = normal_values(key_of[9], (D, D), (max(D // 64, 1)) ** -0.5, 1.75, ((0, 2), (1, 4)))
    b_out = normal_values(key_of[10], (D,), 0.3, 2.0)
    ln2_gain = jnp.clip(1.0 + 0.18 * jax.random.normal(key_of[11], (D,), jnp.float32), 0.099609375, 1.8984375).astype(jnp.bfloat16)
    ln2_bias = normal_values(key_of[12], (D,), 0.3, 2.0)
    w_up = normal_values(key_of[13], (D, FF), D ** -0.5, 0.21875, ((0, 4), (1, 2)))
    b_up = normal_values(key_of[14], (FF,), 0.5, 3.0, ((0, 2),))
    w_down = normal_values(key_of[15], (FF, D), FF ** -0.5, 0.109375, ((0, 2), (1, 4)))
    b_down = normal_values(key_of[16], (D,), 0.3, 2.0)
    cotangent = normal_values(key_of[17], (NSEQ, LEN, D), 1.0, 6.0, ((0, 4), (1, 4)))
    return dict(tokens=tokens, lengths=lengths, ln1_gain=ln1_gain, ln1_bias=ln1_bias, w_query=w_query, b_query=b_query, w_key=w_key, w_value=w_value, b_value=b_value, w_out=w_out, b_out=b_out, ln2_gain=ln2_gain, ln2_bias=ln2_bias, w_up=w_up, b_up=b_up, w_down=w_down, b_down=b_down, cotangent=cotangent)


@jax.custom_vjp
def low(v):
    return lax.optimization_barrier(v.astype(jnp.bfloat16)).astype(jnp.float32)

@jax.custom_vjp
def low_back(v):
    return v

def low_keep(v):
    return (low(v), None)

def low_pass(kept, grad):
    return (grad,)

def back_keep(v):
    return (v, None)

def back_low(kept, grad):
    return (low(grad),)
low.defvjp(low_keep, low_pass)
low_back.defvjp(back_keep, back_low)
epsilon = 1e-06
masked_value = -1e+30

def matmul_high(left, right):
    return jnp.dot(left, right, precision=lax.Precision.HIGHEST)

def norm_rows(values, gain_vec, bias_vec):
    average = lax.optimization_barrier(jnp.mean(values, axis=-1, keepdims=True))
    centred = values - average
    spread = lax.optimization_barrier(jnp.mean(centred * centred, axis=-1, keepdims=True))
    return centred * lax.rsqrt(spread + epsilon) * gain_vec + bias_vec

def one_head(valid, triple):
    head_query, head_keys, head_values = triple
    scores = low_back(matmul_high(head_query, head_keys.T) * HEAD_DIM ** (-0.5))
    masked = jnp.where(valid[None, :], scores, masked_value)
    weights = jax.nn.softmax(masked, axis=-1)
    return matmul_high(low(weights), head_values)

def split_heads(matrix):
    return matrix.reshape(LEN, HEADS, HEAD_DIM).transpose(1, 0, 2)

def seq_forward(seq_rows, seq_length, params):
    gain_one, bias_one, query_weight, query_bias, key_weight, value_weight, value_bias, out_weight, out_bias, gain_two, bias_two, up_weight, up_bias, down_weight, down_bias = params
    places = jnp.arange(LEN, dtype=jnp.int32)
    valid = places < seq_length
    keep = valid.astype(jnp.float32)[:, None]
    normed = low(norm_rows(seq_rows, gain_one, bias_one))
    queries = low_back(low(matmul_high(normed, query_weight) + query_bias))
    keys_all = low_back(low(matmul_high(normed, key_weight)))
    values_all = low_back(low(matmul_high(normed, value_weight) + value_bias))
    per_head = lax.map(jax.checkpoint(partial(one_head, valid)), (split_heads(queries), split_heads(keys_all), split_heads(values_all)))
    context_out = low_back(low(per_head.transpose(1, 0, 2).reshape(LEN, D)))
    attention = low_back(matmul_high(context_out, out_weight) + out_bias)
    middle = seq_rows + keep * attention
    normed_two = low(norm_rows(middle, gain_two, bias_two))
    hidden_pre = low_back(matmul_high(normed_two, up_weight) + up_bias)
    hidden = low(jax.nn.gelu(hidden_pre, approximate=True))
    feed = low_back(matmul_high(hidden, down_weight) + down_bias)
    return middle + keep * feed

def reference(tokens, lengths, ln1_gain, ln1_bias, w_query, b_query, w_key, w_value, b_value, w_out, b_out, ln2_gain, ln2_bias, w_up, b_up, w_down, b_down, cotangent):
    params = tuple((member.astype(jnp.float32) for member in (ln1_gain, ln1_bias, w_query, b_query, w_key, w_value, b_value, w_out, b_out, ln2_gain, ln2_bias, w_up, b_up, w_down, b_down)))
    run_seq = jax.checkpoint(seq_forward)

    def forward(rows_in, weights_in):
        return lax.map(lambda couple: run_seq(couple[0], couple[1], weights_in), (rows_in, lengths))
    result, pull = jax.vjp(forward, tokens.astype(jnp.float32), params)
    grad_rows, grads = pull(cotangent.astype(jnp.float32))
    return (result.astype(jnp.bfloat16), grad_rows.astype(jnp.bfloat16), grads[0], grads[1], grads[2], grads[3], grads[4], grads[5], grads[6], grads[7], grads[8], grads[9], grads[10], grads[11], grads[12], grads[13], grads[14])
```

```python
import jax
import jax.numpy as jnp
from jax import lax
from jax.sharding import PartitionSpec as P

HEAD_DIM = 64


epsilon = 1e-06
masked_value = -1e30


def norm_rows(values, gain_vec, bias_vec):
    average = jnp.mean(values, axis=-1, keepdims=True)
    centred = values - average
    spread = jnp.mean(centred * centred, axis=-1, keepdims=True)
    return centred * lax.rsqrt(spread + epsilon) * gain_vec + bias_vec


def gelu_tanh(values):
    return jax.nn.gelu(values, approximate=True)


def dense(left, right):
    return jnp.dot(left, right, preferred_element_type=jnp.float32)


def dense_tn(left, right):
    return lax.dot_general(
        left, right, (((0,), (0,)), ((), ())), preferred_element_type=jnp.float32
    )


def dense_nt(left, right):
    return lax.dot_general(
        left, right, (((1,), (1,)), ((), ())), preferred_element_type=jnp.float32
    )


def per_device_general(
    tokens,
    lengths,
    ln1_gain,
    ln1_bias,
    w_query,
    b_query,
    w_key,
    w_value,
    b_value,
    w_out,
    b_out,
    ln2_gain,
    ln2_bias,
    w_up,
    b_up,
    w_down,
    b_down,
    cotangent,
):
    seq_count, shard_rows, width = tokens.shape
    full_len = shard_rows * lax.axis_size("context")
    local_width = w_query.shape[1]
    local_heads = local_width // HEAD_DIM
    scale = HEAD_DIM ** (-0.5)
    row_count = seq_count * shard_rows
    query_weight, key_weight, value_weight, up_weight, out_weight, down_weight = (
        lax.all_gather(w_query, "dp", axis=0, tiled=True),
        lax.all_gather(w_key, "dp", axis=0, tiled=True),
        lax.all_gather(w_value, "dp", axis=0, tiled=True),
        lax.all_gather(w_up, "dp", axis=0, tiled=True),
        lax.all_gather(w_out, "dp", axis=1, tiled=True),
        lax.all_gather(w_down, "dp", axis=1, tiled=True),
    )
    gain_one = ln1_gain.astype(jnp.float32)
    bias_one = ln1_bias.astype(jnp.float32)
    query_bias = b_query.astype(jnp.float32)
    value_bias = b_value.astype(jnp.float32)
    out_bias = b_out.astype(jnp.float32)
    gain_two = ln2_gain.astype(jnp.float32)
    bias_two = ln2_bias.astype(jnp.float32)
    up_bias = b_up.astype(jnp.float32)
    down_bias = b_down.astype(jnp.float32)
    places = lax.axis_index("context") * shard_rows + jnp.arange(shard_rows, dtype=jnp.int32)
    keep = (places[None, :] < lengths[:, None]).astype(jnp.float32).reshape(row_count, 1)
    key_places = jnp.arange(full_len, dtype=jnp.int32)
    rows_in = tokens.reshape(row_count, width).astype(jnp.float32)
    normed_one, pull_one = jax.vjp(norm_rows, rows_in, gain_one, bias_one)
    normed_low = normed_one.astype(jnp.bfloat16)
    queries = (dense(normed_low, query_weight) + query_bias).astype(jnp.bfloat16)
    keys_own = dense(normed_low, key_weight).astype(jnp.bfloat16)
    values_own = (dense(normed_low, value_weight) + value_bias).astype(jnp.bfloat16)
    keys_whole, values_whole = (
        lax.all_gather(
            keys_own.reshape(seq_count, shard_rows, local_width), "context", axis=1, tiled=True
        ),
        lax.all_gather(
            values_own.reshape(seq_count, shard_rows, local_width), "context", axis=1, tiled=True
        ),
    )
    query_heads = queries.reshape(seq_count, shard_rows, local_heads, HEAD_DIM)
    head_outs = []
    log_sums = []
    for member in range(seq_count):
        key_heads = keys_whole[member].reshape(full_len, local_heads, HEAD_DIM)
        value_heads = values_whole[member].reshape(full_len, local_heads, HEAD_DIM)
        raw_scores = (
            jnp.einsum(
                "qhd,khd->hqk", query_heads[member], key_heads, preferred_element_type=jnp.float32
            )
            * scale
        )
        live = (key_places < lengths[member])[None, None, :]
        masked = jnp.where(live, raw_scores, masked_value)
        largest = jnp.max(masked, axis=-1, keepdims=True)
        log_total = largest + jnp.log(jnp.sum(jnp.exp(masked - largest), axis=-1, keepdims=True))
        probs_low = jnp.exp(masked - log_total).astype(jnp.bfloat16)
        mixed_heads = jnp.einsum(
            "hqk,khd->qhd", probs_low, value_heads, preferred_element_type=jnp.float32
        )
        head_outs.append(mixed_heads.reshape(shard_rows, local_width))
        log_sums.append(log_total)
    context_low = jnp.concatenate(head_outs, axis=0).astype(jnp.bfloat16)
    attention = (
        lax.psum(dense(context_low, out_weight).astype(jnp.bfloat16), "tensor").astype(jnp.float32)
        + out_bias
    )
    middle = rows_in + keep * attention
    normed_two, pull_two = jax.vjp(norm_rows, middle, gain_two, bias_two)
    normed_two_low = normed_two.astype(jnp.bfloat16)
    hidden_pre = dense(normed_two_low, up_weight) + up_bias
    hidden, pull_gelu = jax.vjp(gelu_tanh, hidden_pre)
    hidden_low = hidden.astype(jnp.bfloat16)
    feed = (
        lax.psum(dense(hidden_low, down_weight).astype(jnp.bfloat16), "tensor").astype(jnp.float32)
        + down_bias
    )
    output = (middle + keep * feed).astype(jnp.bfloat16).reshape(tokens.shape)
    grad_top = cotangent.reshape(row_count, width).astype(jnp.float32)
    d_feed = (keep * grad_top).astype(jnp.bfloat16)
    grad_down_bias = jnp.sum(d_feed.astype(jnp.float32), axis=0)
    grad_down = dense_tn(hidden_low, d_feed)
    d_hidden = dense_nt(d_feed, down_weight)
    d_pre = pull_gelu(d_hidden)[0].astype(jnp.bfloat16)
    grad_up_bias = jnp.sum(d_pre.astype(jnp.float32), axis=0)
    grad_up = dense_tn(normed_two_low, d_pre)
    d_normed_two = lax.psum(dense_nt(d_pre, up_weight).astype(jnp.bfloat16), "tensor").astype(
        jnp.float32
    )
    d_middle, grad_gain_two, grad_bias_two = pull_two(d_normed_two)
    d_middle = d_middle + grad_top
    d_attention = (keep * d_middle).astype(jnp.bfloat16)
    grad_out_bias = jnp.sum(d_attention.astype(jnp.float32), axis=0)
    grad_out = dense_tn(context_low, d_attention)
    d_context = dense_nt(d_attention, out_weight).astype(jnp.bfloat16)
    back_keys, back_values = (keys_whole, values_whole)
    d_context_heads = d_context.reshape(seq_count, shard_rows, local_heads, HEAD_DIM)
    query_grads = []
    own_grads = []
    inner_rows = []
    for member in range(seq_count):
        key_heads = back_keys[member].reshape(full_len, local_heads, HEAD_DIM)
        value_heads = back_values[member].reshape(full_len, local_heads, HEAD_DIM)
        raw_scores = (
            jnp.einsum(
                "qhd,khd->hqk", query_heads[member], key_heads, preferred_element_type=jnp.float32
            )
            * scale
        )
        live = (key_places < lengths[member])[None, None, :]
        probs = jnp.where(live, jnp.exp(raw_scores - log_sums[member]), 0.0)
        d_probs = jnp.einsum(
            "qhd,khd->hqk", d_context_heads[member], value_heads, preferred_element_type=jnp.float32
        )
        inner = jnp.sum(probs * d_probs, axis=-1, keepdims=True)
        d_scores = (probs * (d_probs - inner)).astype(jnp.bfloat16)
        d_query = (
            jnp.einsum("hqk,khd->qhd", d_scores, key_heads, preferred_element_type=jnp.float32)
            * scale
        )
        query_grads.append(d_query.reshape(shard_rows, local_width))
        inner_rows.append(inner[:, :, 0])
        d_keys = (
            jnp.einsum(
                "hqk,qhd->khd", d_scores, query_heads[member], preferred_element_type=jnp.float32
            )
            * scale
        )
        d_values = jnp.einsum(
            "hqk,qhd->khd",
            probs.astype(jnp.bfloat16),
            d_context_heads[member],
            preferred_element_type=jnp.float32,
        )
        key_term = jnp.concatenate(
            [d_keys.reshape(full_len, local_width), d_values.reshape(full_len, local_width)], axis=1
        )
        own_grads.append(
            lax.psum_scatter(
                key_term.astype(jnp.bfloat16), "context", scatter_dimension=0, tiled=True
            ).astype(jnp.float32)
        )
    d_query_low = jnp.concatenate(query_grads, axis=0).astype(jnp.bfloat16)
    key_value_grads = jnp.concatenate(own_grads, axis=0)
    d_keys_low = key_value_grads[:, :local_width].astype(jnp.bfloat16)
    d_values_low = key_value_grads[:, local_width:].astype(jnp.bfloat16)
    grad_query = dense_tn(normed_low, d_query_low)
    grad_query_bias = jnp.sum(d_query_low.astype(jnp.float32), axis=0)
    grad_key = dense_tn(normed_low, d_keys_low)
    grad_value = dense_tn(normed_low, d_values_low)
    grad_value_bias = jnp.sum(d_values_low.astype(jnp.float32), axis=0)
    d_normed_one = lax.psum(
        (
            dense_nt(d_query_low, query_weight)
            + dense_nt(d_keys_low, key_weight)
            + dense_nt(d_values_low, value_weight)
        ).astype(jnp.bfloat16),
        "tensor",
    ).astype(jnp.float32)
    d_rows, grad_gain_one, grad_bias_one = pull_one(d_normed_one)
    input_grad = (d_rows + d_middle).astype(jnp.bfloat16).reshape(tokens.shape)
    data_sums = (
        lax.psum_scatter(
            grad_query.astype(jnp.bfloat16), "dp", scatter_dimension=0, tiled=True
        ).astype(jnp.float32),
        lax.psum_scatter(
            grad_key.astype(jnp.bfloat16), "dp", scatter_dimension=0, tiled=True
        ).astype(jnp.float32),
        lax.psum_scatter(
            grad_value.astype(jnp.bfloat16), "dp", scatter_dimension=0, tiled=True
        ).astype(jnp.float32),
        lax.psum_scatter(
            grad_up.astype(jnp.bfloat16), "dp", scatter_dimension=0, tiled=True
        ).astype(jnp.float32),
        lax.psum_scatter(
            grad_out.astype(jnp.bfloat16), "dp", scatter_dimension=1, tiled=True
        ).astype(jnp.float32),
        lax.psum_scatter(
            grad_down.astype(jnp.bfloat16), "dp", scatter_dimension=1, tiled=True
        ).astype(jnp.float32),
    )
    owned_sums = (
        lax.psum(data_sums[0].astype(jnp.bfloat16), "context").astype(jnp.float32),
        lax.psum(data_sums[1].astype(jnp.bfloat16), "context").astype(jnp.float32),
        lax.psum(data_sums[2].astype(jnp.bfloat16), "context").astype(jnp.float32),
        lax.psum(data_sums[3].astype(jnp.bfloat16), "context").astype(jnp.float32),
        lax.psum(data_sums[4].astype(jnp.bfloat16), "context").astype(jnp.float32),
        lax.psum(data_sums[5].astype(jnp.bfloat16), "context").astype(jnp.float32),
    )
    small_sums = lax.psum(
        (
            grad_gain_one,
            grad_bias_one,
            grad_query_bias,
            grad_value_bias,
            grad_out_bias,
            grad_gain_two,
            grad_bias_two,
            grad_up_bias,
            grad_down_bias,
        ),
        ("dp", "context"),
    )
    return (
        output,
        input_grad,
        small_sums[0],
        small_sums[1],
        owned_sums[0],
        small_sums[2],
        owned_sums[1],
        owned_sums[2],
        small_sums[3],
        owned_sums[4],
        small_sums[4],
        small_sums[5],
        small_sums[6],
        owned_sums[3],
        small_sums[7],
        owned_sums[5],
        small_sums[8],
    )


def exchange(value, bit):
    size = lax.axis_size("dp")
    return lax.ppermute(value, "dp", [(i, i ^ bit) for i in range(size)])


def swap_tensor(value):
    return lax.ppermute(value, "tensor", [(0, 1), (1, 0)])


def route(value, step, inward):
    pairs = []
    for far in range(2):
        for near in range(2):
            for plane in range(4):
                home = (2 * far + near) * 4 + plane
                away = (2 * far + plane // 2) * 4 + 2 * near + (step ^ (plane % 2))
                pairs.append((away, home) if inward else (home, away))
    return lax.ppermute(value, ("dp", "context"), pairs)


def reroute(pair, odd, inward):
    first = route(jnp.where(odd, pair[1], pair[0]), 0, inward)
    second = route(jnp.where(odd, pair[0], pair[1]), 1, inward)
    return jnp.stack([jnp.where(odd, second, first), jnp.where(odd, first, second)])


def gather_rows(shard, place):
    rows = shard.shape[0]
    across = exchange(shard, 2)
    parts = (shard, exchange(shard, 1), across, exchange(across, 1))
    whole = jnp.zeros((4 * rows, shard.shape[1]), shard.dtype)
    for step, part in enumerate(parts):
        whole = lax.dynamic_update_slice(whole, part, ((place ^ step) * rows, 0))
    return whole


def scatter_rows(grad, far, near):
    rows = grad.shape[0] // 4
    blocks = grad.astype(jnp.bfloat16).reshape(2, 2, rows, grad.shape[1])
    take = lambda array, axis, index: lax.dynamic_index_in_dim(array, index, axis, False)
    chip = take(blocks, 1, near) + exchange(take(blocks, 1, 1 - near), 1)
    return take(chip, 0, far) + exchange(take(chip, 0, 1 - far), 2)


def sum_planes(value, plane):
    inner = value + lax.ppermute(value, "context", [(0, 1), (3, 2)])
    middle = inner + lax.ppermute(inner, "context", [(1, 2), (2, 1)])
    outer = lax.ppermute(middle, "context", [(1, 0), (2, 3)])
    return jnp.where((plane == 1) | (plane == 2), middle, outer)


def sum_rows_everywhere(vector):
    vector = vector + exchange(vector, 1)
    vector = vector + exchange(vector, 2)
    for bit in (1, 2):
        vector = vector + lax.ppermute(vector, "context", [(i, i ^ bit) for i in range(4)])
    return vector


def per_device_planes(
    tokens,
    lengths,
    ln1_gain,
    ln1_bias,
    w_query,
    b_query,
    w_key,
    w_value,
    b_value,
    w_out,
    b_out,
    ln2_gain,
    ln2_bias,
    w_up,
    b_up,
    w_down,
    b_down,
    cotangent,
):
    block, width = tokens.shape[1:]
    row_count = 2 * block
    local_width = w_query.shape[1]
    local_heads = local_width // HEAD_DIM
    scale = HEAD_DIM ** (-0.5)
    member = lax.axis_index("dp")
    far, near = member // 2, member % 2
    plane = lax.axis_index("context")
    odd = plane % 2 == 1

    rows_low = reroute(tokens, odd, True).reshape(row_count, width)
    proj = gather_rows(jnp.concatenate([w_query, w_key, w_value], axis=1), member)
    out_t = gather_rows(w_out.T, member)
    up_weight = gather_rows(w_up, member)
    down_t = gather_rows(w_down.T, member)
    top_low = reroute(cotangent, odd, True).reshape(row_count, width)

    gain_one = ln1_gain.astype(jnp.float32)
    bias_one = ln1_bias.astype(jnp.float32)
    query_bias = b_query.astype(jnp.float32)
    value_bias = b_value.astype(jnp.float32)
    out_bias = b_out.astype(jnp.float32)
    gain_two = ln2_gain.astype(jnp.float32)
    bias_two = ln2_bias.astype(jnp.float32)
    up_bias = b_up.astype(jnp.float32)
    down_bias = b_down.astype(jnp.float32)

    lengths_near = jnp.where(plane // 2 == near, lengths, exchange(lengths, 1))
    length = jnp.where(odd, lengths_near[1], lengths_near[0])
    counts = jnp.arange(row_count, dtype=jnp.int32)
    places = near * row_count + counts
    key_places = jnp.concatenate([places, (1 - near) * row_count + counts])
    keep = (places < length).astype(jnp.float32)[:, None]
    live = (key_places < length)[None, None, :]

    rows_in = rows_low.astype(jnp.float32)
    normed_one, pull_one = jax.vjp(norm_rows, rows_in, gain_one, bias_one)
    normed_low = normed_one.astype(jnp.bfloat16)
    mixed = dense(normed_low, proj)
    queries = (mixed[:, :local_width] + query_bias).astype(jnp.bfloat16)
    keys_own = mixed[:, local_width : 2 * local_width].astype(jnp.bfloat16)
    values_own = (mixed[:, 2 * local_width :] + value_bias).astype(jnp.bfloat16)
    pair_own = jnp.concatenate([keys_own, values_own], axis=1)
    pair_whole = jnp.concatenate([pair_own, exchange(pair_own, 1)], axis=0)
    query_heads = queries.reshape(row_count, local_heads, HEAD_DIM)
    key_heads = pair_whole[:, :local_width].reshape(2 * row_count, local_heads, HEAD_DIM)
    value_heads = pair_whole[:, local_width:].reshape(2 * row_count, local_heads, HEAD_DIM)
    raw_scores = (
        jnp.einsum("qhd,khd->hqk", query_heads, key_heads, preferred_element_type=jnp.float32)
        * scale
    )
    masked = jnp.where(live, raw_scores, masked_value)
    largest = jnp.max(masked, axis=-1, keepdims=True)
    log_total = largest + jnp.log(jnp.sum(jnp.exp(masked - largest), axis=-1, keepdims=True))
    probs_low = jnp.exp(masked - log_total).astype(jnp.bfloat16)
    context_low = (
        jnp.einsum("hqk,khd->qhd", probs_low, value_heads, preferred_element_type=jnp.float32)
        .reshape(row_count, local_width)
        .astype(jnp.bfloat16)
    )
    part = dense_nt(context_low, out_t).astype(jnp.bfloat16)
    attention = part.astype(jnp.float32) + swap_tensor(part).astype(jnp.float32) + out_bias
    middle = rows_in + keep * attention
    normed_two, pull_two = jax.vjp(norm_rows, middle, gain_two, bias_two)
    normed_two_low = normed_two.astype(jnp.bfloat16)
    hidden_pre = dense(normed_two_low, up_weight) + up_bias
    hidden, pull_gelu = jax.vjp(gelu_tanh, hidden_pre)
    hidden_low = hidden.astype(jnp.bfloat16)

    grad_top = top_low.astype(jnp.float32)
    d_feed = (keep * grad_top).astype(jnp.bfloat16)
    d_hidden = dense(d_feed, down_t)
    d_pre = pull_gelu(d_hidden)[0].astype(jnp.bfloat16)
    part = dense_nt(d_pre, up_weight).astype(jnp.bfloat16)
    d_normed_two = part.astype(jnp.float32) + swap_tensor(part).astype(jnp.float32)

    part = dense_nt(hidden_low, down_t).astype(jnp.bfloat16)
    feed = part.astype(jnp.float32) + swap_tensor(part).astype(jnp.float32) + down_bias
    output_rows = (middle + keep * feed).astype(jnp.bfloat16)
    output = reroute(output_rows.reshape(2, block, width), odd, False)

    grad_down_t = scatter_rows(dense_tn(d_feed, hidden_low), far, near)
    grad_up = scatter_rows(dense_tn(normed_two_low, d_pre), far, near)
    grad_down_bias = jnp.sum(d_feed.astype(jnp.float32), axis=0)
    grad_up_bias = jnp.sum(d_pre.astype(jnp.float32), axis=0)

    d_middle, grad_gain_two, grad_bias_two = pull_two(d_normed_two)
    d_middle = d_middle + grad_top
    d_attention = (keep * d_middle).astype(jnp.bfloat16)
    grad_out_bias = jnp.sum(d_attention.astype(jnp.float32), axis=0)
    grad_out_t = scatter_rows(dense_tn(d_attention, context_low), far, near)
    d_context = dense(d_attention, out_t).astype(jnp.bfloat16)

    d_context_heads = d_context.reshape(row_count, local_heads, HEAD_DIM)
    probs = jnp.where(live, jnp.exp(raw_scores - log_total), 0.0)
    d_probs = jnp.einsum(
        "qhd,khd->hqk", d_context_heads, value_heads, preferred_element_type=jnp.float32
    )
    inner = jnp.sum(probs * d_probs, axis=-1, keepdims=True)
    d_scores = (probs * (d_probs - inner)).astype(jnp.bfloat16)
    d_query_low = (
        (
            jnp.einsum("hqk,khd->qhd", d_scores, key_heads, preferred_element_type=jnp.float32)
            * scale
        )
        .reshape(row_count, local_width)
        .astype(jnp.bfloat16)
    )
    d_keys = (
        jnp.einsum("hqk,qhd->khd", d_scores, query_heads, preferred_element_type=jnp.float32)
        * scale
    )
    d_values = jnp.einsum(
        "hqk,qhd->khd",
        probs.astype(jnp.bfloat16),
        d_context_heads,
        preferred_element_type=jnp.float32,
    )
    pair_grads = jnp.concatenate(
        [d_keys.reshape(2 * row_count, local_width), d_values.reshape(2 * row_count, local_width)],
        axis=1,
    ).astype(jnp.bfloat16)
    pair_low = pair_grads[:row_count] + exchange(pair_grads[row_count:], 1)
    d_proj = jnp.concatenate([d_query_low, pair_low], axis=1)
    part = dense_nt(d_proj, proj).astype(jnp.bfloat16)
    d_normed_one = part.astype(jnp.float32) + swap_tensor(part).astype(jnp.float32)
    d_rows, grad_gain_one, grad_bias_one = pull_one(d_normed_one)
    input_rows = (d_rows + d_middle).astype(jnp.bfloat16)
    input_grad = reroute(input_rows.reshape(2, block, width), odd, False)
    grad_proj = scatter_rows(dense_tn(normed_low, d_proj), far, near)
    proj_bias = jnp.sum(d_proj.astype(jnp.float32), axis=0)

    grad_down_t = sum_planes(grad_down_t, plane).astype(jnp.float32)
    grad_up = sum_planes(grad_up, plane).astype(jnp.float32)
    grad_out_t = sum_planes(grad_out_t, plane).astype(jnp.float32)
    grad_proj = sum_planes(grad_proj, plane).astype(jnp.float32)

    vectors = (grad_down_bias, grad_up_bias, grad_gain_two, grad_bias_two, grad_out_bias)
    early = sum_rows_everywhere(jnp.concatenate(vectors))
    late = sum_rows_everywhere(jnp.concatenate([proj_bias, grad_gain_one, grad_bias_one]))
    hidden_width = grad_up_bias.shape[0]
    grad_down_bias, grad_up_bias, grad_gain_two, grad_bias_two, grad_out_bias = jnp.split(
        early, [width, width + hidden_width, 2 * width + hidden_width, 3 * width + hidden_width]
    )
    return (
        output,
        input_grad,
        late[3 * local_width : 3 * local_width + width],
        late[3 * local_width + width :],
        grad_proj[:, :local_width],
        late[:local_width],
        grad_proj[:, local_width : 2 * local_width],
        grad_proj[:, 2 * local_width :],
        late[2 * local_width : 3 * local_width],
        grad_out_t.T,
        grad_out_bias,
        grad_gain_two,
        grad_bias_two,
        grad_up,
        grad_up_bias,
        grad_down_t.T,
        grad_down_bias,
    )


def pick(mesh):
    sizes = mesh.shape
    planes = sizes["dp"] == 4 and sizes["context"] == 4 and sizes["tensor"] == 2
    return per_device_planes if planes else per_device_general


def solution(mesh):
    return jax.shard_map(
        pick(mesh),
        mesh=mesh,
        in_specs=(
            P("dp", "context", None),
            P("dp"),
            P(),
            P(),
            P("dp", "tensor"),
            P("tensor"),
            P("dp", "tensor"),
            P("dp", "tensor"),
            P("tensor"),
            P("tensor", "dp"),
            P(),
            P(),
            P(),
            P("dp", "tensor"),
            P("tensor"),
            P("tensor", "dp"),
            P(),
            P("dp", "context", None),
        ),
        out_specs=(
            P("dp", "context", None),
            P("dp", "context", None),
            P(),
            P(),
            P("dp", "tensor"),
            P("tensor"),
            P("dp", "tensor"),
            P("dp", "tensor"),
            P("tensor"),
            P("tensor", "dp"),
            P(),
            P(),
            P(),
            P("dp", "tensor"),
            P("tensor"),
            P("tensor", "dp"),
            P(),
        ),
        check_vma=False,
    )
```

```python
import functools

import jax
import jax.numpy as jnp
from jax import lax
from jax.experimental import pallas as pl
from jax.experimental.pallas import tpu as pltpu
from jax.sharding import PartitionSpec as P

HEAD_DIM = 64


epsilon = 1e-06
masked_value = -1e30


def norm_rows(values, gain_vec, bias_vec):
    average = jnp.mean(values, axis=-1, keepdims=True)
    centred = values - average
    spread = jnp.mean(centred * centred, axis=-1, keepdims=True)
    return centred * lax.rsqrt(spread + epsilon) * gain_vec + bias_vec


def gelu_tanh(values):
    return jax.nn.gelu(values, approximate=True)


def dense(left, right):
    return jnp.dot(left, right, preferred_element_type=jnp.float32)


def dense_tn(left, right):
    return lax.dot_general(
        left, right, (((0,), (0,)), ((), ())), preferred_element_type=jnp.float32
    )


def dense_nt(left, right):
    return lax.dot_general(
        left, right, (((1,), (1,)), ((), ())), preferred_element_type=jnp.float32
    )


def per_device_general(
    tokens,
    lengths,
    ln1_gain,
    ln1_bias,
    w_query,
    b_query,
    w_key,
    w_value,
    b_value,
    w_out,
    b_out,
    ln2_gain,
    ln2_bias,
    w_up,
    b_up,
    w_down,
    b_down,
    cotangent,
):
    seq_count, shard_rows, width = tokens.shape
    full_len = shard_rows * lax.axis_size("context")
    local_width = w_query.shape[1]
    local_heads = local_width // HEAD_DIM
    scale = HEAD_DIM ** (-0.5)
    row_count = seq_count * shard_rows
    query_weight, key_weight, value_weight, up_weight, out_weight, down_weight = (
        lax.all_gather(w_query, "dp", axis=0, tiled=True),
        lax.all_gather(w_key, "dp", axis=0, tiled=True),
        lax.all_gather(w_value, "dp", axis=0, tiled=True),
        lax.all_gather(w_up, "dp", axis=0, tiled=True),
        lax.all_gather(w_out, "dp", axis=1, tiled=True),
        lax.all_gather(w_down, "dp", axis=1, tiled=True),
    )
    gain_one = ln1_gain.astype(jnp.float32)
    bias_one = ln1_bias.astype(jnp.float32)
    query_bias = b_query.astype(jnp.float32)
    value_bias = b_value.astype(jnp.float32)
    out_bias = b_out.astype(jnp.float32)
    gain_two = ln2_gain.astype(jnp.float32)
    bias_two = ln2_bias.astype(jnp.float32)
    up_bias = b_up.astype(jnp.float32)
    down_bias = b_down.astype(jnp.float32)
    places = lax.axis_index("context") * shard_rows + jnp.arange(shard_rows, dtype=jnp.int32)
    keep = (places[None, :] < lengths[:, None]).astype(jnp.float32).reshape(row_count, 1)
    key_places = jnp.arange(full_len, dtype=jnp.int32)
    rows_in = tokens.reshape(row_count, width).astype(jnp.float32)
    normed_one, pull_one = jax.vjp(norm_rows, rows_in, gain_one, bias_one)
    normed_low = normed_one.astype(jnp.bfloat16)
    queries = (dense(normed_low, query_weight) + query_bias).astype(jnp.bfloat16)
    keys_own = dense(normed_low, key_weight).astype(jnp.bfloat16)
    values_own = (dense(normed_low, value_weight) + value_bias).astype(jnp.bfloat16)
    keys_whole, values_whole = (
        lax.all_gather(
            keys_own.reshape(seq_count, shard_rows, local_width), "context", axis=1, tiled=True
        ),
        lax.all_gather(
            values_own.reshape(seq_count, shard_rows, local_width), "context", axis=1, tiled=True
        ),
    )
    query_heads = queries.reshape(seq_count, shard_rows, local_heads, HEAD_DIM)
    head_outs = []
    log_sums = []
    for member in range(seq_count):
        key_heads = keys_whole[member].reshape(full_len, local_heads, HEAD_DIM)
        value_heads = values_whole[member].reshape(full_len, local_heads, HEAD_DIM)
        raw_scores = (
            jnp.einsum(
                "qhd,khd->hqk", query_heads[member], key_heads, preferred_element_type=jnp.float32
            )
            * scale
        )
        live = (key_places < lengths[member])[None, None, :]
        masked = jnp.where(live, raw_scores, masked_value)
        largest = jnp.max(masked, axis=-1, keepdims=True)
        log_total = largest + jnp.log(jnp.sum(jnp.exp(masked - largest), axis=-1, keepdims=True))
        probs_low = jnp.exp(masked - log_total).astype(jnp.bfloat16)
        mixed_heads = jnp.einsum(
            "hqk,khd->qhd", probs_low, value_heads, preferred_element_type=jnp.float32
        )
        head_outs.append(mixed_heads.reshape(shard_rows, local_width))
        log_sums.append(log_total)
    context_low = jnp.concatenate(head_outs, axis=0).astype(jnp.bfloat16)
    attention = (
        lax.psum(dense(context_low, out_weight).astype(jnp.bfloat16), "tensor").astype(jnp.float32)
        + out_bias
    )
    middle = rows_in + keep * attention
    normed_two, pull_two = jax.vjp(norm_rows, middle, gain_two, bias_two)
    normed_two_low = normed_two.astype(jnp.bfloat16)
    hidden_pre = dense(normed_two_low, up_weight) + up_bias
    hidden, pull_gelu = jax.vjp(gelu_tanh, hidden_pre)
    hidden_low = hidden.astype(jnp.bfloat16)
    feed = (
        lax.psum(dense(hidden_low, down_weight).astype(jnp.bfloat16), "tensor").astype(jnp.float32)
        + down_bias
    )
    output = (middle + keep * feed).astype(jnp.bfloat16).reshape(tokens.shape)
    grad_top = cotangent.reshape(row_count, width).astype(jnp.float32)
    d_feed = (keep * grad_top).astype(jnp.bfloat16)
    grad_down_bias = jnp.sum(d_feed.astype(jnp.float32), axis=0)
    grad_down = dense_tn(hidden_low, d_feed)
    d_hidden = dense_nt(d_feed, down_weight)
    d_pre = pull_gelu(d_hidden)[0].astype(jnp.bfloat16)
    grad_up_bias = jnp.sum(d_pre.astype(jnp.float32), axis=0)
    grad_up = dense_tn(normed_two_low, d_pre)
    d_normed_two = lax.psum(dense_nt(d_pre, up_weight).astype(jnp.bfloat16), "tensor").astype(
        jnp.float32
    )
    d_middle, grad_gain_two, grad_bias_two = pull_two(d_normed_two)
    d_middle = d_middle + grad_top
    d_attention = (keep * d_middle).astype(jnp.bfloat16)
    grad_out_bias = jnp.sum(d_attention.astype(jnp.float32), axis=0)
    grad_out = dense_tn(context_low, d_attention)
    d_context = dense_nt(d_attention, out_weight).astype(jnp.bfloat16)
    back_keys, back_values = (keys_whole, values_whole)
    d_context_heads = d_context.reshape(seq_count, shard_rows, local_heads, HEAD_DIM)
    query_grads = []
    own_grads = []
    inner_rows = []
    for member in range(seq_count):
        key_heads = back_keys[member].reshape(full_len, local_heads, HEAD_DIM)
        value_heads = back_values[member].reshape(full_len, local_heads, HEAD_DIM)
        raw_scores = (
            jnp.einsum(
                "qhd,khd->hqk", query_heads[member], key_heads, preferred_element_type=jnp.float32
            )
            * scale
        )
        live = (key_places < lengths[member])[None, None, :]
        probs = jnp.where(live, jnp.exp(raw_scores - log_sums[member]), 0.0)
        d_probs = jnp.einsum(
            "qhd,khd->hqk", d_context_heads[member], value_heads, preferred_element_type=jnp.float32
        )
        inner = jnp.sum(probs * d_probs, axis=-1, keepdims=True)
        d_scores = (probs * (d_probs - inner)).astype(jnp.bfloat16)
        d_query = (
            jnp.einsum("hqk,khd->qhd", d_scores, key_heads, preferred_element_type=jnp.float32)
            * scale
        )
        query_grads.append(d_query.reshape(shard_rows, local_width))
        inner_rows.append(inner[:, :, 0])
        d_keys = (
            jnp.einsum(
                "hqk,qhd->khd", d_scores, query_heads[member], preferred_element_type=jnp.float32
            )
            * scale
        )
        d_values = jnp.einsum(
            "hqk,qhd->khd",
            probs.astype(jnp.bfloat16),
            d_context_heads[member],
            preferred_element_type=jnp.float32,
        )
        key_term = jnp.concatenate(
            [d_keys.reshape(full_len, local_width), d_values.reshape(full_len, local_width)], axis=1
        )
        own_grads.append(
            lax.psum_scatter(
                key_term.astype(jnp.bfloat16), "context", scatter_dimension=0, tiled=True
            ).astype(jnp.float32)
        )
    d_query_low = jnp.concatenate(query_grads, axis=0).astype(jnp.bfloat16)
    key_value_grads = jnp.concatenate(own_grads, axis=0)
    d_keys_low = key_value_grads[:, :local_width].astype(jnp.bfloat16)
    d_values_low = key_value_grads[:, local_width:].astype(jnp.bfloat16)
    grad_query = dense_tn(normed_low, d_query_low)
    grad_query_bias = jnp.sum(d_query_low.astype(jnp.float32), axis=0)
    grad_key = dense_tn(normed_low, d_keys_low)
    grad_value = dense_tn(normed_low, d_values_low)
    grad_value_bias = jnp.sum(d_values_low.astype(jnp.float32), axis=0)
    d_normed_one = lax.psum(
        (
            dense_nt(d_query_low, query_weight)
            + dense_nt(d_keys_low, key_weight)
            + dense_nt(d_values_low, value_weight)
        ).astype(jnp.bfloat16),
        "tensor",
    ).astype(jnp.float32)
    d_rows, grad_gain_one, grad_bias_one = pull_one(d_normed_one)
    input_grad = (d_rows + d_middle).astype(jnp.bfloat16).reshape(tokens.shape)
    data_sums = (
        lax.psum_scatter(
            grad_query.astype(jnp.bfloat16), "dp", scatter_dimension=0, tiled=True
        ).astype(jnp.float32),
        lax.psum_scatter(
            grad_key.astype(jnp.bfloat16), "dp", scatter_dimension=0, tiled=True
        ).astype(jnp.float32),
        lax.psum_scatter(
            grad_value.astype(jnp.bfloat16), "dp", scatter_dimension=0, tiled=True
        ).astype(jnp.float32),
        lax.psum_scatter(
            grad_up.astype(jnp.bfloat16), "dp", scatter_dimension=0, tiled=True
        ).astype(jnp.float32),
        lax.psum_scatter(
            grad_out.astype(jnp.bfloat16), "dp", scatter_dimension=1, tiled=True
        ).astype(jnp.float32),
        lax.psum_scatter(
            grad_down.astype(jnp.bfloat16), "dp", scatter_dimension=1, tiled=True
        ).astype(jnp.float32),
    )
    owned_sums = (
        lax.psum(data_sums[0].astype(jnp.bfloat16), "context").astype(jnp.float32),
        lax.psum(data_sums[1].astype(jnp.bfloat16), "context").astype(jnp.float32),
        lax.psum(data_sums[2].astype(jnp.bfloat16), "context").astype(jnp.float32),
        lax.psum(data_sums[3].astype(jnp.bfloat16), "context").astype(jnp.float32),
        lax.psum(data_sums[4].astype(jnp.bfloat16), "context").astype(jnp.float32),
        lax.psum(data_sums[5].astype(jnp.bfloat16), "context").astype(jnp.float32),
    )
    small_sums = lax.psum(
        (
            grad_gain_one,
            grad_bias_one,
            grad_query_bias,
            grad_value_bias,
            grad_out_bias,
            grad_gain_two,
            grad_bias_two,
            grad_up_bias,
            grad_down_bias,
        ),
        ("dp", "context"),
    )
    return (
        output,
        input_grad,
        small_sums[0],
        small_sums[1],
        owned_sums[0],
        small_sums[2],
        owned_sums[1],
        owned_sums[2],
        small_sums[3],
        owned_sums[4],
        small_sums[4],
        small_sums[5],
        small_sums[6],
        owned_sums[3],
        small_sums[7],
        owned_sums[5],
        small_sums[8],
    )


def live_bias(info, count):
    places = lax.broadcasted_iota(jnp.int32, (count, 2 * HEAD_DIM), 0)
    return jnp.concatenate(
        [jnp.where(info[k] + places < info[8], 0.0, masked_value) for k in range(8)], axis=0
    ).astype(jnp.bfloat16)


def split_pair(array, extra):
    lane = lax.broadcasted_iota(jnp.int32, array.shape, 1)
    zero = jnp.zeros((), jnp.bfloat16)
    left = jnp.where(lane < HEAD_DIM, array, jnp.where(lane == HEAD_DIM, extra, zero))
    right = jnp.where(lane >= HEAD_DIM, array, jnp.where(lane == 0, extra, zero))
    return left, right


LOG_SCALE = HEAD_DIM ** (-0.5) * 1.4426950408889634


def attend_kernel(info, query_ref, own_ref, other_ref, out_ref, log_ref, *, steps):
    pair = 2 * HEAD_DIM
    rows = query_ref.shape[0]
    count = rows // 4
    step = rows // steps
    keys = jnp.concatenate([own_ref[:, :pair], other_ref[:, :pair]], axis=0)
    values = jnp.concatenate([own_ref[:, pair:], other_ref[:, pair:]], axis=0)
    values_t = values.T
    key_heads = split_pair(keys, live_bias(info, count))
    query_heads = split_pair(query_ref[...], jnp.ones((), jnp.bfloat16))
    for s in range(steps):
        mixed = []
        for head in range(2):
            query = query_heads[head][s * step : (s + 1) * step]
            scores = dense_nt(key_heads[head], query)
            largest = jnp.max(scores, axis=0, keepdims=True)
            weights = jnp.exp2((scores - largest) * LOG_SCALE)
            total = jnp.sum(weights, axis=0, keepdims=True)
            part = dense(
                values_t[head * HEAD_DIM : (head + 1) * HEAD_DIM], weights.astype(jnp.bfloat16)
            )
            mixed.append(part / total)
            log_ref[0, head : head + 1, s * step : (s + 1) * step] = (
                largest * LOG_SCALE + jnp.log2(total)
            )
        out_ref[s * step : (s + 1) * step, :] = jnp.concatenate(mixed, axis=0).T.astype(jnp.bfloat16)


def attend(info, queries, pair_own, pair_other, steps=2):
    rows, width = queries.shape
    pair = 2 * HEAD_DIM
    groups = width // pair
    work = 4 * rows * 2 * rows * width
    return pl.pallas_call(
        functools.partial(attend_kernel, steps=steps),
        out_shape=(
            jax.ShapeDtypeStruct((rows, width), jnp.bfloat16),
            jax.ShapeDtypeStruct((groups, 2, rows), jnp.float32),
        ),
        grid_spec=pltpu.PrefetchScalarGridSpec(
            num_scalar_prefetch=1,
            grid=(groups,),
            in_specs=[
                pl.BlockSpec((rows, pair), lambda g, info: (0, g)),
                pl.BlockSpec((rows, 2 * pair), lambda g, info: (0, g)),
                pl.BlockSpec((rows, 2 * pair), lambda g, info: (0, g)),
            ],
            out_specs=(
                pl.BlockSpec((rows, pair), lambda g, info: (0, g)),
                pl.BlockSpec((1, 2, rows), lambda g, info: (g, 0, 0)),
            ),
        ),
        compiler_params=pltpu.CompilerParams(vmem_limit_bytes=48 << 20),
        cost_estimate=pl.CostEstimate(
            flops=4 * work, bytes_accessed=12 * rows * width, transcendentals=work // (2 * HEAD_DIM)
        ),
    )(info, queries, pair_own, pair_other)


def attend_back_kernel(
    info,
    query_ref,
    own_ref,
    other_ref,
    out_ref,
    grad_ref,
    log_ref,
    d_query_ref,
    d_own_ref,
    d_other_ref,
    *,
    steps,
):
    pair = 2 * HEAD_DIM
    rows = query_ref.shape[0]
    step = rows // steps
    scale = HEAD_DIM ** (-0.5)
    keys = jnp.concatenate([own_ref[:, :pair], other_ref[:, :pair]], axis=0)
    values = jnp.concatenate([own_ref[:, pair:], other_ref[:, pair:]], axis=0)
    keys_t = keys.T
    key_heads = split_pair(keys, live_bias(info, rows // 4))
    value_heads = split_pair(values, jnp.zeros((), jnp.bfloat16))
    query_heads = split_pair(query_ref[...], jnp.ones((), jnp.bfloat16))
    inner_t = (grad_ref[...].astype(jnp.float32) * out_ref[...].astype(jnp.float32)).T
    d_keys = [0.0, 0.0]
    d_values = [0.0, 0.0]
    for s in range(steps):
        part = slice(s * step, (s + 1) * step)
        query = query_ref[part, :]
        grad = grad_ref[part, :]
        d_query = []
        for head in range(2):
            dims = slice(head * HEAD_DIM, (head + 1) * HEAD_DIM)
            inner = jnp.sum(inner_t[dims, part], axis=0, keepdims=True)
            scores = dense_nt(key_heads[head], query_heads[head][part])
            probs = jnp.exp2(scores * LOG_SCALE - log_ref[0, head : head + 1, part])
            d_probs = dense_nt(value_heads[head], grad)
            d_scores = (probs * (d_probs - inner)).astype(jnp.bfloat16)
            d_query.append(dense(keys_t[dims], d_scores))
            d_keys[head] += dense(d_scores, query)
            d_values[head] += dense(probs.astype(jnp.bfloat16), grad)
        d_query_ref[part, :] = (jnp.concatenate(d_query, axis=0).T * scale).astype(jnp.bfloat16)
    left = lax.broadcasted_iota(jnp.int32, d_keys[0].shape, 1) < HEAD_DIM
    d_key = (jnp.where(left, d_keys[0], d_keys[1]) * scale).astype(jnp.bfloat16)
    d_value = jnp.where(left, d_values[0], d_values[1]).astype(jnp.bfloat16)
    d_own_ref[:, :pair] = d_key[:rows]
    d_own_ref[:, pair:] = d_value[:rows]
    d_other_ref[:, :pair] = d_key[rows:]
    d_other_ref[:, pair:] = d_value[rows:]


def attend_back(info, queries, pair_own, pair_other, mixed, d_mixed, logs, steps=2):
    rows, width = queries.shape
    pair = 2 * HEAD_DIM
    groups = width // pair
    work = 4 * rows * 2 * rows * width
    narrow = pl.BlockSpec((rows, pair), lambda g, info: (0, g))
    wide = pl.BlockSpec((rows, 2 * pair), lambda g, info: (0, g))
    return pl.pallas_call(
        functools.partial(attend_back_kernel, steps=steps),
        out_shape=(
            jax.ShapeDtypeStruct((rows, width), jnp.bfloat16),
            jax.ShapeDtypeStruct((rows, 2 * width), jnp.bfloat16),
            jax.ShapeDtypeStruct((rows, 2 * width), jnp.bfloat16),
        ),
        grid_spec=pltpu.PrefetchScalarGridSpec(
            num_scalar_prefetch=1,
            grid=(groups,),
            in_specs=[
                narrow,
                wide,
                wide,
                narrow,
                narrow,
                pl.BlockSpec((1, 2, rows), lambda g, info: (g, 0, 0)),
            ],
            out_specs=(narrow, wide, wide),
        ),
        compiler_params=pltpu.CompilerParams(vmem_limit_bytes=48 << 20),
        cost_estimate=pl.CostEstimate(
            flops=10 * work, bytes_accessed=24 * rows * width, transcendentals=work // (2 * HEAD_DIM)
        ),
    )(info, queries, pair_own, pair_other, mixed, d_mixed, logs)


def held(info, quarters, count, width):
    places = lax.broadcasted_iota(jnp.int32, (count, width), 0)
    return jnp.concatenate([info[k] + places < info[8] for k in range(quarters)], axis=0)


def row_stats(values):
    centred = values - jnp.mean(values, axis=-1, keepdims=True)
    spread = jnp.mean(centred * centred, axis=-1, keepdims=True)
    root = lax.rsqrt(spread + epsilon)
    return centred * root, root


def row_pull(normed, root, grad):
    return root * (
        grad
        - jnp.mean(grad, axis=-1, keepdims=True)
        - normed * jnp.mean(grad * normed, axis=-1, keepdims=True)
    )


def settle(parts, out_ref):
    rows = parts[0].shape[0]
    mine = lax.axis_index("dp")
    for step, part in enumerate(parts):
        start = pl.multiple_of((mine ^ step) * rows, rows)
        out_ref[pl.ds(start, rows), :] = part[...]


def enter_kernel(
    first_ref, second_ref, gain_ref, bias_ref, q_bias_ref, v_bias_ref, a, b, c, d,
    rows_ref, normed_ref, query_ref, pair_ref, proj_ref,
):
    pair = 2 * HEAD_DIM
    settle((a, b, c, d), proj_ref)
    rows = jnp.concatenate([first_ref[0], second_ref[0], first_ref[1], second_ref[1]], axis=0)
    rows_ref[...] = rows
    normed, _ = row_stats(rows.astype(jnp.float32))
    normed = normed * gain_ref[...].astype(jnp.float32) + bias_ref[...].astype(jnp.float32)
    normed = normed.astype(jnp.bfloat16)
    normed_ref[...] = normed
    local = query_ref.shape[1]
    mixed = dense(normed, proj_ref[...])
    query_ref[...] = (mixed[:, :local] + q_bias_ref[...].astype(jnp.float32)).astype(jnp.bfloat16)
    for g in range(local // pair):
        cols = slice(g * pair, (g + 1) * pair)
        key = mixed[:, local + g * pair : local + (g + 1) * pair]
        value = mixed[:, 2 * local + g * pair : 2 * local + (g + 1) * pair]
        value = value + v_bias_ref[:, cols].astype(jnp.float32)
        pair_ref[:, 2 * g * pair : (2 * g + 1) * pair] = key.astype(jnp.bfloat16)
        pair_ref[:, (2 * g + 1) * pair : (2 * g + 2) * pair] = value.astype(jnp.bfloat16)


def enter(first, second, gain, bias, q_bias, v_bias, blocks):
    half, width = first.shape[1:]
    rows = 4 * half
    local = q_bias.shape[1]
    low = lambda *shape: jax.ShapeDtypeStruct(shape, jnp.bfloat16)
    return pl.pallas_call(
        enter_kernel,
        out_shape=(
            low(rows, width),
            low(rows, width),
            low(rows, local),
            low(rows, 2 * local),
            low(width, 3 * local),
        ),
        compiler_params=pltpu.CompilerParams(vmem_limit_bytes=48 << 20),
        cost_estimate=pl.CostEstimate(
            flops=6 * rows * width * local, bytes_accessed=10 << 20, transcendentals=rows
        ),
    )(first, second, gain, bias, q_bias, v_bias, *blocks)


ROOT_TWO_OVER_PI = 0.7978845608028654
CUBE = 0.044715


def middle_kernel(
    info, rows_ref, own_ref, peer_ref, top0_ref, top1_ref, gain_ref, bias_ref, out_bias_ref,
    oa, ob, oc, od, ua, ub, uc, ud, da, db, dc, dd, up_bias_ref,
    mid_ref, normed_ref, feed_ref, hidden_ref, d_pre_ref, d_own_ref, d_peer_ref,
    f_own_ref, f_peer_ref, out_ref, g_up_ref, g_down_ref,
    outs, ups, downs, acc_d, acc_f,
):
    step = pl.program_id(0)
    rows, width = rows_ref.shape
    half = rows // 2
    local = own_ref.shape[1]

    @pl.when(step == 0)
    def _():
        settle((oa, ob, oc, od), outs)
        out_ref[...] = outs[:, :local]
        peer = jnp.concatenate([peer_ref[half:, :], peer_ref[:half, :]], axis=0)
        attention = (
            dense_nt(own_ref[...], outs[:, :local])
            + dense_nt(peer, outs[:, local:])
            + out_bias_ref[...].astype(jnp.float32)
        )
        real = held(info, 4, rows // 4, width)
        mid = rows_ref[...].astype(jnp.float32) + jnp.where(real, attention, 0.0)
        mid_ref[...] = mid
        normed, _ = row_stats(mid)
        normed = normed * gain_ref[...].astype(jnp.float32) + bias_ref[...].astype(jnp.float32)
        normed_ref[...] = normed.astype(jnp.bfloat16)
        top = jnp.concatenate([top0_ref[0], top1_ref[0], top0_ref[1], top1_ref[1]], axis=0)
        feed = jnp.where(real, top.astype(jnp.float32), 0.0)
        feed_ref[...] = feed.astype(jnp.bfloat16)
        g_down_ref[...] = jnp.sum(feed, axis=0, keepdims=True)
        acc_d[...] = jnp.zeros_like(acc_d)
        acc_f[...] = jnp.zeros_like(acc_f)

    settle((ua, ub, uc, ud), ups)
    settle((da, db, dc, dd), downs)
    pre = dense(normed_ref[...], ups[...]) + up_bias_ref[...].astype(jnp.float32)
    d_hidden = dense(feed_ref[...], downs[...])
    square = pre * pre
    bend = jnp.tanh(ROOT_TWO_OVER_PI * pre * (1.0 + CUBE * square))
    half_up = 0.5 + 0.5 * bend
    hidden = (pre * half_up).astype(jnp.bfloat16)
    slope = half_up + (pre * half_up) * (1.0 - bend) * (
        ROOT_TWO_OVER_PI + 3.0 * CUBE * ROOT_TWO_OVER_PI * square
    )
    d_pre = (d_hidden * slope).astype(jnp.bfloat16)
    hidden_ref[...] = hidden
    d_pre_ref[...] = d_pre
    g_up_ref[...] = jnp.sum(d_pre.astype(jnp.float32), axis=0, keepdims=True)
    acc_d[...] += dense_nt(d_pre, ups[...])
    acc_f[...] += dense_nt(hidden, downs[...])

    @pl.when(step == pl.num_programs(0) - 1)
    def _():
        low = acc_d[...].astype(jnp.bfloat16)
        d_own_ref[...] = low[:half]
        d_peer_ref[...] = low[half:]
        low = acc_f[...].astype(jnp.bfloat16)
        f_own_ref[...] = low[:half]
        f_peer_ref[...] = low[half:]


def middle_part(info, rows_low, own, peer, top, gain, bias, out_bias, packs, up_bias):
    rows, width = rows_low.shape
    local = own.shape[1]
    shard = packs[0].shape[0]
    hidden = up_bias.shape[1]
    tile = 384
    low = lambda *shape: jax.ShapeDtypeStruct(shape, jnp.bfloat16)
    full = lambda *shape: jax.ShapeDtypeStruct(shape, jnp.float32)
    fixed = lambda array: pl.BlockSpec(array.shape, lambda i, info: (0,) * array.ndim)
    columns = lambda height: pl.BlockSpec((height, tile), lambda i, info: (0, i))
    outs = pl.BlockSpec((shard, width), lambda i, info: (0, 0))
    first_up, first_down = width // tile, (width + hidden) // tile
    ups = pl.BlockSpec((shard, tile), lambda i, info: (0, first_up + i))
    downs = pl.BlockSpec((shard, tile), lambda i, info: (0, first_down + i))
    whole = (rows_low, own, peer, *top, gain, bias, out_bias)
    shapes = (
        full(rows, width),
        low(rows, width),
        low(rows, width),
        low(rows, hidden),
        low(rows, hidden),
        low(rows // 2, width),
        low(rows // 2, width),
        low(rows // 2, width),
        low(rows // 2, width),
        low(width, local),
        full(1, hidden),
        full(1, width),
    )
    tiled = (3, 4, 10)
    return pl.pallas_call(
        middle_kernel,
        out_shape=shapes,
        grid_spec=pltpu.PrefetchScalarGridSpec(
            num_scalar_prefetch=1,
            grid=(hidden // tile,),
            in_specs=[fixed(a) for a in whole] + [outs] * 4 + [ups] * 4 + [downs] * 4 + [columns(1)],
            out_specs=tuple(
                columns(s.shape[0]) if k in tiled else fixed(s) for k, s in enumerate(shapes)
            ),
            scratch_shapes=[
                pltpu.VMEM((width, 2 * local), jnp.bfloat16),
                pltpu.VMEM((width, tile), jnp.bfloat16),
                pltpu.VMEM((width, tile), jnp.bfloat16),
                pltpu.VMEM((rows, width), jnp.float32),
                pltpu.VMEM((rows, width), jnp.float32),
            ],
        ),
        compiler_params=pltpu.CompilerParams(vmem_limit_bytes=52 << 20),
        cost_estimate=pl.CostEstimate(
            flops=8 * rows * width * hidden, bytes_accessed=20 << 20, transcendentals=rows * hidden
        ),
    )(info, *whole, *packs, *packs, *packs, up_bias)


def turn_kernel(
    info, mid_ref, d_own_ref, d_peer_ref, got_own_ref, got_peer_ref, top0_ref, top1_ref,
    gain_ref, out_ref, d_mid_ref, d_att_ref, d_mix_ref, sums_ref,
):
    rows, width = mid_ref.shape
    half = rows // 2
    f32 = lambda ref: ref[...].astype(jnp.float32)
    grad = jnp.concatenate(
        [f32(d_own_ref) + f32(got_own_ref), f32(d_peer_ref) + f32(got_peer_ref)], axis=0
    )
    normed, root = row_stats(mid_ref[...])
    top = jnp.concatenate([top0_ref[0], top1_ref[0], top0_ref[1], top1_ref[1]], axis=0)
    d_mid = top.astype(jnp.float32) + row_pull(
        normed, root, grad * gain_ref[...].astype(jnp.float32)
    )
    d_mid_ref[...] = d_mid[:half]
    d_att = jnp.where(held(info, 4, rows // 4, width), d_mid, 0.0).astype(jnp.bfloat16)
    d_att_ref[...] = d_att
    d_mix_ref[...] = dense(d_att, out_ref[...]).astype(jnp.bfloat16)
    sums_ref[0:1, :] = jnp.sum(grad * normed, axis=0, keepdims=True)
    sums_ref[1:2, :] = jnp.sum(grad, axis=0, keepdims=True)
    sums_ref[2:3, :] = jnp.sum(d_att.astype(jnp.float32), axis=0, keepdims=True)


def turn(info, mid, d_own, d_peer, got_own, got_peer, top, gain, out_t):
    rows, width = mid.shape
    local = out_t.shape[1]
    args = (mid, d_own, d_peer, got_own, got_peer, *top, gain, out_t)
    return pl.pallas_call(
        turn_kernel,
        out_shape=(
            jax.ShapeDtypeStruct((rows // 2, width), jnp.float32),
            jax.ShapeDtypeStruct((rows, width), jnp.bfloat16),
            jax.ShapeDtypeStruct((rows, local), jnp.bfloat16),
            jax.ShapeDtypeStruct((3, width), jnp.float32),
        ),
        in_specs=[pl.BlockSpec(memory_space=pltpu.SMEM)]
        + [pl.BlockSpec(memory_space=pltpu.VMEM)] * len(args),
        compiler_params=pltpu.CompilerParams(vmem_limit_bytes=48 << 20),
        cost_estimate=pl.CostEstimate(
            flops=2 * rows * width * local, bytes_accessed=8 << 20, transcendentals=rows
        ),
    )(info, *args)


def leave_kernel(
    rows_ref, d_query_ref, d_pair_ref, got_ref, proj_ref, d_proj_ref, own_ref, peer_ref, sums_ref,
    bias_ref,
):
    pair = 2 * HEAD_DIM
    rows, local = d_query_ref.shape
    half = rows // 2
    d_proj_ref[:, :local] = d_query_ref[...]
    for g in range(local // pair):
        for k in range(2):
            cols = slice((2 * g + k) * pair, (2 * g + k + 1) * pair)
            total = d_pair_ref[:, cols].astype(jnp.float32) + got_ref[:, cols].astype(jnp.float32)
            start = (k + 1) * local + g * pair
            d_proj_ref[:, start : start + pair] = total.astype(jnp.bfloat16)
    d_proj = d_proj_ref[...]
    bias_ref[...] = jnp.sum(d_proj.astype(jnp.float32), axis=0, keepdims=True)
    grad = dense_nt(d_proj, proj_ref[...])
    low = grad.astype(jnp.bfloat16)
    own_ref[...] = low[:half]
    peer_ref[...] = low[half:]
    normed, _ = row_stats(rows_ref[...].astype(jnp.float32))
    sums_ref[0:1, :] = jnp.sum(grad * normed, axis=0, keepdims=True)
    sums_ref[1:2, :] = jnp.sum(grad, axis=0, keepdims=True)


def leave(rows_low, d_query, d_pair, got, proj):
    rows, width = rows_low.shape
    local = d_query.shape[1]
    low = lambda *shape: jax.ShapeDtypeStruct(shape, jnp.bfloat16)
    return pl.pallas_call(
        leave_kernel,
        out_shape=(
            low(rows, 3 * local),
            low(rows // 2, width),
            low(rows // 2, width),
            jax.ShapeDtypeStruct((2, width), jnp.float32),
            jax.ShapeDtypeStruct((1, 3 * local), jnp.float32),
        ),
        compiler_params=pltpu.CompilerParams(vmem_limit_bytes=48 << 20),
        cost_estimate=pl.CostEstimate(
            flops=6 * rows * width * local, bytes_accessed=8 << 20, transcendentals=rows
        ),
    )(rows_low, d_query, d_pair, got, proj)


def finish_kernel(rows_ref, own_ref, got_ref, gain_ref, d_mid_ref, first_ref, second_ref):
    half = rows_ref.shape[0]
    normed, root = row_stats(rows_ref[...].astype(jnp.float32))
    grad = own_ref[...].astype(jnp.float32) + got_ref[...].astype(jnp.float32)
    d_rows = row_pull(normed, root, grad * gain_ref[...].astype(jnp.float32)) + d_mid_ref[...]
    low = d_rows.astype(jnp.bfloat16)
    first_ref[...] = low[: half // 2]
    second_ref[...] = low[half // 2 :]


def finish(rows_low, own, got, gain, d_mid):
    half, width = own.shape
    top_half = pl.BlockSpec((half, width), lambda i: (0, 0))
    fixed = lambda a: pl.BlockSpec(a.shape, lambda i: (0,) * a.ndim)
    piece = jax.ShapeDtypeStruct((half // 2, width), jnp.bfloat16)
    return pl.pallas_call(
        finish_kernel,
        out_shape=(piece, piece),
        grid=(1,),
        in_specs=[top_half, fixed(own), fixed(got), fixed(gain), fixed(d_mid)],
        out_specs=(fixed(piece), fixed(piece)),
        compiler_params=pltpu.CompilerParams(vmem_limit_bytes=32 << 20),
        cost_estimate=pl.CostEstimate(
            flops=20 * half * width, bytes_accessed=4 << 20, transcendentals=half
        ),
    )(rows_low, own, got, gain, d_mid)


def weight_grad_kernel(*refs, pairs, extra):
    count = 2 * pairs + extra
    lefts, rights = refs[0 : 2 * pairs : 2], refs[1 : 2 * pairs : 2]
    own_ref, far_ref, send_ref = refs[count : count + 3]
    turned = refs[count + 3 :]
    rows = own_ref.shape[0]
    mine = lax.axis_index("dp")
    targets = (own_ref, send_ref.at[:rows], far_ref, send_ref.at[rows : 2 * rows])
    start = 0
    for left, right, scratch in zip(lefts, rights, turned):
        scratch[...] = left[...].T
        width = right.shape[1]
        for step, target in enumerate(targets):
            place = pl.multiple_of((mine ^ step) * rows, rows)
            grad = dense(scratch[pl.ds(place, rows), :], right[...])
            target[:, start : start + width] = grad.astype(jnp.bfloat16)
        start += width
    if extra:
        high, low = split_bits(refs[2 * pairs][...])
        send_ref[2 * rows :, :] = jnp.concatenate([high, low], axis=0)


def split_bits(values):
    high = values.astype(jnp.bfloat16)
    return high, (values - high.astype(jnp.float32)).astype(jnp.bfloat16)


def weight_grad(operands, vectors=None):
    depth, width = operands[0].shape
    columns = sum(right.shape[1] for right in operands[1::2])
    rows = width // 4
    pairs = len(operands) // 2
    extra = () if vectors is None else (vectors,)
    more = 0 if vectors is None else 2 * vectors.shape[0]
    low = lambda *shape: jax.ShapeDtypeStruct(shape, jnp.bfloat16)
    return pl.pallas_call(
        functools.partial(weight_grad_kernel, pairs=pairs, extra=len(extra)),
        out_shape=(low(rows, columns), low(rows, columns), low(2 * rows + more, columns)),
        scratch_shapes=[pltpu.VMEM((width, depth), jnp.bfloat16)] * pairs,
        compiler_params=pltpu.CompilerParams(vmem_limit_bytes=48 << 20),
        cost_estimate=pl.CostEstimate(
            flops=2 * depth * width * columns, bytes_accessed=6 << 20, transcendentals=0
        ),
    )(*operands, *extra)


def add_terms(left, right):
    f32 = lambda value: value.astype(jnp.float32)
    half = left.shape[0] // 2
    total = f32(left[:half]) + f32(left[half:]) + (f32(right[:half]) + f32(right[half:]))
    return jnp.concatenate(split_bits(total), axis=0)


def merge_kernel(own_ref, far_ref, vectors_ref, got_ref, sum_ref, send_ref):
    rows = own_ref.shape[0]
    sum_ref[:rows, :] = own_ref[...] + got_ref[:rows, :]
    send_ref[:rows, :] = far_ref[...] + got_ref[rows : 2 * rows, :]
    terms = jnp.concatenate(split_bits(vectors_ref[...]), axis=0)
    terms = add_terms(terms, got_ref[2 * rows :, :])
    sum_ref[rows:, :] = terms
    send_ref[rows:, :] = terms


def merge(own, far, vectors, got):
    packet = jax.ShapeDtypeStruct((got.shape[0] - own.shape[0], own.shape[1]), jnp.bfloat16)
    return pl.pallas_call(
        merge_kernel,
        out_shape=(packet, packet),
        cost_estimate=pl.CostEstimate(flops=1 << 20, bytes_accessed=4 << 20, transcendentals=0),
    )(own, far, vectors, got)


def add_kernel(left_ref, right_ref, out_ref, *, rows):
    out_ref[:rows, :] = left_ref[:rows, :] + right_ref[:rows, :]
    out_ref[rows:, :] = add_terms(left_ref[rows:, :], right_ref[rows:, :])


def add_packets(left, right, rows):
    return pl.pallas_call(
        functools.partial(add_kernel, rows=rows),
        out_shape=jax.ShapeDtypeStruct(left.shape, left.dtype),
        cost_estimate=pl.CostEstimate(flops=1 << 20, bytes_accessed=2 << 20, transcendentals=0),
    )(left, right)


def exchange(value, bit):
    size = lax.axis_size("dp")
    return lax.ppermute(value, "dp", [(i, i ^ bit) for i in range(size)])


def swap_tensor(value):
    return lax.ppermute(value, "tensor", [(0, 1), (1, 0)])


def together(*values):
    return lax.optimization_barrier(values)


def route(value, step, inward):
    pairs = []
    for far in range(2):
        for near in range(2):
            for plane in range(4):
                home = (2 * far + near) * 4 + plane
                away = (2 * far + plane // 2) * 4 + 2 * near + (step ^ (plane % 2))
                pairs.append((away, home) if inward else (home, away))
    return lax.ppermute(value, ("dp", "context"), pairs)


def pick_in(array, odd, upper):
    picked = []
    for step in range(2):
        one = jnp.where(odd, array[1 - step], array[step])
        picked.append(jnp.where(upper, one[::-1], one))
    return picked


def join_out(near, far, odd, upper):
    arranged = [jnp.where(odd, jnp.stack(v[::-1]), jnp.stack(v)) for v in (near, far)]
    own, peer = arranged
    return jnp.where(upper, jnp.stack([peer, own], axis=1), jnp.stack([own, peer], axis=1))


def gathered(shard, far_shard):
    return (shard, exchange(shard, 1), far_shard, exchange(far_shard, 1))


def inward(value):
    return lax.ppermute(value, "context", [(0, 1), (3, 2)])


def across(value):
    return lax.ppermute(value, "context", [(1, 2), (2, 1)])


def outward(value):
    return lax.ppermute(value, "context", [(1, 0), (2, 3)])


def per_device_planes(
    tokens,
    lengths,
    ln1_gain,
    ln1_bias,
    w_query,
    b_query,
    w_key,
    w_value,
    b_value,
    w_out,
    b_out,
    ln2_gain,
    ln2_bias,
    w_up,
    b_up,
    w_down,
    b_down,
    cotangent,
):
    block, width = tokens.shape[1:]
    half = block // 2
    local_width = w_query.shape[1]
    member = lax.axis_index("dp")
    near = member % 2
    plane = lax.axis_index("context")
    side = lax.axis_index("tensor")
    odd = plane % 2 == 1
    upper = side == 1
    inner = (plane == 1) | (plane == 2)
    row = lambda vector: vector.reshape(1, -1)

    by_half = (2, 2, half, width)
    picked = pick_in(tokens.reshape(by_half), odd, upper)
    *picked, w_query, w_key, w_value, w_out = together(*picked, w_query, w_key, w_value, w_out)
    rows_parts = [route(picked[step], step, True) for step in range(2)]
    proj_own = jnp.concatenate([w_query, w_key, w_value], axis=1)
    proj_far = exchange(proj_own, 2)
    proj_blocks = gathered(proj_own, proj_far)
    out_own = w_out.T
    out_own = jnp.concatenate([out_own, swap_tensor(out_own)], axis=1)
    proj_far, out_own, w_up, w_down = together(proj_far, out_own, w_up, w_down)
    pack_own = jnp.concatenate([out_own, w_up, w_down.T], axis=1)
    pack_far = exchange(pack_own, 2)

    lengths_near = jnp.where(plane // 2 == near, lengths, exchange(lengths, 1))
    length = jnp.where(odd, lengths_near[1], lengths_near[0])
    index = jnp.arange(9, dtype=jnp.int32)
    quarter = index % 4
    core = jnp.where(index < 4, near, 1 - near)
    piece = jnp.where(quarter < 2, side, 1 - side)
    starts = (2 * core + (quarter % 2 ^ plane % 2)) * block + piece * half
    info = jnp.where(index < 8, starts, length)

    rows_low, normed_low, queries, pair_own, proj = enter(
        *rows_parts, row(ln1_gain), row(ln1_bias), row(b_query), row(b_value), proj_blocks
    )
    pair_other = exchange(pair_own, 1)
    pair_other, cotangent = together(pair_other, cotangent)
    top_picked = pick_in(cotangent.reshape(by_half), odd, upper)
    top_parts = [route(top_picked[step], step, True) for step in range(2)]
    mixed, logs = attend(info, queries, pair_own, pair_other, 1)
    mixed_peer = swap_tensor(mixed)
    mixed, pack_own, pack_far = together(mixed, pack_own, pack_far)
    packs = gathered(pack_own, pack_far)

    (
        middle,
        normed_two,
        d_feed,
        hidden,
        d_pre,
        d_own,
        d_peer,
        feed_own,
        feed_peer,
        out_t,
        grad_up_bias,
        grad_down_bias,
    ) = middle_part(
        info,
        rows_low,
        mixed,
        mixed_peer,
        top_parts,
        row(ln2_gain),
        row(ln2_bias),
        row(b_out),
        packs,
        row(b_up),
    )
    got_own = swap_tensor(d_peer)
    got_peer = swap_tensor(d_own)

    own, far, send = weight_grad((d_feed, hidden))
    got = exchange(send, 1)
    shard = got.shape[0] // 2
    down_own, down_far = own + got[:shard], far + got[shard:]
    down_sum = down_own + exchange(down_far, 2)
    own, far, send = weight_grad((normed_two, d_pre))
    got = exchange(send, 1)
    up_own, up_far = own + got[:shard], far + got[shard:]
    up_far, down_sum = together(up_far, down_sum)
    up_sum = up_own + exchange(up_far, 2)

    got_own, got_peer, feed_peer = together(got_own, got_peer, feed_peer)
    feed_got = swap_tensor(feed_peer)
    d_middle, d_attention, d_mixed, sums_two = turn(
        info, middle, d_own, d_peer, got_own, got_peer, top_parts, row(ln2_gain), out_t
    )
    d_mixed, down_sum = together(d_mixed, down_sum)
    down_got = inward(down_sum)
    d_queries, d_pair, d_pair_other = attend_back(
        info, queries, pair_own, pair_other, mixed, d_mixed, logs, 1
    )
    d_pair_other, down_got, up_sum, feed_got = together(d_pair_other, down_got, up_sum, feed_got)
    down_sum = down_sum + down_got
    down_got = across(down_sum)
    up_got = inward(up_sum)
    d_proj, one_own, one_peer, sums_one, proj_bias = leave(
        rows_low, d_queries, d_pair, exchange(d_pair_other, 1), proj
    )
    sums_one = sums_one + swap_tensor(sums_one)
    one_got = swap_tensor(one_peer)
    vectors = jnp.concatenate(
        [
            grad_up_bias,
            jnp.concatenate([grad_down_bias, sums_two[2:]], axis=1),
            sums_two[:2].reshape(1, -1),
            sums_one.reshape(1, -1),
            jnp.pad(proj_bias, ((0, 0), (0, local_width))),
            jnp.zeros((3, 4 * local_width), jnp.float32),
        ],
        axis=0,
    )
    own, far, send = weight_grad((normed_low, d_proj, d_attention, mixed), vectors)
    packet, packet_far = merge(own, far, vectors, exchange(send, 1))
    packet = add_packets(packet, exchange(packet_far, 2), shard)

    first_row = info[:2, None, None] + lax.broadcasted_iota(jnp.int32, (2, half, 1), 1)
    feed = feed_own.astype(jnp.float32) + feed_got.astype(jnp.float32) + b_down.astype(jnp.float32)
    keep = (first_row < length).astype(jnp.float32)
    output_rows = middle[:block].reshape(2, half, width) + keep * feed.reshape(2, half, width)
    output_rows = output_rows.astype(jnp.bfloat16)
    out_near = [route(output_rows[step], step, False) for step in range(2)]
    output = join_out(out_near, [swap_tensor(v) for v in out_near], odd, upper)

    input_rows = finish(rows_low, one_own, one_got, row(ln1_gain), d_middle)
    in_near = [route(input_rows[step], step, False) for step in range(2)]
    input_grad = join_out(in_near, [swap_tensor(v) for v in in_near], odd, upper)

    down_sum = down_sum + down_got
    down_sum = jnp.where(inner, down_sum, outward(down_sum))
    up_sum = up_sum + up_got
    up_sum = up_sum + across(up_sum)
    up_sum = jnp.where(inner, up_sum, outward(up_sum))
    packet = add_packets(packet, inward(packet), shard)
    packet = add_packets(packet, across(packet), shard)
    packet = jnp.where(inner, packet, outward(packet)).astype(jnp.float32)

    count = vectors.shape[0]
    vectors = packet[shard : shard + count] + packet[shard + count :]
    grads = packet[:shard]
    return (
        output.reshape(tokens.shape),
        input_grad.reshape(tokens.shape),
        vectors[3, :width],
        vectors[3, width:],
        grads[:, :local_width],
        vectors[4, :local_width],
        grads[:, local_width : 2 * local_width],
        grads[:, 2 * local_width : 3 * local_width],
        vectors[4, 2 * local_width : 3 * local_width],
        grads[:, 3 * local_width :].T,
        vectors[1, width:],
        vectors[2, :width],
        vectors[2, width:],
        up_sum.astype(jnp.float32),
        vectors[0],
        down_sum.astype(jnp.float32).T,
        vectors[1, :width],
    )


def pick(mesh):
    sizes = mesh.shape
    planes = sizes["dp"] == 4 and sizes["context"] == 4 and sizes["tensor"] == 2
    return per_device_planes if planes else per_device_general


def solution(mesh):
    return jax.shard_map(
        pick(mesh),
        mesh=mesh,
        in_specs=(
            P("dp", "context", None),
            P("dp"),
            P(),
            P(),
            P("dp", "tensor"),
            P("tensor"),
            P("dp", "tensor"),
            P("dp", "tensor"),
            P("tensor"),
            P("tensor", "dp"),
            P(),
            P(),
            P(),
            P("dp", "tensor"),
            P("tensor"),
            P("tensor", "dp"),
            P(),
            P("dp", "context", None),
        ),
        out_specs=(
            P("dp", "context", None),
            P("dp", "context", None),
            P(),
            P(),
            P("dp", "tensor"),
            P("tensor"),
            P("dp", "tensor"),
            P("dp", "tensor"),
            P("tensor"),
            P("tensor", "dp"),
            P(),
            P(),
            P(),
            P("dp", "tensor"),
            P("tensor"),
            P("tensor", "dp"),
            P(),
        ),
        check_vma=False,
    )
```

```python
import functools

import jax
import jax.numpy as jnp
from jax import lax
from jax.experimental import pallas as pl
from jax.experimental.pallas import tpu as pltpu
from jax.sharding import PartitionSpec as P

HEAD_DIM = 64


epsilon = 1e-06
masked_value = -1e30


def norm_rows(values, gain_vec, bias_vec):
    average = jnp.mean(values, axis=-1, keepdims=True)
    centred = values - average
    spread = jnp.mean(centred * centred, axis=-1, keepdims=True)
    return centred * lax.rsqrt(spread + epsilon) * gain_vec + bias_vec


def gelu_tanh(values):
    return jax.nn.gelu(values, approximate=True)


def dense(left, right):
    return jnp.dot(left, right, preferred_element_type=jnp.float32)


def dense_tn(left, right):
    return lax.dot_general(
        left, right, (((0,), (0,)), ((), ())), preferred_element_type=jnp.float32
    )


def dense_nt(left, right):
    return lax.dot_general(
        left, right, (((1,), (1,)), ((), ())), preferred_element_type=jnp.float32
    )


def per_device_general(
    tokens,
    lengths,
    ln1_gain,
    ln1_bias,
    w_query,
    b_query,
    w_key,
    w_value,
    b_value,
    w_out,
    b_out,
    ln2_gain,
    ln2_bias,
    w_up,
    b_up,
    w_down,
    b_down,
    cotangent,
):
    seq_count, shard_rows, width = tokens.shape
    full_len = shard_rows * lax.axis_size("context")
    local_width = w_query.shape[1]
    local_heads = local_width // HEAD_DIM
    scale = HEAD_DIM ** (-0.5)
    row_count = seq_count * shard_rows
    query_weight, key_weight, value_weight, up_weight, out_weight, down_weight = (
        lax.all_gather(w_query, "dp", axis=0, tiled=True),
        lax.all_gather(w_key, "dp", axis=0, tiled=True),
        lax.all_gather(w_value, "dp", axis=0, tiled=True),
        lax.all_gather(w_up, "dp", axis=0, tiled=True),
        lax.all_gather(w_out, "dp", axis=1, tiled=True),
        lax.all_gather(w_down, "dp", axis=1, tiled=True),
    )
    gain_one = ln1_gain.astype(jnp.float32)
    bias_one = ln1_bias.astype(jnp.float32)
    query_bias = b_query.astype(jnp.float32)
    value_bias = b_value.astype(jnp.float32)
    out_bias = b_out.astype(jnp.float32)
    gain_two = ln2_gain.astype(jnp.float32)
    bias_two = ln2_bias.astype(jnp.float32)
    up_bias = b_up.astype(jnp.float32)
    down_bias = b_down.astype(jnp.float32)
    places = lax.axis_index("context") * shard_rows + jnp.arange(shard_rows, dtype=jnp.int32)
    keep = (places[None, :] < lengths[:, None]).astype(jnp.float32).reshape(row_count, 1)
    key_places = jnp.arange(full_len, dtype=jnp.int32)
    rows_in = tokens.reshape(row_count, width).astype(jnp.float32)
    normed_one, pull_one = jax.vjp(norm_rows, rows_in, gain_one, bias_one)
    normed_low = normed_one.astype(jnp.bfloat16)
    queries = (dense(normed_low, query_weight) + query_bias).astype(jnp.bfloat16)
    keys_own = dense(normed_low, key_weight).astype(jnp.bfloat16)
    values_own = (dense(normed_low, value_weight) + value_bias).astype(jnp.bfloat16)
    keys_whole, values_whole = (
        lax.all_gather(
            keys_own.reshape(seq_count, shard_rows, local_width), "context", axis=1, tiled=True
        ),
        lax.all_gather(
            values_own.reshape(seq_count, shard_rows, local_width), "context", axis=1, tiled=True
        ),
    )
    query_heads = queries.reshape(seq_count, shard_rows, local_heads, HEAD_DIM)
    head_outs = []
    log_sums = []
    for member in range(seq_count):
        key_heads = keys_whole[member].reshape(full_len, local_heads, HEAD_DIM)
        value_heads = values_whole[member].reshape(full_len, local_heads, HEAD_DIM)
        raw_scores = (
            jnp.einsum(
                "qhd,khd->hqk", query_heads[member], key_heads, preferred_element_type=jnp.float32
            )
            * scale
        )
        live = (key_places < lengths[member])[None, None, :]
        masked = jnp.where(live, raw_scores, masked_value)
        largest = jnp.max(masked, axis=-1, keepdims=True)
        log_total = largest + jnp.log(jnp.sum(jnp.exp(masked - largest), axis=-1, keepdims=True))
        probs_low = jnp.exp(masked - log_total).astype(jnp.bfloat16)
        mixed_heads = jnp.einsum(
            "hqk,khd->qhd", probs_low, value_heads, preferred_element_type=jnp.float32
        )
        head_outs.append(mixed_heads.reshape(shard_rows, local_width))
        log_sums.append(log_total)
    context_low = jnp.concatenate(head_outs, axis=0).astype(jnp.bfloat16)
    attention = (
        lax.psum(dense(context_low, out_weight).astype(jnp.bfloat16), "tensor").astype(jnp.float32)
        + out_bias
    )
    middle = rows_in + keep * attention
    normed_two, pull_two = jax.vjp(norm_rows, middle, gain_two, bias_two)
    normed_two_low = normed_two.astype(jnp.bfloat16)
    hidden_pre = dense(normed_two_low, up_weight) + up_bias
    hidden, pull_gelu = jax.vjp(gelu_tanh, hidden_pre)
    hidden_low = hidden.astype(jnp.bfloat16)
    feed = (
        lax.psum(dense(hidden_low, down_weight).astype(jnp.bfloat16), "tensor").astype(jnp.float32)
        + down_bias
    )
    output = (middle + keep * feed).astype(jnp.bfloat16).reshape(tokens.shape)
    grad_top = cotangent.reshape(row_count, width).astype(jnp.float32)
    d_feed = (keep * grad_top).astype(jnp.bfloat16)
    grad_down_bias = jnp.sum(d_feed.astype(jnp.float32), axis=0)
    grad_down = dense_tn(hidden_low, d_feed)
    d_hidden = dense_nt(d_feed, down_weight)
    d_pre = pull_gelu(d_hidden)[0].astype(jnp.bfloat16)
    grad_up_bias = jnp.sum(d_pre.astype(jnp.float32), axis=0)
    grad_up = dense_tn(normed_two_low, d_pre)
    d_normed_two = lax.psum(dense_nt(d_pre, up_weight).astype(jnp.bfloat16), "tensor").astype(
        jnp.float32
    )
    d_middle, grad_gain_two, grad_bias_two = pull_two(d_normed_two)
    d_middle = d_middle + grad_top
    d_attention = (keep * d_middle).astype(jnp.bfloat16)
    grad_out_bias = jnp.sum(d_attention.astype(jnp.float32), axis=0)
    grad_out = dense_tn(context_low, d_attention)
    d_context = dense_nt(d_attention, out_weight).astype(jnp.bfloat16)
    back_keys, back_values = (keys_whole, values_whole)
    d_context_heads = d_context.reshape(seq_count, shard_rows, local_heads, HEAD_DIM)
    query_grads = []
    own_grads = []
    inner_rows = []
    for member in range(seq_count):
        key_heads = back_keys[member].reshape(full_len, local_heads, HEAD_DIM)
        value_heads = back_values[member].reshape(full_len, local_heads, HEAD_DIM)
        raw_scores = (
            jnp.einsum(
                "qhd,khd->hqk", query_heads[member], key_heads, preferred_element_type=jnp.float32
            )
            * scale
        )
        live = (key_places < lengths[member])[None, None, :]
        probs = jnp.where(live, jnp.exp(raw_scores - log_sums[member]), 0.0)
        d_probs = jnp.einsum(
            "qhd,khd->hqk", d_context_heads[member], value_heads, preferred_element_type=jnp.float32
        )
        inner = jnp.sum(probs * d_probs, axis=-1, keepdims=True)
        d_scores = (probs * (d_probs - inner)).astype(jnp.bfloat16)
        d_query = (
            jnp.einsum("hqk,khd->qhd", d_scores, key_heads, preferred_element_type=jnp.float32)
            * scale
        )
        query_grads.append(d_query.reshape(shard_rows, local_width))
        inner_rows.append(inner[:, :, 0])
        d_keys = (
            jnp.einsum(
                "hqk,qhd->khd", d_scores, query_heads[member], preferred_element_type=jnp.float32
            )
            * scale
        )
        d_values = jnp.einsum(
            "hqk,qhd->khd",
            probs.astype(jnp.bfloat16),
            d_context_heads[member],
            preferred_element_type=jnp.float32,
        )
        key_term = jnp.concatenate(
            [d_keys.reshape(full_len, local_width), d_values.reshape(full_len, local_width)], axis=1
        )
        own_grads.append(
            lax.psum_scatter(
                key_term.astype(jnp.bfloat16), "context", scatter_dimension=0, tiled=True
            ).astype(jnp.float32)
        )
    d_query_low = jnp.concatenate(query_grads, axis=0).astype(jnp.bfloat16)
    key_value_grads = jnp.concatenate(own_grads, axis=0)
    d_keys_low = key_value_grads[:, :local_width].astype(jnp.bfloat16)
    d_values_low = key_value_grads[:, local_width:].astype(jnp.bfloat16)
    grad_query = dense_tn(normed_low, d_query_low)
    grad_query_bias = jnp.sum(d_query_low.astype(jnp.float32), axis=0)
    grad_key = dense_tn(normed_low, d_keys_low)
    grad_value = dense_tn(normed_low, d_values_low)
    grad_value_bias = jnp.sum(d_values_low.astype(jnp.float32), axis=0)
    d_normed_one = lax.psum(
        (
            dense_nt(d_query_low, query_weight)
            + dense_nt(d_keys_low, key_weight)
            + dense_nt(d_values_low, value_weight)
        ).astype(jnp.bfloat16),
        "tensor",
    ).astype(jnp.float32)
    d_rows, grad_gain_one, grad_bias_one = pull_one(d_normed_one)
    input_grad = (d_rows + d_middle).astype(jnp.bfloat16).reshape(tokens.shape)
    data_sums = (
        lax.psum_scatter(
            grad_query.astype(jnp.bfloat16), "dp", scatter_dimension=0, tiled=True
        ).astype(jnp.float32),
        lax.psum_scatter(
            grad_key.astype(jnp.bfloat16), "dp", scatter_dimension=0, tiled=True
        ).astype(jnp.float32),
        lax.psum_scatter(
            grad_value.astype(jnp.bfloat16), "dp", scatter_dimension=0, tiled=True
        ).astype(jnp.float32),
        lax.psum_scatter(
            grad_up.astype(jnp.bfloat16), "dp", scatter_dimension=0, tiled=True
        ).astype(jnp.float32),
        lax.psum_scatter(
            grad_out.astype(jnp.bfloat16), "dp", scatter_dimension=1, tiled=True
        ).astype(jnp.float32),
        lax.psum_scatter(
            grad_down.astype(jnp.bfloat16), "dp", scatter_dimension=1, tiled=True
        ).astype(jnp.float32),
    )
    owned_sums = (
        lax.psum(data_sums[0].astype(jnp.bfloat16), "context").astype(jnp.float32),
        lax.psum(data_sums[1].astype(jnp.bfloat16), "context").astype(jnp.float32),
        lax.psum(data_sums[2].astype(jnp.bfloat16), "context").astype(jnp.float32),
        lax.psum(data_sums[3].astype(jnp.bfloat16), "context").astype(jnp.float32),
        lax.psum(data_sums[4].astype(jnp.bfloat16), "context").astype(jnp.float32),
        lax.psum(data_sums[5].astype(jnp.bfloat16), "context").astype(jnp.float32),
    )
    small_sums = lax.psum(
        (
            grad_gain_one,
            grad_bias_one,
            grad_query_bias,
            grad_value_bias,
            grad_out_bias,
            grad_gain_two,
            grad_bias_two,
            grad_up_bias,
            grad_down_bias,
        ),
        ("dp", "context"),
    )
    return (
        output,
        input_grad,
        small_sums[0],
        small_sums[1],
        owned_sums[0],
        small_sums[2],
        owned_sums[1],
        owned_sums[2],
        small_sums[3],
        owned_sums[4],
        small_sums[4],
        small_sums[5],
        small_sums[6],
        owned_sums[3],
        small_sums[7],
        owned_sums[5],
        small_sums[8],
    )


def live_bias(info, count):
    places = lax.broadcasted_iota(jnp.int32, (count, 2 * HEAD_DIM), 0)
    return jnp.concatenate(
        [jnp.where(info[k] + places < info[8], 0.0, masked_value) for k in range(8)], axis=0
    ).astype(jnp.bfloat16)


def split_pair(array, extra):
    lane = lax.broadcasted_iota(jnp.int32, array.shape, 1)
    zero = jnp.zeros((), jnp.bfloat16)
    left = jnp.where(lane < HEAD_DIM, array, jnp.where(lane == HEAD_DIM, extra, zero))
    right = jnp.where(lane >= HEAD_DIM, array, jnp.where(lane == 0, extra, zero))
    return left, right


LOG_SCALE = HEAD_DIM ** (-0.5) * 1.4426950408889634


def attend_kernel(info, query_ref, own_ref, other_ref, out_ref, log_ref):
    pair = 2 * HEAD_DIM
    count = query_ref.shape[0] // 4
    keys = jnp.concatenate([own_ref[:, :pair], other_ref[:, :pair]], axis=0)
    values = jnp.concatenate([own_ref[:, pair:], other_ref[:, pair:]], axis=0)
    values_t = values.T
    key_heads = split_pair(keys, live_bias(info, count))
    query_heads = split_pair(query_ref[...], jnp.ones((), jnp.bfloat16))
    mixed = []
    for head in range(2):
        scores = dense_nt(key_heads[head], query_heads[head])
        largest = jnp.max(scores, axis=0, keepdims=True)
        weights = jnp.exp2((scores - largest) * LOG_SCALE)
        total = jnp.sum(weights, axis=0, keepdims=True)
        dims = slice(head * HEAD_DIM, (head + 1) * HEAD_DIM)
        mixed.append(dense(values_t[dims], weights.astype(jnp.bfloat16)) / total)
        log_ref[0, head : head + 1, :] = largest * LOG_SCALE + jnp.log2(total)
    out_ref[...] = jnp.concatenate(mixed, axis=0).T.astype(jnp.bfloat16)


def attend(info, queries, pair_own, pair_other):
    rows, width = queries.shape
    pair = 2 * HEAD_DIM
    groups = width // pair
    work = 4 * rows * 2 * rows * width
    return pl.pallas_call(
        attend_kernel,
        out_shape=(
            jax.ShapeDtypeStruct((rows, width), jnp.bfloat16),
            jax.ShapeDtypeStruct((groups, 2, rows), jnp.float32),
        ),
        grid_spec=pltpu.PrefetchScalarGridSpec(
            num_scalar_prefetch=1,
            grid=(groups,),
            in_specs=[
                pl.BlockSpec((rows, pair), lambda g, info: (0, g)),
                pl.BlockSpec((rows, 2 * pair), lambda g, info: (0, g)),
                pl.BlockSpec((rows, 2 * pair), lambda g, info: (0, g)),
            ],
            out_specs=(
                pl.BlockSpec((rows, pair), lambda g, info: (0, g)),
                pl.BlockSpec((1, 2, rows), lambda g, info: (g, 0, 0)),
            ),
        ),
        compiler_params=pltpu.CompilerParams(vmem_limit_bytes=48 << 20),
        cost_estimate=pl.CostEstimate(
            flops=4 * work, bytes_accessed=12 * rows * width, transcendentals=work // (2 * HEAD_DIM)
        ),
    )(info, queries, pair_own, pair_other)


def attend_back_kernel(
    info,
    query_ref,
    own_ref,
    other_ref,
    out_ref,
    d_own_ref,
    d_peer_ref,
    proj_ref,
    log_ref,
    d_query_ref,
    d_pair_ref,
    d_other_ref,
):
    pair = 2 * HEAD_DIM
    rows = query_ref.shape[0]
    scale = HEAD_DIM ** (-0.5)
    keys = jnp.concatenate([own_ref[:, :pair], other_ref[:, :pair]], axis=0)
    values = jnp.concatenate([own_ref[:, pair:], other_ref[:, pair:]], axis=0)
    keys_t = keys.T
    key_heads = split_pair(keys, live_bias(info, rows // 4))
    value_heads = split_pair(values, jnp.zeros((), jnp.bfloat16))
    query = query_ref[...]
    query_heads = split_pair(query, jnp.ones((), jnp.bfloat16))
    d_att = jnp.concatenate([d_own_ref[...], d_peer_ref[...]], axis=0)
    grad = dense(d_att, proj_ref[...]).astype(jnp.bfloat16)
    inner_t = (grad.astype(jnp.float32) * out_ref[...].astype(jnp.float32)).T
    d_query, d_keys, d_values = [], [], []
    for head in range(2):
        dims = slice(head * HEAD_DIM, (head + 1) * HEAD_DIM)
        inner = jnp.sum(inner_t[dims], axis=0, keepdims=True)
        scores = dense_nt(key_heads[head], query_heads[head])
        probs = jnp.exp2(scores * LOG_SCALE - log_ref[0, head : head + 1, :])
        d_probs = dense_nt(value_heads[head], grad)
        d_scores = (probs * (d_probs - inner)).astype(jnp.bfloat16)
        d_query.append(dense(keys_t[dims], d_scores))
        d_keys.append(dense(d_scores, query))
        d_values.append(dense(probs.astype(jnp.bfloat16), grad))
    d_query_ref[...] = (jnp.concatenate(d_query, axis=0).T * scale).astype(jnp.bfloat16)
    left = lax.broadcasted_iota(jnp.int32, d_keys[0].shape, 1) < HEAD_DIM
    d_key = (jnp.where(left, d_keys[0], d_keys[1]) * scale).astype(jnp.bfloat16)
    d_value = jnp.where(left, d_values[0], d_values[1]).astype(jnp.bfloat16)
    d_pair_ref[:, :pair] = d_key[:rows]
    d_pair_ref[:, pair:] = d_value[:rows]
    d_other_ref[:, :pair] = d_key[rows:]
    d_other_ref[:, pair:] = d_value[rows:]


def attend_back(info, queries, pair_own, pair_other, mixed, d_own, d_peer, out_t, logs):
    rows, local = queries.shape
    width = out_t.shape[0]
    pair = 2 * HEAD_DIM
    work = 4 * rows * 2 * rows * local
    narrow = pl.BlockSpec((rows, pair), lambda g, info: (0, g))
    wide = pl.BlockSpec((rows, 2 * pair), lambda g, info: (0, g))
    halves = pl.BlockSpec((rows // 2, width), lambda g, info: (0, 0))
    return pl.pallas_call(
        attend_back_kernel,
        out_shape=tuple(
            jax.ShapeDtypeStruct((rows, columns), jnp.bfloat16)
            for columns in (local, 2 * local, 2 * local)
        ),
        grid_spec=pltpu.PrefetchScalarGridSpec(
            num_scalar_prefetch=1,
            grid=(local // pair,),
            in_specs=[
                narrow,
                wide,
                wide,
                narrow,
                halves,
                halves,
                pl.BlockSpec((width, pair), lambda g, info: (0, g)),
                pl.BlockSpec((1, 2, rows), lambda g, info: (g, 0, 0)),
            ],
            out_specs=(narrow, wide, wide),
        ),
        compiler_params=pltpu.CompilerParams(vmem_limit_bytes=48 << 20),
        cost_estimate=pl.CostEstimate(
            flops=10 * work, bytes_accessed=24 * rows * local, transcendentals=work // (2 * HEAD_DIM)
        ),
    )(info, queries, pair_own, pair_other, mixed, d_own, d_peer, out_t, logs)


def held(info, quarters, count, width):
    places = lax.broadcasted_iota(jnp.int32, (count, width), 0)
    return jnp.concatenate([info[k] + places < info[8] for k in range(quarters)], axis=0)


def fixed(array):
    return pl.BlockSpec(array.shape, lambda i: (0,) * len(array.shape))


def call_once(kernel, args, shapes, flops, scratch=()):
    moved = sum(a.size * a.dtype.itemsize for a in (*args, *shapes))
    return pl.pallas_call(
        kernel,
        out_shape=tuple(shapes),
        grid=(1,),
        in_specs=[fixed(a) for a in args],
        out_specs=tuple(fixed(s) for s in shapes),
        scratch_shapes=list(scratch),
        compiler_params=pltpu.CompilerParams(vmem_limit_bytes=48 << 20),
        cost_estimate=pl.CostEstimate(flops=flops, bytes_accessed=moved, transcendentals=0),
    )(*args)


def low(*shape):
    return jax.ShapeDtypeStruct(shape, jnp.bfloat16)


def full(*shape):
    return jax.ShapeDtypeStruct(shape, jnp.float32)


def row_stats(values):
    centred = values - jnp.mean(values, axis=-1, keepdims=True)
    spread = jnp.mean(centred * centred, axis=-1, keepdims=True)
    root = lax.rsqrt(spread + epsilon)
    return centred * root, root


def row_pull(normed, root, grad):
    return root * (
        grad
        - jnp.mean(grad, axis=-1, keepdims=True)
        - normed * jnp.mean(grad * normed, axis=-1, keepdims=True)
    )


def settle(parts, out_ref):
    rows = parts[0].shape[0]
    mine = lax.axis_index("dp")
    for step, part in enumerate(parts):
        start = pl.multiple_of((mine ^ step) * rows, rows)
        out_ref[pl.ds(start, rows), :] = part[...]


def enter_kernel(
    own0, own1, peer0, peer1, gain_ref, bias_ref, q_bias_ref, v_bias_ref, a, b, c, d,
    rows_ref, normed_ref, query_ref, pair_ref, proj_ref,
):
    pair = 2 * HEAD_DIM
    settle((a, b, c, d), proj_ref)
    rows = jnp.concatenate([own0[...], own1[...], peer0[...], peer1[...]], axis=0)
    rows_ref[...] = rows
    normed, _ = row_stats(rows.astype(jnp.float32))
    normed = normed * gain_ref[...].astype(jnp.float32) + bias_ref[...].astype(jnp.float32)
    normed = normed.astype(jnp.bfloat16)
    normed_ref[...] = normed
    local = query_ref.shape[1]
    mixed = dense(normed, proj_ref[...])
    query_ref[...] = (mixed[:, :local] + q_bias_ref[...].astype(jnp.float32)).astype(jnp.bfloat16)
    for g in range(local // pair):
        cols = slice(g * pair, (g + 1) * pair)
        key = mixed[:, local + g * pair : local + (g + 1) * pair]
        value = mixed[:, 2 * local + g * pair : 2 * local + (g + 1) * pair]
        value = value + v_bias_ref[:, cols].astype(jnp.float32)
        pair_ref[:, 2 * g * pair : (2 * g + 1) * pair] = key.astype(jnp.bfloat16)
        pair_ref[:, (2 * g + 1) * pair : (2 * g + 2) * pair] = value.astype(jnp.bfloat16)


def enter(pieces, gain, bias, q_bias, v_bias, blocks):
    half, width = pieces[0].shape
    rows = 4 * half
    local = q_bias.shape[1]
    shapes = (
        low(rows, width),
        low(rows, width),
        low(rows, local),
        low(rows, 2 * local),
        low(width, 3 * local),
    )
    args = (*pieces, gain, bias, q_bias, v_bias, *blocks)
    return call_once(enter_kernel, args, shapes, 6 * rows * width * local)


ROOT_TWO_OVER_PI = 0.7978845608028654
CUBE = 0.044715


def middle_kernel(
    info, rows_ref, own_ref, peer_ref, top0, top1, top2, top3, gain_ref, bias_ref, out_bias_ref,
    oa, ob, oc, od, ua, ub, uc, ud, da, db, dc, dd, up_bias_ref,
    mid_ref, normed_ref, feed_ref, hidden_ref, d_pre_ref, d_own_ref, d_peer_ref,
    f_own_ref, f_peer_ref, out_ref, g_up_ref, g_down_ref,
    outs, ups, downs, acc_d, acc_f,
):
    step = pl.program_id(0)
    rows, width = rows_ref.shape
    half = rows // 2
    local = own_ref.shape[1]

    @pl.when(step == 0)
    def _():
        settle((oa, ob, oc, od), outs)
        out_ref[...] = outs[:, :local]
        peer = jnp.concatenate([peer_ref[half:, :], peer_ref[:half, :]], axis=0)
        attention = (
            dense_nt(own_ref[...], outs[:, :local])
            + dense_nt(peer, outs[:, local:])
            + out_bias_ref[...].astype(jnp.float32)
        )
        real = held(info, 4, rows // 4, width)
        mid = rows_ref[...].astype(jnp.float32) + jnp.where(real, attention, 0.0)
        mid_ref[...] = mid
        normed, _ = row_stats(mid)
        normed = normed * gain_ref[...].astype(jnp.float32) + bias_ref[...].astype(jnp.float32)
        normed_ref[...] = normed.astype(jnp.bfloat16)
        top = jnp.concatenate([top0[...], top1[...], top2[...], top3[...]], axis=0)
        feed = jnp.where(real, top.astype(jnp.float32), 0.0)
        feed_ref[...] = feed.astype(jnp.bfloat16)
        g_down_ref[...] = jnp.sum(feed, axis=0, keepdims=True)
        acc_d[...] = jnp.zeros_like(acc_d)
        acc_f[...] = jnp.zeros_like(acc_f)

    settle((ua, ub, uc, ud), ups)
    settle((da, db, dc, dd), downs)
    pre = dense(normed_ref[...], ups[...]) + up_bias_ref[...].astype(jnp.float32)
    d_hidden = dense(feed_ref[...], downs[...])
    square = pre * pre
    bend = jnp.tanh(ROOT_TWO_OVER_PI * pre * (1.0 + CUBE * square))
    half_up = 0.5 + 0.5 * bend
    hidden = (pre * half_up).astype(jnp.bfloat16)
    slope = half_up + (pre * half_up) * (1.0 - bend) * (
        ROOT_TWO_OVER_PI + 3.0 * CUBE * ROOT_TWO_OVER_PI * square
    )
    d_pre = (d_hidden * slope).astype(jnp.bfloat16)
    hidden_ref[...] = hidden
    d_pre_ref[...] = d_pre
    g_up_ref[...] = jnp.sum(d_pre.astype(jnp.float32), axis=0, keepdims=True)
    acc_d[...] += dense_nt(d_pre, ups[...])
    acc_f[...] += dense_nt(hidden, downs[...])

    @pl.when(step == pl.num_programs(0) - 1)
    def _():
        low = acc_d[...].astype(jnp.bfloat16)
        d_own_ref[...] = low[:half]
        d_peer_ref[...] = low[half:]
        low = acc_f[...].astype(jnp.bfloat16)
        f_own_ref[...] = low[:half]
        f_peer_ref[...] = low[half:]


def middle_part(info, rows_low, own, peer, top, gain, bias, out_bias, packs, downs, up_bias):
    rows, width = rows_low.shape
    local = own.shape[1]
    shard = downs[0].shape[0]
    hidden = up_bias.shape[1]
    tile = 384
    fixed = lambda array: pl.BlockSpec(array.shape, lambda i, info: (0,) * len(array.shape))
    columns = lambda height: pl.BlockSpec((height, tile), lambda i, info: (0, i))
    outs = pl.BlockSpec((shard, width), lambda i, info: (0, hidden // width))
    whole = (rows_low, own, peer, *top, gain, bias, out_bias)
    shapes = (
        full(rows, width),
        low(rows, width),
        low(rows, width),
        low(rows, hidden),
        low(rows, hidden),
        low(rows // 2, width),
        low(rows // 2, width),
        low(rows // 2, width),
        low(rows // 2, width),
        low(width, local),
        full(1, hidden),
        full(1, width),
    )
    tiled = (3, 4, 10)
    return pl.pallas_call(
        middle_kernel,
        out_shape=shapes,
        grid_spec=pltpu.PrefetchScalarGridSpec(
            num_scalar_prefetch=1,
            grid=(hidden // tile,),
            in_specs=[fixed(a) for a in whole] + [outs] * 4 + [columns(shard)] * 8 + [columns(1)],
            out_specs=tuple(
                columns(s.shape[0]) if k in tiled else fixed(s) for k, s in enumerate(shapes)
            ),
            scratch_shapes=[
                pltpu.VMEM((width, 2 * local), jnp.bfloat16),
                pltpu.VMEM((width, tile), jnp.bfloat16),
                pltpu.VMEM((width, tile), jnp.bfloat16),
                pltpu.VMEM((rows, width), jnp.float32),
                pltpu.VMEM((rows, width), jnp.float32),
            ],
        ),
        compiler_params=pltpu.CompilerParams(vmem_limit_bytes=52 << 20),
        cost_estimate=pl.CostEstimate(
            flops=8 * rows * width * hidden, bytes_accessed=20 << 20, transcendentals=rows * hidden
        ),
    )(info, *whole, *packs, *packs, *downs, up_bias)


def turn_kernel(
    info, mid_ref, d_own_ref, got_ref, top0, top1, gain_ref, d_mid_ref, d_att_ref, sums_ref
):
    half, width = d_own_ref.shape
    grad = d_own_ref[...].astype(jnp.float32) + got_ref[...].astype(jnp.float32)
    normed, root = row_stats(mid_ref[...])
    top = jnp.concatenate([top0[...], top1[...]], axis=0).astype(jnp.float32)
    d_mid = top + row_pull(normed, root, grad * gain_ref[...].astype(jnp.float32))
    d_mid_ref[...] = d_mid
    d_att = jnp.where(held(info, 2, half // 2, width), d_mid, 0.0).astype(jnp.bfloat16)
    d_att_ref[...] = d_att
    sums_ref[0:1, :] = jnp.sum(grad * normed, axis=0, keepdims=True)
    sums_ref[1:2, :] = jnp.sum(grad, axis=0, keepdims=True)
    sums_ref[2:3, :] = jnp.sum(d_att.astype(jnp.float32), axis=0, keepdims=True)


def turn(info, mid, d_own, got, top, gain):
    half, width = d_own.shape
    fixed = lambda a: pl.BlockSpec(a.shape, lambda i, info: (0,) * len(a.shape))
    first = pl.BlockSpec((half, width), lambda i, info: (0, 0))
    shapes = (
        jax.ShapeDtypeStruct((half, width), jnp.float32),
        jax.ShapeDtypeStruct((half, width), jnp.bfloat16),
        jax.ShapeDtypeStruct((3, width), jnp.float32),
    )
    return pl.pallas_call(
        turn_kernel,
        out_shape=shapes,
        grid_spec=pltpu.PrefetchScalarGridSpec(
            num_scalar_prefetch=1,
            grid=(1,),
            in_specs=[first, fixed(d_own), fixed(got), fixed(top[0]), fixed(top[1]), fixed(gain)],
            out_specs=tuple(fixed(s) for s in shapes),
        ),
        compiler_params=pltpu.CompilerParams(vmem_limit_bytes=32 << 20),
        cost_estimate=pl.CostEstimate(
            flops=40 * half * width, bytes_accessed=4 << 20, transcendentals=half
        ),
    )(info, mid, d_own, got, *top, gain)


def leave_kernel(
    rows_ref, proj_ref, d_query_ref, d_pair_ref, got_ref,
    d_proj_ref, own_ref, peer_ref, sums_ref, bias_ref,
):
    pair = 2 * HEAD_DIM
    rows, local = d_query_ref.shape
    half = rows // 2
    d_proj_ref[:, :local] = d_query_ref[...]
    total = (d_pair_ref[...].astype(jnp.float32) + got_ref[...].astype(jnp.float32)).astype(
        jnp.bfloat16
    )
    for g in range(local // pair):
        for k in range(2):
            start = (k + 1) * local + g * pair
            d_proj_ref[:, start : start + pair] = total[:, (2 * g + k) * pair : (2 * g + k + 1) * pair]
    d_proj = d_proj_ref[...]
    bias_ref[...] = jnp.sum(d_proj.astype(jnp.float32), axis=0, keepdims=True)
    grad = dense_nt(d_proj, proj_ref[...])
    low = grad.astype(jnp.bfloat16)
    own_ref[...] = low[:half]
    peer_ref[...] = low[half:]
    normed, _ = row_stats(rows_ref[...].astype(jnp.float32))
    sums_ref[0:1, :] = jnp.sum(grad * normed, axis=0, keepdims=True)
    sums_ref[1:2, :] = jnp.sum(grad, axis=0, keepdims=True)


def leave(rows_low, proj, d_query, d_pair, got):
    rows, width = rows_low.shape
    columns = proj.shape[1]
    shapes = (
        low(rows, columns),
        low(rows // 2, width),
        low(rows // 2, width),
        full(2, width),
        full(1, columns),
    )
    args = (rows_low, proj, d_query, d_pair, got)
    return call_once(leave_kernel, args, shapes, 2 * rows * width * columns)


def finish_kernel(rows_ref, own_ref, got_ref, gain_ref, d_mid_ref, first_ref, second_ref):
    half = rows_ref.shape[0]
    normed, root = row_stats(rows_ref[...].astype(jnp.float32))
    grad = own_ref[...].astype(jnp.float32) + got_ref[...].astype(jnp.float32)
    d_rows = row_pull(normed, root, grad * gain_ref[...].astype(jnp.float32)) + d_mid_ref[...]
    low = d_rows.astype(jnp.bfloat16)
    first_ref[...] = low[: half // 2]
    second_ref[...] = low[half // 2 :]


def finish(rows_low, own, got, gain, d_mid):
    half, width = own.shape
    top_half = pl.BlockSpec((half, width), lambda i: (0, 0))
    fixed = lambda a: pl.BlockSpec(a.shape, lambda i: (0,) * a.ndim)
    piece = jax.ShapeDtypeStruct((half // 2, width), jnp.bfloat16)
    return pl.pallas_call(
        finish_kernel,
        out_shape=(piece, piece),
        grid=(1,),
        in_specs=[top_half, fixed(own), fixed(got), fixed(gain), fixed(d_mid)],
        out_specs=(fixed(piece), fixed(piece)),
        compiler_params=pltpu.CompilerParams(vmem_limit_bytes=32 << 20),
        cost_estimate=pl.CostEstimate(
            flops=20 * half * width, bytes_accessed=4 << 20, transcendentals=half
        ),
    )(rows_low, own, got, gain, d_mid)


def weight_grad_kernel(*refs, counts):
    lefts, used = [], 0
    for count in counts:
        lefts.append((refs[used : used + count], refs[used + count]))
        used += count + 1
    own_ref, far_ref, send_ref = refs[used : used + 3]
    rows = own_ref.shape[0]
    mine = lax.axis_index("dp")
    targets = (own_ref, send_ref.at[:rows], far_ref, send_ref.at[rows:])
    start = 0
    for (pieces, right), turned in zip(lefts, refs[used + 3 :]):
        turned[...] = jnp.concatenate([piece[...] for piece in pieces], axis=0).T
        width = right.shape[1]
        for step, target in enumerate(targets):
            place = pl.multiple_of((mine ^ step) * rows, rows)
            grad = dense(turned[pl.ds(place, rows), :], right[...])
            target[:, start : start + width] = grad.astype(jnp.bfloat16)
        start += width


def split_bits(values):
    high = values.astype(jnp.bfloat16)
    return high, (values - high.astype(jnp.float32)).astype(jnp.bfloat16)


def weight_grad(*products):
    depth, width = products[0][-1].shape[0], products[0][0].shape[1]
    columns = sum(product[-1].shape[1] for product in products)
    rows = width // 4
    shapes = (low(rows, columns), low(rows, columns), low(2 * rows, columns))
    turned = [pltpu.VMEM((width, depth), jnp.bfloat16)] * len(products)
    kernel = functools.partial(
        weight_grad_kernel, counts=tuple(len(product) - 1 for product in products)
    )
    args = [array for product in products for array in product]
    return call_once(kernel, args, shapes, 2 * depth * width * columns, turned)


def add_terms(left, right):
    f32 = lambda value: value.astype(jnp.float32)
    half = left.shape[0] // 2
    total = f32(left[:half]) + f32(left[half:]) + (f32(right[:half]) + f32(right[half:]))
    return jnp.concatenate(split_bits(total), axis=0)


def merge_kernel(own_ref, far_ref, got_ref, mine_ref, theirs_ref, sum_ref, send_ref):
    rows = own_ref.shape[0]
    sum_ref[:rows, :] = own_ref[...] + got_ref[:rows, :]
    send_ref[:rows, :] = far_ref[...] + got_ref[rows:, :]
    terms = jnp.concatenate(split_bits(mine_ref[...] + theirs_ref[...]), axis=0)
    sum_ref[rows:, :] = terms
    send_ref[rows:, :] = terms


def merge(own, far, got, mine, theirs):
    rows, columns = own.shape
    packet = low(rows + 2 * mine.shape[0], columns)
    args = (own, far, got, mine, theirs)
    return call_once(merge_kernel, args, (packet, packet), own.size)


def add_kernel(left_ref, right_ref, out_ref, *, rows):
    out_ref[:rows, :] = left_ref[:rows, :] + right_ref[:rows, :]
    out_ref[rows:, :] = add_terms(left_ref[rows:, :], right_ref[rows:, :])


def add_packets(left, right, rows):
    kernel = functools.partial(add_kernel, rows=rows)
    return call_once(kernel, (left, right), (low(*left.shape),), left.size)[0]


def exchange(value, bit):
    size = lax.axis_size("dp")
    return lax.ppermute(value, "dp", [(i, i ^ bit) for i in range(size)])


def swap_tensor(value):
    return lax.ppermute(value, "tensor", [(0, 1), (1, 0)])


def together(*values):
    return lax.optimization_barrier(values)


def route(value, step, inward):
    pairs = []
    for far in range(2):
        for near in range(2):
            for plane in range(4):
                home = (2 * far + near) * 4 + plane
                away = (2 * far + plane // 2) * 4 + 2 * near + (step ^ (plane % 2))
                pairs.append((away, home) if inward else (home, away))
    return lax.ppermute(value, ("dp", "context"), pairs)


def pick_in(array, odd, upper):
    mine = jnp.where(upper, array[:, 1], array[:, 0])
    return [jnp.where(odd, mine[1 - step], mine[step]) for step in range(2)]


def join_out(near, far, odd, upper):
    arranged = [jnp.where(odd, jnp.stack(v[::-1]), jnp.stack(v)) for v in (near, far)]
    own, peer = arranged
    return jnp.where(upper, jnp.stack([peer, own], axis=1), jnp.stack([own, peer], axis=1))


def gathered(shard, far_shard):
    return (shard, exchange(shard, 1), far_shard, exchange(far_shard, 1))


def edges(value):
    return lax.ppermute(value, "context", [(0, 1), (1, 0), (2, 3), (3, 2)])


def inward(value):
    return lax.ppermute(value, "context", [(0, 1), (3, 2)])


def across(value):
    return lax.ppermute(value, "context", [(1, 2), (2, 1)])


def outward(value):
    return lax.ppermute(value, "context", [(1, 0), (2, 3)])


def per_device_planes(
    tokens,
    lengths,
    ln1_gain,
    ln1_bias,
    w_query,
    b_query,
    w_key,
    w_value,
    b_value,
    w_out,
    b_out,
    ln2_gain,
    ln2_bias,
    w_up,
    b_up,
    w_down,
    b_down,
    cotangent,
):
    block, width = tokens.shape[1:]
    half = block // 2
    local_width = w_query.shape[1]
    member = lax.axis_index("dp")
    near = member % 2
    plane = lax.axis_index("context")
    side = lax.axis_index("tensor")
    odd = plane % 2 == 1
    upper = side == 1
    inner = (plane == 1) | (plane == 2)
    row = lambda vector: vector.reshape(1, -1)

    by_half = (2, 2, half, width)
    groups = local_width // (2 * HEAD_DIM)
    picked = pick_in(tokens.reshape(by_half), odd, upper)
    *picked, w_query, w_key, w_value = together(*picked, w_query, w_key, w_value)
    rows_parts = [route(picked[step], step, True) for step in range(2)]
    proj_own = jnp.concatenate([w_query, w_key, w_value], axis=1)
    proj_far = exchange(proj_own, 2)
    proj_near = exchange(proj_own, 1)
    out_own = w_out.T
    out_peer = swap_tensor(out_own)
    lengths_other = exchange(lengths, 1)
    *rows_parts, proj_far, proj_near, out_peer, lengths_other, w_down, cotangent = together(
        *rows_parts, proj_far, proj_near, out_peer, lengths_other, w_down, cotangent
    )

    rows_parts += [swap_tensor(v) for v in rows_parts]
    proj_last = exchange(proj_far, 1)
    down_own = w_down.T
    down_far = exchange(down_own, 2)
    top_picked = pick_in(cotangent.reshape(by_half), odd, upper)
    top_parts = [route(top_picked[step], step, True) for step in range(2)]
    *rows_parts, proj_last, down_far, w_up, top_0, top_1 = together(
        *rows_parts, proj_last, down_far, w_up, *top_parts
    )

    pack_own = jnp.concatenate([w_up, out_own, out_peer], axis=1)
    pack_far = exchange(pack_own, 2)
    top_parts = [top_0, top_1, swap_tensor(top_0), swap_tensor(top_1)]
    proj_blocks = (proj_own, proj_near, proj_far, proj_last)
    lengths_near = jnp.where(plane // 2 == near, lengths, lengths_other)
    length = jnp.where(odd, lengths_near[1], lengths_near[0])
    index = jnp.arange(9, dtype=jnp.int32)
    quarter = index % 4
    core = jnp.where(index < 4, near, 1 - near)
    piece = jnp.where(quarter < 2, side, 1 - side)
    starts = (2 * core + (quarter % 2 ^ plane % 2)) * block + piece * half
    info = jnp.where(index < 8, starts, length)

    rows_low, normed_low, queries, pair_own, proj = enter(
        rows_parts, row(ln1_gain), row(ln1_bias), row(b_query), row(b_value), proj_blocks
    )
    pair_other = exchange(pair_own, 1)
    mixed, logs = attend(info, queries, pair_own, pair_other)

    mixed, down_own, down_far, pack_own, *top_parts = together(
        mixed, down_own, down_far, pack_own, *top_parts
    )
    mixed_peer = swap_tensor(mixed)
    down_blocks = gathered(down_own, down_far)
    pack_near = exchange(pack_own, 1)
    mixed_peer, pack_near, pack_far, *down_blocks = together(
        mixed_peer, pack_near, pack_far, *down_blocks
    )
    pack_blocks = (pack_own, pack_near, pack_far, exchange(pack_far, 1))
    (
        middle,
        normed_two,
        d_feed,
        hidden,
        d_pre,
        d_own,
        d_peer,
        feed_own,
        feed_peer,
        out_t,
        grad_up_bias,
        grad_down_bias,
    ) = middle_part(
        info,
        rows_low,
        mixed,
        mixed_peer,
        top_parts,
        row(ln2_gain),
        row(ln2_bias),
        row(b_out),
        pack_blocks,
        down_blocks,
        row(b_up),
    )

    got = swap_tensor(d_peer)
    down_own, down_far, down_send = weight_grad((d_feed, hidden))
    up_own, up_far, up_send = weight_grad((normed_two, d_pre))
    got, down_send, up_send, feed_peer = together(got, down_send, up_send, feed_peer)

    down_got = exchange(down_send, 1)
    d_middle, d_att, sums_two = turn(info, middle, d_own, got, top_parts[:2], row(ln2_gain))
    d_att, down_got, up_send = together(d_att, down_got, up_send)

    shard = down_own.shape[0]
    columns = hidden.shape[1]
    d_att_peer = swap_tensor(d_att)
    got_1 = exchange(down_far + down_got[shard:], 2)
    down_own = down_own + down_got[:shard]
    up_got = exchange(up_send, 1)
    d_att_peer, got_1, up_got, feed_peer = together(d_att_peer, got_1, up_got, feed_peer)

    sum_1 = down_own + got_1
    got_1 = inward(sum_1)
    got_2 = exchange(up_far + up_got[shard:], 2)
    up_own = up_own + up_got[:shard]
    feed_got = swap_tensor(feed_peer)
    d_queries, d_pair, d_send = attend_back(
        info, queries, pair_own, pair_other, mixed, d_att, d_att_peer, out_t, logs
    )
    d_send, got_1, got_2, feed_got = together(d_send, got_1, got_2, feed_got)

    first_row = info[:2, None, None] + lax.broadcasted_iota(jnp.int32, (2, half, 1), 1)
    feed = feed_own.astype(jnp.float32) + feed_got.astype(jnp.float32) + b_down.astype(jnp.float32)
    keep = (first_row < length).astype(jnp.float32)
    output_rows = middle[:block].reshape(2, half, width) + keep * feed.reshape(2, half, width)
    output_rows = output_rows.astype(jnp.bfloat16)
    out_near = [route(output_rows[step], step, False) for step in range(2)]
    sum_1 = sum_1 + got_1
    sum_2 = up_own + got_2
    d_proj, one_own, one_peer, sums_one, proj_bias = leave(
        rows_low, proj, d_queries, d_pair, exchange(d_send, 1)
    )
    sides = jnp.concatenate([sums_one, sums_two], axis=0)
    one_peer, sides, sum_1, sum_2, *out_near = together(one_peer, sides, sum_1, sum_2, *out_near)

    one_got = swap_tensor(one_peer)
    got_1 = across(sum_1)
    got_2 = inward(sum_2)
    own, far, send = weight_grad((normed_low, d_proj), (d_att, d_att_peer, mixed))
    send, one_got, got_1, got_2 = together(send, one_got, got_1, got_2)

    input_rows = finish(rows_low, one_own, one_got, row(ln1_gain), d_middle)
    send_got = exchange(send, 1)
    sides_got = swap_tensor(sides)
    *input_rows, send_got, sides_got = together(*input_rows, send_got, sides_got)

    flat = jnp.concatenate(
        [proj_bias[0], (sides + sides_got).reshape(-1), grad_up_bias[0], grad_down_bias[0]]
    )
    vectors = jnp.pad(flat, (0, 8 * columns - flat.shape[0])).reshape(8, columns)
    packet, packet_far = merge(own, far, send_got, vectors, exchange(vectors, 1))
    packet_got = exchange(packet_far, 2)
    in_near = [route(input_rows[step], step, False) for step in range(2)]
    out_far = [swap_tensor(v) for v in out_near]
    sum_1 = sum_1 + got_1
    sum_2 = sum_2 + got_2
    packet_got, sum_1, sum_2, *pieces = together(packet_got, sum_1, sum_2, *in_near, *out_far)

    in_near, out_far = pieces[:2], pieces[2:]
    packet = add_packets(packet, packet_got, shard)
    padded = jnp.concatenate([sum_1, packet[shard:]], axis=0)
    got_3 = edges(jnp.where(inner, padded, packet))
    got_2 = across(sum_2)
    in_far = [swap_tensor(v) for v in in_near]
    got_2, got_3, *in_far = together(got_2, got_3, *in_far)

    sum_2 = sum_2 + got_2
    sum_1 = jnp.where(inner, sum_1, got_3[:shard])
    packet = add_packets(packet, got_3, shard)
    packet_got = across(packet)
    got_2 = outward(sum_2)
    input_grad = join_out(in_near, in_far, odd, upper)
    grad_down = sum_1.astype(jnp.float32).T
    packet_got, got_2 = together(packet_got, got_2)

    packet = add_packets(packet, packet_got, shard)
    packet_got = outward(packet)
    grad_up = jnp.where(inner, sum_2, got_2).astype(jnp.float32)
    output = join_out(out_near, out_far, odd, upper)
    packet = jnp.where(inner, packet, packet_got).astype(jnp.float32)

    count = vectors.shape[0]
    flat = (packet[shard : shard + count] + packet[shard + count :]).reshape(-1)
    wide = 3 * local_width
    ends = [wide + k * width for k in range(6)] + [wide + 5 * width + columns]
    part = lambda k, size: flat[ends[k] : ends[k] + size]
    grads = packet[:shard]
    return (
        output.reshape(tokens.shape),
        input_grad.reshape(tokens.shape),
        part(0, width),
        part(1, width),
        grads[:, :local_width],
        flat[:local_width],
        grads[:, local_width : 2 * local_width],
        grads[:, 2 * local_width : wide],
        flat[2 * local_width : wide],
        grads[:, wide:].T,
        part(4, width),
        part(2, width),
        part(3, width),
        grad_up,
        part(5, columns),
        grad_down,
        part(6, width),
    )


def pick(mesh):
    sizes = mesh.shape
    planes = sizes["dp"] == 4 and sizes["context"] == 4 and sizes["tensor"] == 2
    return per_device_planes if planes else per_device_general


def solution(mesh):
    return jax.shard_map(
        pick(mesh),
        mesh=mesh,
        in_specs=(
            P("dp", "context", None),
            P("dp"),
            P(),
            P(),
            P("dp", "tensor"),
            P("tensor"),
            P("dp", "tensor"),
            P("dp", "tensor"),
            P("tensor"),
            P("tensor", "dp"),
            P(),
            P(),
            P(),
            P("dp", "tensor"),
            P("tensor"),
            P("tensor", "dp"),
            P(),
            P("dp", "context", None),
        ),
        out_specs=(
            P("dp", "context", None),
            P("dp", "context", None),
            P(),
            P(),
            P("dp", "tensor"),
            P("tensor"),
            P("dp", "tensor"),
            P("dp", "tensor"),
            P("tensor"),
            P("tensor", "dp"),
            P(),
            P(),
            P(),
            P("dp", "tensor"),
            P("tensor"),
            P("tensor", "dp"),
            P(),
        ),
        check_vma=False,
    )
```

```python
import functools

import jax
import jax.numpy as jnp
from jax import lax
from jax.experimental import pallas as pl
from jax.experimental.pallas import tpu as pltpu
from jax.sharding import PartitionSpec as P

HEAD_DIM = 64


epsilon = 1e-06
masked_value = -1e30


def norm_rows(values, gain_vec, bias_vec):
    average = jnp.mean(values, axis=-1, keepdims=True)
    centred = values - average
    spread = jnp.mean(centred * centred, axis=-1, keepdims=True)
    return centred * lax.rsqrt(spread + epsilon) * gain_vec + bias_vec


def gelu_tanh(values):
    return jax.nn.gelu(values, approximate=True)


def dense(left, right):
    return jnp.dot(left, right, preferred_element_type=jnp.float32)


def dense_tn(left, right):
    return lax.dot_general(
        left, right, (((0,), (0,)), ((), ())), preferred_element_type=jnp.float32
    )


def dense_nt(left, right):
    return lax.dot_general(
        left, right, (((1,), (1,)), ((), ())), preferred_element_type=jnp.float32
    )


def per_device_general(
    tokens,
    lengths,
    ln1_gain,
    ln1_bias,
    w_query,
    b_query,
    w_key,
    w_value,
    b_value,
    w_out,
    b_out,
    ln2_gain,
    ln2_bias,
    w_up,
    b_up,
    w_down,
    b_down,
    cotangent,
):
    seq_count, shard_rows, width = tokens.shape
    full_len = shard_rows * lax.axis_size("context")
    local_width = w_query.shape[1]
    local_heads = local_width // HEAD_DIM
    scale = HEAD_DIM ** (-0.5)
    row_count = seq_count * shard_rows
    query_weight, key_weight, value_weight, up_weight, out_weight, down_weight = (
        lax.all_gather(w_query, "dp", axis=0, tiled=True),
        lax.all_gather(w_key, "dp", axis=0, tiled=True),
        lax.all_gather(w_value, "dp", axis=0, tiled=True),
        lax.all_gather(w_up, "dp", axis=0, tiled=True),
        lax.all_gather(w_out, "dp", axis=1, tiled=True),
        lax.all_gather(w_down, "dp", axis=1, tiled=True),
    )
    gain_one = ln1_gain.astype(jnp.float32)
    bias_one = ln1_bias.astype(jnp.float32)
    query_bias = b_query.astype(jnp.float32)
    value_bias = b_value.astype(jnp.float32)
    out_bias = b_out.astype(jnp.float32)
    gain_two = ln2_gain.astype(jnp.float32)
    bias_two = ln2_bias.astype(jnp.float32)
    up_bias = b_up.astype(jnp.float32)
    down_bias = b_down.astype(jnp.float32)
    places = lax.axis_index("context") * shard_rows + jnp.arange(shard_rows, dtype=jnp.int32)
    keep = (places[None, :] < lengths[:, None]).astype(jnp.float32).reshape(row_count, 1)
    key_places = jnp.arange(full_len, dtype=jnp.int32)
    rows_in = tokens.reshape(row_count, width).astype(jnp.float32)
    normed_one, pull_one = jax.vjp(norm_rows, rows_in, gain_one, bias_one)
    normed_low = normed_one.astype(jnp.bfloat16)
    queries = (dense(normed_low, query_weight) + query_bias).astype(jnp.bfloat16)
    keys_own = dense(normed_low, key_weight).astype(jnp.bfloat16)
    values_own = (dense(normed_low, value_weight) + value_bias).astype(jnp.bfloat16)
    keys_whole, values_whole = (
        lax.all_gather(
            keys_own.reshape(seq_count, shard_rows, local_width), "context", axis=1, tiled=True
        ),
        lax.all_gather(
            values_own.reshape(seq_count, shard_rows, local_width), "context", axis=1, tiled=True
        ),
    )
    query_heads = queries.reshape(seq_count, shard_rows, local_heads, HEAD_DIM)
    head_outs = []
    log_sums = []
    for member in range(seq_count):
        key_heads = keys_whole[member].reshape(full_len, local_heads, HEAD_DIM)
        value_heads = values_whole[member].reshape(full_len, local_heads, HEAD_DIM)
        raw_scores = (
            jnp.einsum(
                "qhd,khd->hqk", query_heads[member], key_heads, preferred_element_type=jnp.float32
            )
            * scale
        )
        live = (key_places < lengths[member])[None, None, :]
        masked = jnp.where(live, raw_scores, masked_value)
        largest = jnp.max(masked, axis=-1, keepdims=True)
        log_total = largest + jnp.log(jnp.sum(jnp.exp(masked - largest), axis=-1, keepdims=True))
        probs_low = jnp.exp(masked - log_total).astype(jnp.bfloat16)
        mixed_heads = jnp.einsum(
            "hqk,khd->qhd", probs_low, value_heads, preferred_element_type=jnp.float32
        )
        head_outs.append(mixed_heads.reshape(shard_rows, local_width))
        log_sums.append(log_total)
    context_low = jnp.concatenate(head_outs, axis=0).astype(jnp.bfloat16)
    attention = (
        lax.psum(dense(context_low, out_weight).astype(jnp.bfloat16), "tensor").astype(jnp.float32)
        + out_bias
    )
    middle = rows_in + keep * attention
    normed_two, pull_two = jax.vjp(norm_rows, middle, gain_two, bias_two)
    normed_two_low = normed_two.astype(jnp.bfloat16)
    hidden_pre = dense(normed_two_low, up_weight) + up_bias
    hidden, pull_gelu = jax.vjp(gelu_tanh, hidden_pre)
    hidden_low = hidden.astype(jnp.bfloat16)
    feed = (
        lax.psum(dense(hidden_low, down_weight).astype(jnp.bfloat16), "tensor").astype(jnp.float32)
        + down_bias
    )
    output = (middle + keep * feed).astype(jnp.bfloat16).reshape(tokens.shape)
    grad_top = cotangent.reshape(row_count, width).astype(jnp.float32)
    d_feed = (keep * grad_top).astype(jnp.bfloat16)
    grad_down_bias = jnp.sum(d_feed.astype(jnp.float32), axis=0)
    grad_down = dense_tn(hidden_low, d_feed)
    d_hidden = dense_nt(d_feed, down_weight)
    d_pre = pull_gelu(d_hidden)[0].astype(jnp.bfloat16)
    grad_up_bias = jnp.sum(d_pre.astype(jnp.float32), axis=0)
    grad_up = dense_tn(normed_two_low, d_pre)
    d_normed_two = lax.psum(dense_nt(d_pre, up_weight).astype(jnp.bfloat16), "tensor").astype(
        jnp.float32
    )
    d_middle, grad_gain_two, grad_bias_two = pull_two(d_normed_two)
    d_middle = d_middle + grad_top
    d_attention = (keep * d_middle).astype(jnp.bfloat16)
    grad_out_bias = jnp.sum(d_attention.astype(jnp.float32), axis=0)
    grad_out = dense_tn(context_low, d_attention)
    d_context = dense_nt(d_attention, out_weight).astype(jnp.bfloat16)
    back_keys, back_values = (keys_whole, values_whole)
    d_context_heads = d_context.reshape(seq_count, shard_rows, local_heads, HEAD_DIM)
    query_grads = []
    own_grads = []
    inner_rows = []
    for member in range(seq_count):
        key_heads = back_keys[member].reshape(full_len, local_heads, HEAD_DIM)
        value_heads = back_values[member].reshape(full_len, local_heads, HEAD_DIM)
        raw_scores = (
            jnp.einsum(
                "qhd,khd->hqk", query_heads[member], key_heads, preferred_element_type=jnp.float32
            )
            * scale
        )
        live = (key_places < lengths[member])[None, None, :]
        probs = jnp.where(live, jnp.exp(raw_scores - log_sums[member]), 0.0)
        d_probs = jnp.einsum(
            "qhd,khd->hqk", d_context_heads[member], value_heads, preferred_element_type=jnp.float32
        )
        inner = jnp.sum(probs * d_probs, axis=-1, keepdims=True)
        d_scores = (probs * (d_probs - inner)).astype(jnp.bfloat16)
        d_query = (
            jnp.einsum("hqk,khd->qhd", d_scores, key_heads, preferred_element_type=jnp.float32)
            * scale
        )
        query_grads.append(d_query.reshape(shard_rows, local_width))
        inner_rows.append(inner[:, :, 0])
        d_keys = (
            jnp.einsum(
                "hqk,qhd->khd", d_scores, query_heads[member], preferred_element_type=jnp.float32
            )
            * scale
        )
        d_values = jnp.einsum(
            "hqk,qhd->khd",
            probs.astype(jnp.bfloat16),
            d_context_heads[member],
            preferred_element_type=jnp.float32,
        )
        key_term = jnp.concatenate(
            [d_keys.reshape(full_len, local_width), d_values.reshape(full_len, local_width)], axis=1
        )
        own_grads.append(
            lax.psum_scatter(
                key_term.astype(jnp.bfloat16), "context", scatter_dimension=0, tiled=True
            ).astype(jnp.float32)
        )
    d_query_low = jnp.concatenate(query_grads, axis=0).astype(jnp.bfloat16)
    key_value_grads = jnp.concatenate(own_grads, axis=0)
    d_keys_low = key_value_grads[:, :local_width].astype(jnp.bfloat16)
    d_values_low = key_value_grads[:, local_width:].astype(jnp.bfloat16)
    grad_query = dense_tn(normed_low, d_query_low)
    grad_query_bias = jnp.sum(d_query_low.astype(jnp.float32), axis=0)
    grad_key = dense_tn(normed_low, d_keys_low)
    grad_value = dense_tn(normed_low, d_values_low)
    grad_value_bias = jnp.sum(d_values_low.astype(jnp.float32), axis=0)
    d_normed_one = lax.psum(
        (
            dense_nt(d_query_low, query_weight)
            + dense_nt(d_keys_low, key_weight)
            + dense_nt(d_values_low, value_weight)
        ).astype(jnp.bfloat16),
        "tensor",
    ).astype(jnp.float32)
    d_rows, grad_gain_one, grad_bias_one = pull_one(d_normed_one)
    input_grad = (d_rows + d_middle).astype(jnp.bfloat16).reshape(tokens.shape)
    data_sums = (
        lax.psum_scatter(
            grad_query.astype(jnp.bfloat16), "dp", scatter_dimension=0, tiled=True
        ).astype(jnp.float32),
        lax.psum_scatter(
            grad_key.astype(jnp.bfloat16), "dp", scatter_dimension=0, tiled=True
        ).astype(jnp.float32),
        lax.psum_scatter(
            grad_value.astype(jnp.bfloat16), "dp", scatter_dimension=0, tiled=True
        ).astype(jnp.float32),
        lax.psum_scatter(
            grad_up.astype(jnp.bfloat16), "dp", scatter_dimension=0, tiled=True
        ).astype(jnp.float32),
        lax.psum_scatter(
            grad_out.astype(jnp.bfloat16), "dp", scatter_dimension=1, tiled=True
        ).astype(jnp.float32),
        lax.psum_scatter(
            grad_down.astype(jnp.bfloat16), "dp", scatter_dimension=1, tiled=True
        ).astype(jnp.float32),
    )
    owned_sums = (
        lax.psum(data_sums[0].astype(jnp.bfloat16), "context").astype(jnp.float32),
        lax.psum(data_sums[1].astype(jnp.bfloat16), "context").astype(jnp.float32),
        lax.psum(data_sums[2].astype(jnp.bfloat16), "context").astype(jnp.float32),
        lax.psum(data_sums[3].astype(jnp.bfloat16), "context").astype(jnp.float32),
        lax.psum(data_sums[4].astype(jnp.bfloat16), "context").astype(jnp.float32),
        lax.psum(data_sums[5].astype(jnp.bfloat16), "context").astype(jnp.float32),
    )
    small_sums = lax.psum(
        (
            grad_gain_one,
            grad_bias_one,
            grad_query_bias,
            grad_value_bias,
            grad_out_bias,
            grad_gain_two,
            grad_bias_two,
            grad_up_bias,
            grad_down_bias,
        ),
        ("dp", "context"),
    )
    return (
        output,
        input_grad,
        small_sums[0],
        small_sums[1],
        owned_sums[0],
        small_sums[2],
        owned_sums[1],
        owned_sums[2],
        small_sums[3],
        owned_sums[4],
        small_sums[4],
        small_sums[5],
        small_sums[6],
        owned_sums[3],
        small_sums[7],
        owned_sums[5],
        small_sums[8],
    )


def live_bias(info, count):
    places = lax.broadcasted_iota(jnp.int32, (count, 2 * HEAD_DIM), 0)
    return jnp.concatenate(
        [jnp.where(info[k] + places < info[8], 0.0, masked_value) for k in range(8)], axis=0
    ).astype(jnp.bfloat16)


def split_pair(array, extra):
    lane = lax.broadcasted_iota(jnp.int32, array.shape, 1)
    zero = jnp.zeros((), jnp.bfloat16)
    left = jnp.where(lane < HEAD_DIM, array, jnp.where(lane == HEAD_DIM, extra, zero))
    right = jnp.where(lane >= HEAD_DIM, array, jnp.where(lane == 0, extra, zero))
    return left, right


LOG_SCALE = HEAD_DIM ** (-0.5) * 1.4426950408889634


def attend_kernel(info, query_ref, own_ref, other_ref, out_ref, log_ref):
    pair = 2 * HEAD_DIM
    count = query_ref.shape[0] // 4
    keys = jnp.concatenate([own_ref[:, :pair], other_ref[:, :pair]], axis=0)
    values = jnp.concatenate([own_ref[:, pair:], other_ref[:, pair:]], axis=0)
    values_t = values.T
    key_heads = split_pair(keys, live_bias(info, count))
    query_heads = split_pair(query_ref[...], jnp.ones((), jnp.bfloat16))
    mixed = []
    for head in range(2):
        scores = dense_nt(key_heads[head], query_heads[head])
        largest = jnp.max(scores, axis=0, keepdims=True)
        weights = jnp.exp2((scores - largest) * LOG_SCALE)
        total = jnp.sum(weights, axis=0, keepdims=True)
        dims = slice(head * HEAD_DIM, (head + 1) * HEAD_DIM)
        mixed.append(dense(values_t[dims], weights.astype(jnp.bfloat16)) / total)
        log_ref[0, head : head + 1, :] = largest * LOG_SCALE + jnp.log2(total)
    out_ref[...] = jnp.concatenate(mixed, axis=0).T.astype(jnp.bfloat16)


def attend(info, queries, pair_own, pair_other):
    rows, width = queries.shape
    pair = 2 * HEAD_DIM
    groups = width // pair
    work = 4 * rows * 2 * rows * width
    return pl.pallas_call(
        attend_kernel,
        out_shape=(
            jax.ShapeDtypeStruct((rows, width), jnp.bfloat16),
            jax.ShapeDtypeStruct((groups, 2, rows), jnp.float32),
        ),
        grid_spec=pltpu.PrefetchScalarGridSpec(
            num_scalar_prefetch=1,
            grid=(groups,),
            in_specs=[
                pl.BlockSpec((rows, pair), lambda g, info: (0, g)),
                pl.BlockSpec((rows, 2 * pair), lambda g, info: (0, g)),
                pl.BlockSpec((rows, 2 * pair), lambda g, info: (0, g)),
            ],
            out_specs=(
                pl.BlockSpec((rows, pair), lambda g, info: (0, g)),
                pl.BlockSpec((1, 2, rows), lambda g, info: (g, 0, 0)),
            ),
        ),
        compiler_params=pltpu.CompilerParams(vmem_limit_bytes=48 << 20),
        cost_estimate=pl.CostEstimate(
            flops=4 * work, bytes_accessed=12 * rows * width, transcendentals=work // (2 * HEAD_DIM)
        ),
    )(info, queries, pair_own, pair_other)


def attend_back_kernel(
    info,
    query_ref,
    own_ref,
    other_ref,
    out_ref,
    d_own_ref,
    d_peer_ref,
    proj_ref,
    log_ref,
    d_query_ref,
    d_pair_ref,
    d_other_ref,
):
    pair = 2 * HEAD_DIM
    rows = query_ref.shape[0]
    scale = HEAD_DIM ** (-0.5)
    keys = jnp.concatenate([own_ref[:, :pair], other_ref[:, :pair]], axis=0)
    values = jnp.concatenate([own_ref[:, pair:], other_ref[:, pair:]], axis=0)
    keys_t = keys.T
    key_heads = split_pair(keys, live_bias(info, rows // 4))
    value_heads = split_pair(values, jnp.zeros((), jnp.bfloat16))
    query = query_ref[...]
    query_heads = split_pair(query, jnp.ones((), jnp.bfloat16))
    d_att = jnp.concatenate([d_own_ref[...], d_peer_ref[...]], axis=0)
    grad = dense(d_att, proj_ref[...]).astype(jnp.bfloat16)
    inner_t = (grad.astype(jnp.float32) * out_ref[...].astype(jnp.float32)).T
    d_query, d_keys, d_values = [], [], []
    for head in range(2):
        dims = slice(head * HEAD_DIM, (head + 1) * HEAD_DIM)
        inner = jnp.sum(inner_t[dims], axis=0, keepdims=True)
        scores = dense_nt(key_heads[head], query_heads[head])
        probs = jnp.exp2(scores * LOG_SCALE - log_ref[0, head : head + 1, :])
        d_probs = dense_nt(value_heads[head], grad)
        d_scores = (probs * (d_probs - inner)).astype(jnp.bfloat16)
        d_query.append(dense(keys_t[dims], d_scores))
        d_keys.append(dense(d_scores, query))
        d_values.append(dense(probs.astype(jnp.bfloat16), grad))
    d_query_ref[...] = (jnp.concatenate(d_query, axis=0).T * scale).astype(jnp.bfloat16)
    left = lax.broadcasted_iota(jnp.int32, d_keys[0].shape, 1) < HEAD_DIM
    d_key = (jnp.where(left, d_keys[0], d_keys[1]) * scale).astype(jnp.bfloat16)
    d_value = jnp.where(left, d_values[0], d_values[1]).astype(jnp.bfloat16)
    d_pair_ref[:, :pair] = d_key[:rows]
    d_pair_ref[:, pair:] = d_value[:rows]
    d_other_ref[:, :pair] = d_key[rows:]
    d_other_ref[:, pair:] = d_value[rows:]


def attend_back(info, queries, pair_own, pair_other, mixed, d_own, d_peer, out_t, logs):
    rows, local = queries.shape
    width = out_t.shape[0]
    pair = 2 * HEAD_DIM
    work = 4 * rows * 2 * rows * local
    narrow = pl.BlockSpec((rows, pair), lambda g, info: (0, g))
    wide = pl.BlockSpec((rows, 2 * pair), lambda g, info: (0, g))
    halves = pl.BlockSpec((rows // 2, width), lambda g, info: (0, 0))
    return pl.pallas_call(
        attend_back_kernel,
        out_shape=tuple(
            jax.ShapeDtypeStruct((rows, columns), jnp.bfloat16)
            for columns in (local, 2 * local, 2 * local)
        ),
        grid_spec=pltpu.PrefetchScalarGridSpec(
            num_scalar_prefetch=1,
            grid=(local // pair,),
            in_specs=[
                narrow,
                wide,
                wide,
                narrow,
                halves,
                halves,
                pl.BlockSpec((width, pair), lambda g, info: (0, g)),
                pl.BlockSpec((1, 2, rows), lambda g, info: (g, 0, 0)),
            ],
            out_specs=(narrow, wide, wide),
        ),
        compiler_params=pltpu.CompilerParams(vmem_limit_bytes=48 << 20),
        cost_estimate=pl.CostEstimate(
            flops=10 * work, bytes_accessed=24 * rows * local, transcendentals=work // (2 * HEAD_DIM)
        ),
    )(info, queries, pair_own, pair_other, mixed, d_own, d_peer, out_t, logs)


def held(info, quarters, count, width):
    places = lax.broadcasted_iota(jnp.int32, (count, width), 0)
    return jnp.concatenate([info[k] + places < info[8] for k in range(quarters)], axis=0)


def fixed(array):
    return pl.BlockSpec(array.shape, lambda i: (0,) * len(array.shape))


def call_once(kernel, args, shapes, flops, scratch=()):
    moved = sum(a.size * a.dtype.itemsize for a in (*args, *shapes))
    return pl.pallas_call(
        kernel,
        out_shape=tuple(shapes),
        grid=(1,),
        in_specs=[fixed(a) for a in args],
        out_specs=tuple(fixed(s) for s in shapes),
        scratch_shapes=list(scratch),
        compiler_params=pltpu.CompilerParams(vmem_limit_bytes=48 << 20),
        cost_estimate=pl.CostEstimate(flops=flops, bytes_accessed=moved, transcendentals=0),
    )(*args)


def low(*shape):
    return jax.ShapeDtypeStruct(shape, jnp.bfloat16)


def full(*shape):
    return jax.ShapeDtypeStruct(shape, jnp.float32)


def row_stats(values):
    centred = values - jnp.mean(values, axis=-1, keepdims=True)
    spread = jnp.mean(centred * centred, axis=-1, keepdims=True)
    root = lax.rsqrt(spread + epsilon)
    return centred * root, root


def row_pull(normed, root, grad):
    return root * (
        grad
        - jnp.mean(grad, axis=-1, keepdims=True)
        - normed * jnp.mean(grad * normed, axis=-1, keepdims=True)
    )


def settle(parts, out_ref):
    rows = parts[0].shape[0]
    mine = lax.axis_index("dp")
    for step, part in enumerate(parts):
        start = pl.multiple_of((mine ^ step) * rows, rows)
        out_ref[pl.ds(start, rows), :] = part[...]


def enter_kernel(
    own0, own1, peer0, peer1, gain_ref, bias_ref, q_bias_ref, v_bias_ref, a, b, c, d,
    rows_ref, normed_ref, query_ref, pair_ref, proj_ref,
):
    pair = 2 * HEAD_DIM
    settle((a, b, c, d), proj_ref)
    rows = jnp.concatenate([own0[...], own1[...], peer0[...], peer1[...]], axis=0)
    rows_ref[...] = rows
    normed, _ = row_stats(rows.astype(jnp.float32))
    normed = normed * gain_ref[...].astype(jnp.float32) + bias_ref[...].astype(jnp.float32)
    normed = normed.astype(jnp.bfloat16)
    normed_ref[...] = normed
    local = query_ref.shape[1]
    mixed = dense(normed, proj_ref[...])
    query_ref[...] = (mixed[:, :local] + q_bias_ref[...].astype(jnp.float32)).astype(jnp.bfloat16)
    for g in range(local // pair):
        cols = slice(g * pair, (g + 1) * pair)
        key = mixed[:, local + g * pair : local + (g + 1) * pair]
        value = mixed[:, 2 * local + g * pair : 2 * local + (g + 1) * pair]
        value = value + v_bias_ref[:, cols].astype(jnp.float32)
        pair_ref[:, 2 * g * pair : (2 * g + 1) * pair] = key.astype(jnp.bfloat16)
        pair_ref[:, (2 * g + 1) * pair : (2 * g + 2) * pair] = value.astype(jnp.bfloat16)


def enter(pieces, gain, bias, q_bias, v_bias, blocks):
    half, width = pieces[0].shape
    rows = 4 * half
    local = q_bias.shape[1]
    shapes = (
        low(rows, width),
        low(rows, width),
        low(rows, local),
        low(rows, 2 * local),
        low(width, 3 * local),
    )
    args = (*pieces, gain, bias, q_bias, v_bias, *blocks)
    return call_once(enter_kernel, args, shapes, 6 * rows * width * local)


ROOT_TWO_OVER_PI = 0.7978845608028654
CUBE = 0.044715


def fetch(parts, columns, out_ref, sems):
    rows = parts[0].shape[0]
    mine = lax.axis_index("dp")
    copies = []
    for step, part in enumerate(parts):
        start = pl.multiple_of((mine ^ step) * rows, rows)
        copy = pltpu.make_async_copy(
            part.at[:, columns], out_ref.at[pl.ds(start, rows)], sems.at[step]
        )
        copy.start()
        copies.append(copy)
    return copies


def middle_kernel(
    info, rows_ref, own_ref, peer_ref, top0, top1, top2, top3, gain_ref, bias_ref, out_bias_ref,
    up_bias_ref, down_bias_ref, pa, pb, pc, pd, da, db, dc, dd,
    mid_ref, normed_ref, feed_ref, hidden_ref, d_pre_ref, d_own_ref, d_peer_ref,
    part0_ref, part1_ref, out_ref, g_up_ref, g_down_ref,
    outs, ups, downs, whole_mid, sems,
):
    rows, width = rows_ref.shape
    half = rows // 2
    local = own_ref.shape[1]
    hidden_width = up_bias_ref.shape[1]
    steps = ups.shape[0]
    tile = hidden_width // steps
    packs, lasts = (pa, pb, pc, pd), (da, db, dc, dd)
    waits = [fetch(packs, pl.ds(hidden_width, width), outs, sems.at[0])]
    for s in range(steps):
        columns = pl.ds(s * tile, tile)
        waits.append(fetch(packs, columns, ups.at[s], sems.at[1 + 2 * s]))
        waits.append(fetch(lasts, columns, downs.at[s], sems.at[2 + 2 * s]))

    real = held(info, 4, rows // 4, width)
    top = jnp.concatenate([top0[...], top1[...], top2[...], top3[...]], axis=0)
    feed = jnp.where(real, top.astype(jnp.float32), 0.0)
    feed_ref[...] = feed.astype(jnp.bfloat16)
    g_down_ref[...] = jnp.sum(feed, axis=0, keepdims=True)
    peer = jnp.concatenate([peer_ref[half:, :], peer_ref[:half, :]], axis=0)
    for copy in waits[0]:
        copy.wait()
    out_ref[...] = outs[:, :local]
    attention = (
        dense_nt(own_ref[...], outs[:, :local])
        + dense_nt(peer, outs[:, local:])
        + out_bias_ref[...].astype(jnp.float32)
    )
    mid = rows_ref[...].astype(jnp.float32) + jnp.where(real, attention, 0.0)
    mid_ref[...] = mid[:half]
    whole_mid[...] = mid
    normed, _ = row_stats(mid)
    normed = normed * gain_ref[...].astype(jnp.float32) + bias_ref[...].astype(jnp.float32)
    normed_ref[...] = normed.astype(jnp.bfloat16)

    for s in range(steps):
        columns = slice(s * tile, (s + 1) * tile)
        for copy in waits[1 + 2 * s] + waits[2 + 2 * s]:
            copy.wait()
        pre = dense(normed_ref[...], ups[s]) + up_bias_ref[:, columns].astype(jnp.float32)
        d_hidden = dense(feed_ref[...], downs[s])
        square = pre * pre
        bend = jnp.tanh(pre * (ROOT_TWO_OVER_PI + CUBE * ROOT_TWO_OVER_PI * square))
        half_up = 0.5 + 0.5 * bend
        active = pre * half_up
        slope = half_up + active * (1.0 - bend) * (
            ROOT_TWO_OVER_PI + 3.0 * CUBE * ROOT_TWO_OVER_PI * square
        )
        hidden_ref[:, columns] = active.astype(jnp.bfloat16)
        d_pre = (d_hidden * slope).astype(jnp.bfloat16)
        d_pre_ref[:, columns] = d_pre
        g_up_ref[:, columns] = jnp.sum(d_pre.astype(jnp.float32), axis=0, keepdims=True)

    def back(left_ref, right_ref):
        total = 0.0
        for s in range(steps):
            total += dense_nt(left_ref[:, s * tile : (s + 1) * tile], right_ref[s])
        return total

    grad = back(d_pre_ref, ups).astype(jnp.bfloat16)
    d_own_ref[...] = grad[:half]
    d_peer_ref[...] = grad[half:]
    first = lax.axis_index("tensor") == 0
    share = back(hidden_ref, downs)
    share += jnp.where(first, down_bias_ref[...].astype(jnp.float32), 0.0)
    share = jnp.where(real, share, 0.0) + jnp.where(first, whole_mid[...], 0.0)
    share = share.astype(jnp.bfloat16)
    for k, part in enumerate((part0_ref, part1_ref)):
        start = k * (half // 2)
        part[0] = share[start : start + half // 2]
        part[1] = share[half + start : half + start + half // 2]


def middle_part(
    info, rows_low, own, peer, top, gain, bias, out_bias, packs, downs, up_bias, down_bias
):
    rows, width = rows_low.shape
    local = own.shape[1]
    hidden = up_bias.shape[1]
    steps = 2
    small = (rows_low, own, peer, *top, gain, bias, out_bias, up_bias, down_bias)
    inside = pl.BlockSpec(memory_space=pltpu.VMEM)
    shapes = (
        full(rows // 2, width),
        low(rows, width),
        low(rows, width),
        low(rows, hidden),
        low(rows, hidden),
        low(rows // 2, width),
        low(rows // 2, width),
        low(2, rows // 4, width),
        low(2, rows // 4, width),
        low(width, local),
        full(1, hidden),
        full(1, width),
    )
    return pl.pallas_call(
        middle_kernel,
        out_shape=shapes,
        in_specs=[pl.BlockSpec(memory_space=pltpu.SMEM)]
        + [inside] * len(small)
        + [pl.BlockSpec(memory_space=pltpu.HBM)] * 8,
        out_specs=(inside,) * len(shapes),
        scratch_shapes=[
            pltpu.VMEM((width, width), jnp.bfloat16),
            pltpu.VMEM((steps, width, hidden // steps), jnp.bfloat16),
            pltpu.VMEM((steps, width, hidden // steps), jnp.bfloat16),
            pltpu.VMEM((rows, width), jnp.float32),
            pltpu.SemaphoreType.DMA((1 + 2 * steps, 4)),
        ],
        compiler_params=pltpu.CompilerParams(vmem_limit_bytes=36 << 20),
        cost_estimate=pl.CostEstimate(
            flops=8 * rows * width * hidden, bytes_accessed=20 << 20, transcendentals=rows * hidden
        ),
    )(info, *small, *packs, *downs)


def turn_kernel(
    info, mid_ref, d_own_ref, got_ref, top0, top1, gain_ref, d_mid_ref, d_att_ref, sums_ref
):
    half, width = d_own_ref.shape
    grad = d_own_ref[...].astype(jnp.float32) + got_ref[...].astype(jnp.float32)
    normed, root = row_stats(mid_ref[...])
    top = jnp.concatenate([top0[...], top1[...]], axis=0).astype(jnp.float32)
    d_mid = top + row_pull(normed, root, grad * gain_ref[...].astype(jnp.float32))
    d_mid_ref[...] = d_mid
    d_att = jnp.where(held(info, 2, half // 2, width), d_mid, 0.0).astype(jnp.bfloat16)
    d_att_ref[...] = d_att
    sums_ref[0:1, :] = jnp.sum(grad * normed, axis=0, keepdims=True)
    sums_ref[1:2, :] = jnp.sum(grad, axis=0, keepdims=True)
    sums_ref[2:3, :] = jnp.sum(d_att.astype(jnp.float32), axis=0, keepdims=True)


def turn(info, mid, d_own, got, top, gain):
    half, width = d_own.shape
    fixed = lambda a: pl.BlockSpec(a.shape, lambda i, info: (0,) * len(a.shape))
    first = pl.BlockSpec((half, width), lambda i, info: (0, 0))
    shapes = (
        jax.ShapeDtypeStruct((half, width), jnp.float32),
        jax.ShapeDtypeStruct((half, width), jnp.bfloat16),
        jax.ShapeDtypeStruct((3, width), jnp.float32),
    )
    return pl.pallas_call(
        turn_kernel,
        out_shape=shapes,
        grid_spec=pltpu.PrefetchScalarGridSpec(
            num_scalar_prefetch=1,
            grid=(1,),
            in_specs=[first, fixed(d_own), fixed(got), fixed(top[0]), fixed(top[1]), fixed(gain)],
            out_specs=tuple(fixed(s) for s in shapes),
        ),
        compiler_params=pltpu.CompilerParams(vmem_limit_bytes=32 << 20),
        cost_estimate=pl.CostEstimate(
            flops=40 * half * width, bytes_accessed=4 << 20, transcendentals=half
        ),
    )(info, mid, d_own, got, *top, gain)


def leave_kernel(
    rows_ref, proj_ref, d_query_ref, d_pair_ref, got_ref, sums_two_ref,
    d_proj_ref, own_ref, peer_ref, sums_ref, bias_ref,
):
    pair = 2 * HEAD_DIM
    rows, local = d_query_ref.shape
    half = rows // 2
    d_proj_ref[:, :local] = d_query_ref[...]
    total = (d_pair_ref[...].astype(jnp.float32) + got_ref[...].astype(jnp.float32)).astype(
        jnp.bfloat16
    )
    for g in range(local // pair):
        for k in range(2):
            start = (k + 1) * local + g * pair
            d_proj_ref[:, start : start + pair] = total[:, (2 * g + k) * pair : (2 * g + k + 1) * pair]
    d_proj = d_proj_ref[...]
    bias_ref[...] = jnp.sum(d_proj.astype(jnp.float32), axis=0, keepdims=True)
    grad = dense_nt(d_proj, proj_ref[...])
    low = grad.astype(jnp.bfloat16)
    own_ref[...] = low[:half]
    peer_ref[...] = low[half:]
    normed, _ = row_stats(rows_ref[...].astype(jnp.float32))
    sums_ref[0:1, :] = jnp.sum(grad * normed, axis=0, keepdims=True)
    sums_ref[1:2, :] = jnp.sum(grad, axis=0, keepdims=True)
    sums_ref[2:5, :] = sums_two_ref[...]


def leave(rows_low, proj, d_query, d_pair, got, sums_two):
    rows, width = rows_low.shape
    columns = proj.shape[1]
    shapes = (
        low(rows, columns),
        low(rows // 2, width),
        low(rows // 2, width),
        full(5, width),
        full(1, columns),
    )
    args = (rows_low, proj, d_query, d_pair, got, sums_two)
    return call_once(leave_kernel, args, shapes, 2 * rows * width * columns)


def finish_kernel(rows_ref, own_ref, got_ref, gain_ref, d_mid_ref, first_ref, second_ref):
    half = rows_ref.shape[0]
    normed, root = row_stats(rows_ref[...].astype(jnp.float32))
    grad = own_ref[...].astype(jnp.float32) + got_ref[...].astype(jnp.float32)
    d_rows = row_pull(normed, root, grad * gain_ref[...].astype(jnp.float32)) + d_mid_ref[...]
    low = d_rows.astype(jnp.bfloat16)
    first_ref[...] = low[: half // 2]
    second_ref[...] = low[half // 2 :]


def finish(rows_low, own, got, gain, d_mid):
    half, width = own.shape
    top_half = pl.BlockSpec((half, width), lambda i: (0, 0))
    fixed = lambda a: pl.BlockSpec(a.shape, lambda i: (0,) * a.ndim)
    piece = jax.ShapeDtypeStruct((half // 2, width), jnp.bfloat16)
    return pl.pallas_call(
        finish_kernel,
        out_shape=(piece, piece),
        grid=(1,),
        in_specs=[top_half, fixed(own), fixed(got), fixed(gain), fixed(d_mid)],
        out_specs=(fixed(piece), fixed(piece)),
        compiler_params=pltpu.CompilerParams(vmem_limit_bytes=32 << 20),
        cost_estimate=pl.CostEstimate(
            flops=20 * half * width, bytes_accessed=4 << 20, transcendentals=half
        ),
    )(rows_low, own, got, gain, d_mid)


def weight_grad_kernel(*refs, counts):
    lefts, used = [], 0
    for count in counts:
        lefts.append((refs[used : used + count], refs[used + count]))
        used += count + 1
    own_ref, far_ref, send_ref = refs[used : used + 3]
    rows = own_ref.shape[0]
    mine = lax.axis_index("dp")
    targets = (own_ref, send_ref.at[:rows], far_ref, send_ref.at[rows:])
    start = 0
    for (pieces, right), turned in zip(lefts, refs[used + 3 :]):
        turned[...] = jnp.concatenate([piece[...] for piece in pieces], axis=0).T
        width = right.shape[1]
        for step, target in enumerate(targets):
            place = pl.multiple_of((mine ^ step) * rows, rows)
            grad = dense(turned[pl.ds(place, rows), :], right[...])
            target[:, start : start + width] = grad.astype(jnp.bfloat16)
        start += width


def split_bits(values):
    high = values.astype(jnp.bfloat16)
    return high, (values - high.astype(jnp.float32)).astype(jnp.bfloat16)


def weight_grad(*products):
    depth, width = products[0][-1].shape[0], products[0][0].shape[1]
    columns = sum(product[-1].shape[1] for product in products)
    rows = width // 4
    shapes = (low(rows, columns), low(rows, columns), low(2 * rows, columns))
    turned = [pltpu.VMEM((width, depth), jnp.bfloat16)] * len(products)
    kernel = functools.partial(
        weight_grad_kernel, counts=tuple(len(product) - 1 for product in products)
    )
    args = [array for product in products for array in product]
    return call_once(kernel, args, shapes, 2 * depth * width * columns, turned)


def add_terms(left, right):
    f32 = lambda value: value.astype(jnp.float32)
    half = left.shape[0] // 2
    total = f32(left[:half]) + f32(left[half:]) + (f32(right[:half]) + f32(right[half:]))
    return jnp.concatenate(split_bits(total), axis=0)


def merge_kernel(own_ref, far_ref, got_ref, mine_ref, theirs_ref, sum_ref, send_ref):
    rows = own_ref.shape[0]
    sum_ref[:rows, :] = own_ref[...] + got_ref[:rows, :]
    send_ref[:rows, :] = far_ref[...] + got_ref[rows:, :]
    terms = jnp.concatenate(split_bits(mine_ref[...] + theirs_ref[...]), axis=0)
    sum_ref[rows:, :] = terms
    send_ref[rows:, :] = terms


def merge(own, far, got, mine, theirs):
    rows, columns = own.shape
    packet = low(rows + 2 * mine.shape[0], columns)
    args = (own, far, got, mine, theirs)
    return call_once(merge_kernel, args, (packet, packet), own.size)


def spread_kernel(left_ref, right_ref, *outs, rows):
    plane = lax.axis_index("context")
    terms = add_terms(left_ref[rows:, :], right_ref[rows:, :])
    piece = rows // 4
    for step, out in enumerate(outs):
        start = pl.multiple_of((plane + step) % 4 * piece, piece)
        out[:piece, :] = left_ref[pl.ds(start, piece), :] + right_ref[pl.ds(start, piece), :]
        out[piece:, :] = terms


def spread(left, right, rows):
    piece = low(rows // 4 + left.shape[0] - rows, left.shape[1])
    kernel = functools.partial(spread_kernel, rows=rows)
    return call_once(kernel, (left, right), (piece,) * 4, left.size)


def total_kernel(*refs, piece):
    parts, (sum_ref, vectors_ref, held_ref) = refs[:4], refs[4:]
    plane = lax.axis_index("context")
    f32 = lambda value: value.astype(jnp.float32)
    total = f32(parts[0][:piece, :]) + f32(parts[1][:piece, :])
    total += f32(parts[2][:piece, :]) + f32(parts[3][:piece, :])
    sum_ref[...] = total.astype(jnp.bfloat16)
    count = vectors_ref.shape[0]
    for step, part in enumerate(parts):
        held_ref[(plane + 4 - step) % 4] = f32(part[piece : piece + count, :]) + f32(
            part[piece + count :, :]
        )
    vectors_ref[...] = held_ref[0] + held_ref[1] + held_ref[2] + held_ref[3]


def total(parts, piece, count):
    columns = parts[0].shape[1]
    shapes = (low(piece, columns), full(count, columns))
    held_terms = pltpu.VMEM((4, count, columns), jnp.float32)
    kernel = functools.partial(total_kernel, piece=piece)
    return call_once(kernel, parts, shapes, 4 * piece * columns, [held_terms])


def assemble_kernel(a, b, c, d, query_ref, key_ref, value_ref, out_ref, turned):
    plane = lax.axis_index("context")
    piece = a.shape[0]
    local = query_ref.shape[1]
    for step, part in enumerate((a, b, c, d)):
        start = pl.multiple_of((plane + 4 - step) % 4 * piece, piece)
        here = part[...].astype(jnp.float32)
        for k, ref in enumerate((query_ref, key_ref, value_ref, turned)):
            ref[pl.ds(start, piece), :] = here[:, k * local : (k + 1) * local]
    out_ref[...] = turned[...].T


def assemble(parts):
    piece, columns = parts[0].shape
    rows, local = 4 * piece, columns // 4
    shapes = (full(rows, local),) * 3 + (full(local, rows),)
    turned = pltpu.VMEM((rows, local), jnp.float32)
    return call_once(assemble_kernel, parts, shapes, 4 * piece * columns, [turned])


def vectors_kernel(up_ref, down_ref, proj_ref, mine_ref, theirs_ref, out_ref):
    width = down_ref.shape[1]
    sides = mine_ref[...] + theirs_ref[...]
    out_ref[...] = jnp.zeros_like(out_ref)
    out_ref[0:1, :] = up_ref[...]
    for k in range(2):
        out_ref[1 + k : 2 + k, :width] = sides[2 * k : 2 * k + 1]
        out_ref[1 + k : 2 + k, width:] = sides[2 * k + 1 : 2 * k + 2]
    out_ref[3:4, :width] = sides[4:5]
    out_ref[3:4, width:] = down_ref[...]
    out_ref[4:5, : proj_ref.shape[1]] = proj_ref[...]


def gather_vectors(up, down, proj, mine, theirs):
    args = (up, down, proj, mine, theirs)
    return call_once(vectors_kernel, args, (full(8, up.shape[1]),), up.size)[0]


def exchange(value, bit):
    size = lax.axis_size("dp")
    return lax.ppermute(value, "dp", [(i, i ^ bit) for i in range(size)])


def swap_tensor(value):
    return lax.ppermute(value, "tensor", [(0, 1), (1, 0)])


def together(*values):
    return lax.optimization_barrier(values)


def route(value, step, inward):
    pairs = []
    for far in range(2):
        for near in range(2):
            for plane in range(4):
                home = (2 * far + near) * 4 + plane
                away = (2 * far + plane // 2) * 4 + 2 * near + (step ^ (plane % 2))
                pairs.append((away, home) if inward else (home, away))
    return lax.ppermute(value, ("dp", "context"), pairs)


def pick_in(array, odd, upper):
    mine = jnp.where(upper, array[:, 1], array[:, 0])
    return [jnp.where(odd, mine[1 - step], mine[step]) for step in range(2)]


def join_out(near, far, odd, upper):
    arranged = [jnp.where(odd, jnp.stack(v[::-1]), jnp.stack(v)) for v in (near, far)]
    own, peer = arranged
    return jnp.where(upper, jnp.stack([peer, own], axis=1), jnp.stack([own, peer], axis=1))


def join_shares(mine, theirs, odd, upper):
    total = lambda a, b: a.astype(jnp.float32) + b[::-1].astype(jnp.float32)
    values = [total(a, b).astype(jnp.bfloat16) for a, b in zip(mine, theirs)]
    arranged = jnp.where(odd, jnp.stack(values[::-1]), jnp.stack(values))
    return jnp.where(upper, arranged[:, ::-1], arranged)


def gathered(shard, far_shard):
    return (shard, exchange(shard, 1), far_shard, exchange(far_shard, 1))


def turn_planes(value, step):
    return lax.ppermute(value, "context", [(i, (i + step) % 4) for i in range(4)])


def inward(value):
    return lax.ppermute(value, "context", [(0, 1), (3, 2)])


def across(value):
    return lax.ppermute(value, "context", [(1, 2), (2, 1)])


def outward(value):
    return lax.ppermute(value, "context", [(1, 0), (2, 3)])


def per_device_planes(
    tokens,
    lengths,
    ln1_gain,
    ln1_bias,
    w_query,
    b_query,
    w_key,
    w_value,
    b_value,
    w_out,
    b_out,
    ln2_gain,
    ln2_bias,
    w_up,
    b_up,
    w_down,
    b_down,
    cotangent,
):
    block, width = tokens.shape[1:]
    half = block // 2
    local_width = w_query.shape[1]
    member = lax.axis_index("dp")
    near = member % 2
    plane = lax.axis_index("context")
    side = lax.axis_index("tensor")
    odd = plane % 2 == 1
    upper = side == 1
    inner = (plane == 1) | (plane == 2)
    row = lambda vector: vector.reshape(1, -1)

    by_half = (2, 2, half, width)
    groups = local_width // (2 * HEAD_DIM)
    picked = pick_in(tokens.reshape(by_half), odd, upper)
    *picked, w_query, w_key, w_value = together(*picked, w_query, w_key, w_value)
    rows_parts = [route(picked[step], step, True) for step in range(2)]
    proj_own = jnp.concatenate([w_query, w_key, w_value], axis=1)
    proj_far = exchange(proj_own, 2)
    proj_near = exchange(proj_own, 1)
    out_own = w_out.T
    out_peer = swap_tensor(out_own)
    lengths_other = exchange(lengths, 1)
    down_own = w_down.T
    *rows_parts, proj_far, proj_near, out_peer, lengths_other, down_own, cotangent = together(
        *rows_parts, proj_far, proj_near, out_peer, lengths_other, down_own, cotangent
    )

    rows_parts += [swap_tensor(v) for v in rows_parts]
    proj_last = exchange(proj_far, 1)
    down_far = exchange(down_own, 2)
    pack_own = jnp.concatenate([w_up, out_own, out_peer], axis=1)
    top_picked = pick_in(cotangent.reshape(by_half), odd, upper)
    top_parts = [route(top_picked[step], step, True) for step in range(2)]
    *rows_parts, proj_last, down_far, pack_own, top_0, top_1 = together(
        *rows_parts, proj_last, down_far, pack_own, *top_parts
    )

    pack_far = exchange(pack_own, 2)
    top_parts = [top_0, top_1, swap_tensor(top_0), swap_tensor(top_1)]
    proj_blocks = (proj_own, proj_near, proj_far, proj_last)
    lengths_near = jnp.where(plane // 2 == near, lengths, lengths_other)
    length = jnp.where(odd, lengths_near[1], lengths_near[0])
    index = jnp.arange(9, dtype=jnp.int32)
    quarter = index % 4
    core = jnp.where(index < 4, near, 1 - near)
    piece = jnp.where(quarter < 2, side, 1 - side)
    starts = (2 * core + (quarter % 2 ^ plane % 2)) * block + piece * half
    info = jnp.where(index < 8, starts, length)

    rows_low, normed_low, queries, pair_own, proj = enter(
        rows_parts, row(ln1_gain), row(ln1_bias), row(b_query), row(b_value), proj_blocks
    )
    pair_other = exchange(pair_own, 1)
    mixed, logs = attend(info, queries, pair_own, pair_other)

    mixed, down_own, down_far, pack_own, *top_parts = together(
        mixed, down_own, down_far, pack_own, *top_parts
    )
    mixed_peer = swap_tensor(mixed)
    down_blocks = gathered(down_own, down_far)
    pack_near = exchange(pack_own, 1)
    mixed_peer, pack_near, pack_far, *down_blocks = together(
        mixed_peer, pack_near, pack_far, *down_blocks
    )
    pack_blocks = (pack_own, pack_near, pack_far, exchange(pack_far, 1))
    (
        middle,
        normed_two,
        d_feed,
        hidden,
        d_pre,
        d_own,
        d_peer,
        *shares,
        out_t,
        grad_up_bias,
        grad_down_bias,
    ) = middle_part(
        info,
        rows_low,
        mixed,
        mixed_peer,
        top_parts,
        row(ln2_gain),
        row(ln2_bias),
        row(b_out),
        pack_blocks,
        down_blocks,
        row(b_up),
        row(b_down),
    )

    got = swap_tensor(d_peer)
    share_0 = route(shares[0], 0, False)
    down_own, down_far, down_send = weight_grad((d_feed, hidden))
    up_own, up_far, up_send = weight_grad((normed_two, d_pre))
    got, down_send, up_send, share_0, share_1 = together(
        got, down_send, up_send, share_0, shares[1]
    )

    down_got = exchange(down_send, 1)
    d_middle, d_att, sums_two = turn(info, middle, d_own, got, top_parts[:2], row(ln2_gain))
    d_att, down_got, up_send, share_1 = together(d_att, down_got, up_send, share_1)

    shard = down_own.shape[0]
    columns = hidden.shape[1]
    d_att_peer = swap_tensor(d_att)
    got_1 = exchange(down_far + down_got[shard:], 2)
    down_own = down_own + down_got[:shard]
    up_got = exchange(up_send, 1)
    share_1 = route(share_1, 1, False)
    d_att_peer, got_1, up_got, share_1 = together(d_att_peer, got_1, up_got, share_1)

    sum_1 = down_own + got_1
    got_1 = inward(sum_1)
    got_2 = exchange(up_far + up_got[shard:], 2)
    up_own = up_own + up_got[:shard]
    share_got = [swap_tensor(v) for v in (share_0, share_1)]
    d_queries, d_pair, d_send = attend_back(
        info, queries, pair_own, pair_other, mixed, d_att, d_att_peer, out_t, logs
    )
    d_send, got_1, got_2, *share_got = together(d_send, got_1, got_2, *share_got)

    d_got = exchange(d_send, 1)
    sum_1 = sum_1 + got_1
    sum_2 = up_own + got_2
    got_1 = across(sum_1)
    got_2 = inward(sum_2)
    d_proj, one_own, one_peer, sides, proj_bias = leave(
        rows_low, proj, d_queries, d_pair, d_got, sums_two
    )
    own, far, send = weight_grad((normed_low, d_proj), (d_att, d_att_peer, mixed))
    one_peer, sides, send, got_1, got_2 = together(one_peer, sides, send, got_1, got_2)

    send_got = exchange(send, 1)
    sides_got = swap_tensor(sides)
    one_got = swap_tensor(one_peer)
    sum_1 = sum_1 + got_1
    sum_2 = sum_2 + got_2
    got_1 = outward(sum_1)
    got_2 = across(sum_2)
    send_got, one_got, got_1, got_2, sides_got = together(
        send_got, one_got, got_1, got_2, sides_got
    )

    vectors = gather_vectors(grad_up_bias, grad_down_bias, proj_bias, sides, sides_got)
    vectors_got = exchange(vectors, 1)
    input_rows = finish(rows_low, one_own, one_got, row(ln1_gain), d_middle)
    *input_rows, vectors_got = together(*input_rows, vectors_got)

    packet, packet_far = merge(own, far, send_got, vectors, vectors_got)
    packet_got = exchange(packet_far, 2)
    in_near = [route(input_rows[step], step, False) for step in range(2)]
    sum_2 = sum_2 + got_2
    got_2 = outward(sum_2)
    grad_down = jnp.where(inner, sum_1, got_1).astype(jnp.float32).T
    packet_got, got_2, *pieces = together(packet_got, got_2, *in_near, *share_got)
    in_near, share_got = pieces[:2], pieces[2:]

    quarters = spread(packet, packet_got, shard)
    arrived = [turn_planes(quarters[step], step) for step in range(1, 4)]
    in_far = [swap_tensor(v) for v in in_near]
    grad_up = jnp.where(inner, sum_2, got_2).astype(jnp.float32)
    output = join_shares((share_0, share_1), share_got, odd, upper)
    pieces = together(quarters[0], *arrived, *in_far)

    in_far = pieces[4:]
    quarter, vectors = total(pieces[:4], shard // 4, vectors.shape[0])
    quarters = [quarter] + [turn_planes(quarter, step) for step in range(1, 4)]
    input_grad = join_out(in_near, in_far, odd, upper)
    grad_query, grad_key, grad_value, grad_out = assemble(quarters)

    return (
        output.reshape(tokens.shape),
        input_grad.reshape(tokens.shape),
        vectors[1, :width],
        vectors[1, width:],
        grad_query,
        vectors[4, :local_width],
        grad_key,
        grad_value,
        vectors[4, 2 * local_width : 3 * local_width],
        grad_out,
        vectors[3, :width],
        vectors[2, :width],
        vectors[2, width:],
        grad_up,
        vectors[0],
        grad_down,
        vectors[3, width:],
    )


def pick(mesh):
    sizes = mesh.shape
    planes = sizes["dp"] == 4 and sizes["context"] == 4 and sizes["tensor"] == 2
    return per_device_planes if planes else per_device_general


def solution(mesh):
    return jax.shard_map(
        pick(mesh),
        mesh=mesh,
        in_specs=(
            P("dp", "context", None),
            P("dp"),
            P(),
            P(),
            P("dp", "tensor"),
            P("tensor"),
            P("dp", "tensor"),
            P("dp", "tensor"),
            P("tensor"),
            P("tensor", "dp"),
            P(),
            P(),
            P(),
            P("dp", "tensor"),
            P("tensor"),
            P("tensor", "dp"),
            P(),
            P("dp", "context", None),
        ),
        out_specs=(
            P("dp", "context", None),
            P("dp", "context", None),
            P(),
            P(),
            P("dp", "tensor"),
            P("tensor"),
            P("dp", "tensor"),
            P("dp", "tensor"),
            P("tensor"),
            P("tensor", "dp"),
            P(),
            P(),
            P(),
            P("dp", "tensor"),
            P("tensor"),
            P("tensor", "dp"),
            P(),
        ),
        check_vma=False,
    )
```

```python
import functools

import jax
import jax.numpy as jnp
from jax import lax
from jax.experimental import pallas as pl
from jax.experimental.pallas import tpu as pltpu
from jax.sharding import PartitionSpec as P

HEAD_DIM = 64


epsilon = 1e-06
masked_value = -1e30


def norm_rows(values, gain_vec, bias_vec):
    average = jnp.mean(values, axis=-1, keepdims=True)
    centred = values - average
    spread = jnp.mean(centred * centred, axis=-1, keepdims=True)
    return centred * lax.rsqrt(spread + epsilon) * gain_vec + bias_vec


def gelu_tanh(values):
    return jax.nn.gelu(values, approximate=True)


def dense(left, right):
    return jnp.dot(left, right, preferred_element_type=jnp.float32)


def dense_tn(left, right):
    return lax.dot_general(
        left, right, (((0,), (0,)), ((), ())), preferred_element_type=jnp.float32
    )


def dense_nt(left, right):
    return lax.dot_general(
        left, right, (((1,), (1,)), ((), ())), preferred_element_type=jnp.float32
    )


def per_device_general(
    tokens,
    lengths,
    ln1_gain,
    ln1_bias,
    w_query,
    b_query,
    w_key,
    w_value,
    b_value,
    w_out,
    b_out,
    ln2_gain,
    ln2_bias,
    w_up,
    b_up,
    w_down,
    b_down,
    cotangent,
):
    seq_count, shard_rows, width = tokens.shape
    full_len = shard_rows * lax.axis_size("context")
    local_width = w_query.shape[1]
    local_heads = local_width // HEAD_DIM
    scale = HEAD_DIM ** (-0.5)
    row_count = seq_count * shard_rows
    query_weight, key_weight, value_weight, up_weight, out_weight, down_weight = (
        lax.all_gather(w_query, "dp", axis=0, tiled=True),
        lax.all_gather(w_key, "dp", axis=0, tiled=True),
        lax.all_gather(w_value, "dp", axis=0, tiled=True),
        lax.all_gather(w_up, "dp", axis=0, tiled=True),
        lax.all_gather(w_out, "dp", axis=1, tiled=True),
        lax.all_gather(w_down, "dp", axis=1, tiled=True),
    )
    gain_one = ln1_gain.astype(jnp.float32)
    bias_one = ln1_bias.astype(jnp.float32)
    query_bias = b_query.astype(jnp.float32)
    value_bias = b_value.astype(jnp.float32)
    out_bias = b_out.astype(jnp.float32)
    gain_two = ln2_gain.astype(jnp.float32)
    bias_two = ln2_bias.astype(jnp.float32)
    up_bias = b_up.astype(jnp.float32)
    down_bias = b_down.astype(jnp.float32)
    places = lax.axis_index("context") * shard_rows + jnp.arange(shard_rows, dtype=jnp.int32)
    keep = (places[None, :] < lengths[:, None]).astype(jnp.float32).reshape(row_count, 1)
    key_places = jnp.arange(full_len, dtype=jnp.int32)
    rows_in = tokens.reshape(row_count, width).astype(jnp.float32)
    normed_one, pull_one = jax.vjp(norm_rows, rows_in, gain_one, bias_one)
    normed_low = normed_one.astype(jnp.bfloat16)
    queries = (dense(normed_low, query_weight) + query_bias).astype(jnp.bfloat16)
    keys_own = dense(normed_low, key_weight).astype(jnp.bfloat16)
    values_own = (dense(normed_low, value_weight) + value_bias).astype(jnp.bfloat16)
    keys_whole, values_whole = (
        lax.all_gather(
            keys_own.reshape(seq_count, shard_rows, local_width), "context", axis=1, tiled=True
        ),
        lax.all_gather(
            values_own.reshape(seq_count, shard_rows, local_width), "context", axis=1, tiled=True
        ),
    )
    query_heads = queries.reshape(seq_count, shard_rows, local_heads, HEAD_DIM)
    head_outs = []
    log_sums = []
    for member in range(seq_count):
        key_heads = keys_whole[member].reshape(full_len, local_heads, HEAD_DIM)
        value_heads = values_whole[member].reshape(full_len, local_heads, HEAD_DIM)
        raw_scores = (
            jnp.einsum(
                "qhd,khd->hqk", query_heads[member], key_heads, preferred_element_type=jnp.float32
            )
            * scale
        )
        live = (key_places < lengths[member])[None, None, :]
        masked = jnp.where(live, raw_scores, masked_value)
        largest = jnp.max(masked, axis=-1, keepdims=True)
        log_total = largest + jnp.log(jnp.sum(jnp.exp(masked - largest), axis=-1, keepdims=True))
        probs_low = jnp.exp(masked - log_total).astype(jnp.bfloat16)
        mixed_heads = jnp.einsum(
            "hqk,khd->qhd", probs_low, value_heads, preferred_element_type=jnp.float32
        )
        head_outs.append(mixed_heads.reshape(shard_rows, local_width))
        log_sums.append(log_total)
    context_low = jnp.concatenate(head_outs, axis=0).astype(jnp.bfloat16)
    attention = (
        lax.psum(dense(context_low, out_weight).astype(jnp.bfloat16), "tensor").astype(jnp.float32)
        + out_bias
    )
    middle = rows_in + keep * attention
    normed_two, pull_two = jax.vjp(norm_rows, middle, gain_two, bias_two)
    normed_two_low = normed_two.astype(jnp.bfloat16)
    hidden_pre = dense(normed_two_low, up_weight) + up_bias
    hidden, pull_gelu = jax.vjp(gelu_tanh, hidden_pre)
    hidden_low = hidden.astype(jnp.bfloat16)
    feed = (
        lax.psum(dense(hidden_low, down_weight).astype(jnp.bfloat16), "tensor").astype(jnp.float32)
        + down_bias
    )
    output = (middle + keep * feed).astype(jnp.bfloat16).reshape(tokens.shape)
    grad_top = cotangent.reshape(row_count, width).astype(jnp.float32)
    d_feed = (keep * grad_top).astype(jnp.bfloat16)
    grad_down_bias = jnp.sum(d_feed.astype(jnp.float32), axis=0)
    grad_down = dense_tn(hidden_low, d_feed)
    d_hidden = dense_nt(d_feed, down_weight)
    d_pre = pull_gelu(d_hidden)[0].astype(jnp.bfloat16)
    grad_up_bias = jnp.sum(d_pre.astype(jnp.float32), axis=0)
    grad_up = dense_tn(normed_two_low, d_pre)
    d_normed_two = lax.psum(dense_nt(d_pre, up_weight).astype(jnp.bfloat16), "tensor").astype(
        jnp.float32
    )
    d_middle, grad_gain_two, grad_bias_two = pull_two(d_normed_two)
    d_middle = d_middle + grad_top
    d_attention = (keep * d_middle).astype(jnp.bfloat16)
    grad_out_bias = jnp.sum(d_attention.astype(jnp.float32), axis=0)
    grad_out = dense_tn(context_low, d_attention)
    d_context = dense_nt(d_attention, out_weight).astype(jnp.bfloat16)
    back_keys, back_values = (keys_whole, values_whole)
    d_context_heads = d_context.reshape(seq_count, shard_rows, local_heads, HEAD_DIM)
    query_grads = []
    own_grads = []
    inner_rows = []
    for member in range(seq_count):
        key_heads = back_keys[member].reshape(full_len, local_heads, HEAD_DIM)
        value_heads = back_values[member].reshape(full_len, local_heads, HEAD_DIM)
        raw_scores = (
            jnp.einsum(
                "qhd,khd->hqk", query_heads[member], key_heads, preferred_element_type=jnp.float32
            )
            * scale
        )
        live = (key_places < lengths[member])[None, None, :]
        probs = jnp.where(live, jnp.exp(raw_scores - log_sums[member]), 0.0)
        d_probs = jnp.einsum(
            "qhd,khd->hqk", d_context_heads[member], value_heads, preferred_element_type=jnp.float32
        )
        inner = jnp.sum(probs * d_probs, axis=-1, keepdims=True)
        d_scores = (probs * (d_probs - inner)).astype(jnp.bfloat16)
        d_query = (
            jnp.einsum("hqk,khd->qhd", d_scores, key_heads, preferred_element_type=jnp.float32)
            * scale
        )
        query_grads.append(d_query.reshape(shard_rows, local_width))
        inner_rows.append(inner[:, :, 0])
        d_keys = (
            jnp.einsum(
                "hqk,qhd->khd", d_scores, query_heads[member], preferred_element_type=jnp.float32
            )
            * scale
        )
        d_values = jnp.einsum(
            "hqk,qhd->khd",
            probs.astype(jnp.bfloat16),
            d_context_heads[member],
            preferred_element_type=jnp.float32,
        )
        key_term = jnp.concatenate(
            [d_keys.reshape(full_len, local_width), d_values.reshape(full_len, local_width)], axis=1
        )
        own_grads.append(
            lax.psum_scatter(
                key_term.astype(jnp.bfloat16), "context", scatter_dimension=0, tiled=True
            ).astype(jnp.float32)
        )
    d_query_low = jnp.concatenate(query_grads, axis=0).astype(jnp.bfloat16)
    key_value_grads = jnp.concatenate(own_grads, axis=0)
    d_keys_low = key_value_grads[:, :local_width].astype(jnp.bfloat16)
    d_values_low = key_value_grads[:, local_width:].astype(jnp.bfloat16)
    grad_query = dense_tn(normed_low, d_query_low)
    grad_query_bias = jnp.sum(d_query_low.astype(jnp.float32), axis=0)
    grad_key = dense_tn(normed_low, d_keys_low)
    grad_value = dense_tn(normed_low, d_values_low)
    grad_value_bias = jnp.sum(d_values_low.astype(jnp.float32), axis=0)
    d_normed_one = lax.psum(
        (
            dense_nt(d_query_low, query_weight)
            + dense_nt(d_keys_low, key_weight)
            + dense_nt(d_values_low, value_weight)
        ).astype(jnp.bfloat16),
        "tensor",
    ).astype(jnp.float32)
    d_rows, grad_gain_one, grad_bias_one = pull_one(d_normed_one)
    input_grad = (d_rows + d_middle).astype(jnp.bfloat16).reshape(tokens.shape)
    data_sums = (
        lax.psum_scatter(
            grad_query.astype(jnp.bfloat16), "dp", scatter_dimension=0, tiled=True
        ).astype(jnp.float32),
        lax.psum_scatter(
            grad_key.astype(jnp.bfloat16), "dp", scatter_dimension=0, tiled=True
        ).astype(jnp.float32),
        lax.psum_scatter(
            grad_value.astype(jnp.bfloat16), "dp", scatter_dimension=0, tiled=True
        ).astype(jnp.float32),
        lax.psum_scatter(
            grad_up.astype(jnp.bfloat16), "dp", scatter_dimension=0, tiled=True
        ).astype(jnp.float32),
        lax.psum_scatter(
            grad_out.astype(jnp.bfloat16), "dp", scatter_dimension=1, tiled=True
        ).astype(jnp.float32),
        lax.psum_scatter(
            grad_down.astype(jnp.bfloat16), "dp", scatter_dimension=1, tiled=True
        ).astype(jnp.float32),
    )
    owned_sums = (
        lax.psum(data_sums[0].astype(jnp.bfloat16), "context").astype(jnp.float32),
        lax.psum(data_sums[1].astype(jnp.bfloat16), "context").astype(jnp.float32),
        lax.psum(data_sums[2].astype(jnp.bfloat16), "context").astype(jnp.float32),
        lax.psum(data_sums[3].astype(jnp.bfloat16), "context").astype(jnp.float32),
        lax.psum(data_sums[4].astype(jnp.bfloat16), "context").astype(jnp.float32),
        lax.psum(data_sums[5].astype(jnp.bfloat16), "context").astype(jnp.float32),
    )
    small_sums = lax.psum(
        (
            grad_gain_one,
            grad_bias_one,
            grad_query_bias,
            grad_value_bias,
            grad_out_bias,
            grad_gain_two,
            grad_bias_two,
            grad_up_bias,
            grad_down_bias,
        ),
        ("dp", "context"),
    )
    return (
        output,
        input_grad,
        small_sums[0],
        small_sums[1],
        owned_sums[0],
        small_sums[2],
        owned_sums[1],
        owned_sums[2],
        small_sums[3],
        owned_sums[4],
        small_sums[4],
        small_sums[5],
        small_sums[6],
        owned_sums[3],
        small_sums[7],
        owned_sums[5],
        small_sums[8],
    )


def live_bias(info, count):
    places = lax.broadcasted_iota(jnp.int32, (count, 2 * HEAD_DIM), 0)
    return jnp.concatenate(
        [jnp.where(info[k] + places < info[8], 0.0, masked_value) for k in range(8)], axis=0
    ).astype(jnp.bfloat16)


def split_pair(array, extra):
    lane = lax.broadcasted_iota(jnp.int32, array.shape, 1)
    zero = jnp.zeros((), jnp.bfloat16)
    left = jnp.where(lane < HEAD_DIM, array, jnp.where(lane == HEAD_DIM, extra, zero))
    right = jnp.where(lane >= HEAD_DIM, array, jnp.where(lane == 0, extra, zero))
    return left, right


LOG_SCALE = HEAD_DIM ** (-0.5) * 1.4426950408889634


def attend_kernel(info, query_ref, own_ref, other_ref, out_ref, log_ref):
    pair = 2 * HEAD_DIM
    count = query_ref.shape[0] // 4
    keys = jnp.concatenate([own_ref[:, :pair], other_ref[:, :pair]], axis=0)
    values = jnp.concatenate([own_ref[:, pair:], other_ref[:, pair:]], axis=0)
    values_t = values.T
    key_heads = split_pair(keys, live_bias(info, count))
    query_heads = split_pair(query_ref[...], jnp.ones((), jnp.bfloat16))
    mixed = []
    for head in range(2):
        scores = dense_nt(key_heads[head], query_heads[head])
        largest = jnp.max(scores, axis=0, keepdims=True)
        weights = jnp.exp2((scores - largest) * LOG_SCALE)
        total = jnp.sum(weights, axis=0, keepdims=True)
        dims = slice(head * HEAD_DIM, (head + 1) * HEAD_DIM)
        mixed.append(dense(values_t[dims], weights.astype(jnp.bfloat16)) / total)
        log_ref[0, head : head + 1, :] = largest * LOG_SCALE + jnp.log2(total)
    out_ref[...] = jnp.concatenate(mixed, axis=0).T.astype(jnp.bfloat16)


def attend(info, queries, pair_own, pair_other):
    rows, width = queries.shape
    pair = 2 * HEAD_DIM
    groups = width // pair
    work = 4 * rows * 2 * rows * width
    return pl.pallas_call(
        attend_kernel,
        out_shape=(
            jax.ShapeDtypeStruct((rows, width), jnp.bfloat16),
            jax.ShapeDtypeStruct((groups, 2, rows), jnp.float32),
        ),
        grid_spec=pltpu.PrefetchScalarGridSpec(
            num_scalar_prefetch=1,
            grid=(groups,),
            in_specs=[
                pl.BlockSpec((rows, pair), lambda g, info: (0, g)),
                pl.BlockSpec((rows, 2 * pair), lambda g, info: (0, g)),
                pl.BlockSpec((rows, 2 * pair), lambda g, info: (0, g)),
            ],
            out_specs=(
                pl.BlockSpec((rows, pair), lambda g, info: (0, g)),
                pl.BlockSpec((1, 2, rows), lambda g, info: (g, 0, 0)),
            ),
        ),
        compiler_params=pltpu.CompilerParams(vmem_limit_bytes=32 << 20),
        cost_estimate=pl.CostEstimate(
            flops=4 * work, bytes_accessed=12 * rows * width, transcendentals=work // (2 * HEAD_DIM)
        ),
    )(info, queries, pair_own, pair_other)


def attend_back_kernel(
    info,
    query_ref,
    own_ref,
    other_ref,
    out_ref,
    d_own_ref,
    d_peer_ref,
    proj_ref,
    log_ref,
    d_query_ref,
    d_pair_ref,
    d_other_ref,
):
    pair = 2 * HEAD_DIM
    rows = query_ref.shape[0]
    scale = HEAD_DIM ** (-0.5)
    keys = jnp.concatenate([own_ref[:, :pair], other_ref[:, :pair]], axis=0)
    values = jnp.concatenate([own_ref[:, pair:], other_ref[:, pair:]], axis=0)
    keys_t = keys.T
    key_heads = split_pair(keys, live_bias(info, rows // 4))
    value_heads = split_pair(values, jnp.zeros((), jnp.bfloat16))
    query = query_ref[...]
    query_heads = split_pair(query, jnp.ones((), jnp.bfloat16))
    d_att = jnp.concatenate([d_own_ref[...], d_peer_ref[...]], axis=0)
    grad = dense(d_att, proj_ref[...]).astype(jnp.bfloat16)
    inner_t = (grad.astype(jnp.float32) * out_ref[...].astype(jnp.float32)).T
    d_query, d_keys, d_values = [], [], []
    for head in range(2):
        dims = slice(head * HEAD_DIM, (head + 1) * HEAD_DIM)
        inner = jnp.sum(inner_t[dims], axis=0, keepdims=True)
        scores = dense_nt(key_heads[head], query_heads[head])
        probs = jnp.exp2(scores * LOG_SCALE - log_ref[0, head : head + 1, :])
        d_probs = dense_nt(value_heads[head], grad)
        d_scores = (probs * (d_probs - inner)).astype(jnp.bfloat16)
        d_query.append(dense(keys_t[dims], d_scores))
        d_keys.append(dense(d_scores, query))
        d_values.append(dense(probs.astype(jnp.bfloat16), grad))
    d_query_ref[...] = (jnp.concatenate(d_query, axis=0).T * scale).astype(jnp.bfloat16)
    left = lax.broadcasted_iota(jnp.int32, d_keys[0].shape, 1) < HEAD_DIM
    d_key = (jnp.where(left, d_keys[0], d_keys[1]) * scale).astype(jnp.bfloat16)
    d_value = jnp.where(left, d_values[0], d_values[1]).astype(jnp.bfloat16)
    d_pair_ref[:, :pair] = d_key[:rows]
    d_pair_ref[:, pair:] = d_value[:rows]
    d_other_ref[:, :pair] = d_key[rows:]
    d_other_ref[:, pair:] = d_value[rows:]


def attend_back(info, queries, pair_own, pair_other, mixed, d_own, d_peer, out_t, logs):
    rows, local = queries.shape
    width = out_t.shape[0]
    pair = 2 * HEAD_DIM
    work = 4 * rows * 2 * rows * local
    narrow = pl.BlockSpec((rows, pair), lambda g, info: (0, g))
    wide = pl.BlockSpec((rows, 2 * pair), lambda g, info: (0, g))
    halves = pl.BlockSpec((rows // 2, width), lambda g, info: (0, 0))
    return pl.pallas_call(
        attend_back_kernel,
        out_shape=tuple(
            jax.ShapeDtypeStruct((rows, columns), jnp.bfloat16)
            for columns in (local, 2 * local, 2 * local)
        ),
        grid_spec=pltpu.PrefetchScalarGridSpec(
            num_scalar_prefetch=1,
            grid=(local // pair,),
            in_specs=[
                narrow,
                wide,
                wide,
                narrow,
                halves,
                halves,
                pl.BlockSpec((width, pair), lambda g, info: (0, g)),
                pl.BlockSpec((1, 2, rows), lambda g, info: (g, 0, 0)),
            ],
            out_specs=(narrow, wide, wide),
        ),
        compiler_params=pltpu.CompilerParams(vmem_limit_bytes=32 << 20),
        cost_estimate=pl.CostEstimate(
            flops=10 * work, bytes_accessed=24 * rows * local, transcendentals=work // (2 * HEAD_DIM)
        ),
    )(info, queries, pair_own, pair_other, mixed, d_own, d_peer, out_t, logs)


def held(info, quarters, count, width):
    places = lax.broadcasted_iota(jnp.int32, (count, width), 0)
    return jnp.concatenate([info[k] + places < info[8] for k in range(quarters)], axis=0)


def fixed(array):
    return pl.BlockSpec(array.shape, lambda i: (0,) * len(array.shape))


def call_once(kernel, args, shapes, flops, scratch=()):
    moved = sum(a.size * a.dtype.itemsize for a in (*args, *shapes))
    return pl.pallas_call(
        kernel,
        out_shape=tuple(shapes),
        grid=(1,),
        in_specs=[fixed(a) for a in args],
        out_specs=tuple(fixed(s) for s in shapes),
        scratch_shapes=list(scratch),
        compiler_params=pltpu.CompilerParams(vmem_limit_bytes=24 << 20),
        cost_estimate=pl.CostEstimate(flops=flops, bytes_accessed=moved, transcendentals=0),
    )(*args)


def low(*shape):
    return jax.ShapeDtypeStruct(shape, jnp.bfloat16)


def full(*shape):
    return jax.ShapeDtypeStruct(shape, jnp.float32)


def row_stats(values):
    centred = values - jnp.mean(values, axis=-1, keepdims=True)
    spread = jnp.mean(centred * centred, axis=-1, keepdims=True)
    root = lax.rsqrt(spread + epsilon)
    return centred * root, root


def row_pull(normed, root, grad):
    return root * (
        grad
        - jnp.mean(grad, axis=-1, keepdims=True)
        - normed * jnp.mean(grad * normed, axis=-1, keepdims=True)
    )


def settle(parts, out_ref):
    rows = parts[0].shape[0]
    mine = lax.axis_index("dp")
    for step, part in enumerate(parts):
        start = pl.multiple_of((mine ^ step) * rows, rows)
        out_ref[pl.ds(start, rows), :] = part[...]


def enter_kernel(
    own0, own1, peer0, peer1, gain_ref, bias_ref, q_bias_ref, v_bias_ref, a, b, c, d,
    rows_ref, normed_ref, query_ref, pair_ref, proj_ref,
):
    pair = 2 * HEAD_DIM
    settle((a, b, c, d), proj_ref)
    rows = jnp.concatenate([own0[...], own1[...], peer0[...], peer1[...]], axis=0)
    rows_ref[...] = rows
    normed, _ = row_stats(rows.astype(jnp.float32))
    normed = normed * gain_ref[...].astype(jnp.float32) + bias_ref[...].astype(jnp.float32)
    normed = normed.astype(jnp.bfloat16)
    normed_ref[...] = normed
    local = query_ref.shape[1]
    mixed = dense(normed, proj_ref[...])
    query_ref[...] = (mixed[:, :local] + q_bias_ref[...].astype(jnp.float32)).astype(jnp.bfloat16)
    for g in range(local // pair):
        cols = slice(g * pair, (g + 1) * pair)
        key = mixed[:, local + g * pair : local + (g + 1) * pair]
        value = mixed[:, 2 * local + g * pair : 2 * local + (g + 1) * pair]
        value = value + v_bias_ref[:, cols].astype(jnp.float32)
        pair_ref[:, 2 * g * pair : (2 * g + 1) * pair] = key.astype(jnp.bfloat16)
        pair_ref[:, (2 * g + 1) * pair : (2 * g + 2) * pair] = value.astype(jnp.bfloat16)


def enter(pieces, gain, bias, q_bias, v_bias, blocks):
    half, width = pieces[0].shape
    rows = 4 * half
    local = q_bias.shape[1]
    shapes = (
        low(rows, width),
        low(rows, width),
        low(rows, local),
        low(rows, 2 * local),
        low(width, 3 * local),
    )
    args = (*pieces, gain, bias, q_bias, v_bias, *blocks)
    return call_once(enter_kernel, args, shapes, 6 * rows * width * local)


ROOT_TWO_OVER_PI = 0.7978845608028654
CUBE = 0.044715


def fetch(parts, columns, out_ref, sems):
    rows = parts[0].shape[0]
    mine = lax.axis_index("dp")
    copies = []
    for step, part in enumerate(parts):
        start = pl.multiple_of((mine ^ step) * rows, rows)
        copy = pltpu.make_async_copy(
            part.at[:, columns], out_ref.at[pl.ds(start, rows)], sems.at[step]
        )
        copy.start()
        copies.append(copy)
    return copies


def middle_kernel(
    info, rows_ref, own_ref, peer_ref, top0, top1, top2, top3, gain_ref, bias_ref, out_bias_ref,
    up_bias_ref, down_bias_ref, pa, pb, pc, pd, da, db, dc, dd,
    mid_ref, normed_ref, feed_ref, hidden_ref, d_pre_ref, d_own_ref, d_peer_ref,
    part0_ref, part1_ref, out_ref, g_up_ref, g_down_ref,
    outs, ups, downs, whole_mid, sent, sems,
):
    rows, width = rows_ref.shape
    half = rows // 2
    local = own_ref.shape[1]
    hidden_width = up_bias_ref.shape[1]
    steps = ups.shape[0]
    tile = hidden_width // steps
    packs, lasts = (pa, pb, pc, pd), (da, db, dc, dd)
    waits = [fetch(packs, pl.ds(hidden_width, width), outs, sems.at[0])]
    for s in range(steps):
        columns = pl.ds(s * tile, tile)
        waits.append(fetch(packs, columns, ups.at[s], sems.at[1 + 2 * s]))
        waits.append(fetch(lasts, columns, downs.at[s], sems.at[2 + 2 * s]))

    real = held(info, 4, rows // 4, width)
    top = jnp.concatenate([top0[...], top1[...], top2[...], top3[...]], axis=0)
    feed = jnp.where(real, top.astype(jnp.float32), 0.0)
    feed_ref[...] = feed.astype(jnp.bfloat16)
    g_down_ref[...] = jnp.sum(feed, axis=0, keepdims=True)
    peer = jnp.concatenate([peer_ref[half:, :], peer_ref[:half, :]], axis=0)
    for copy in waits[0]:
        copy.wait()
    out_ref[...] = outs[:, :local]
    attention = (
        dense_nt(own_ref[...], outs[:, :local])
        + dense_nt(peer, outs[:, local:])
        + out_bias_ref[...].astype(jnp.float32)
    )
    mid = rows_ref[...].astype(jnp.float32) + jnp.where(real, attention, 0.0)
    mid_ref[...] = mid[:half]
    whole_mid[...] = mid
    normed, _ = row_stats(mid)
    normed = normed * gain_ref[...].astype(jnp.float32) + bias_ref[...].astype(jnp.float32)
    normed_ref[...] = normed.astype(jnp.bfloat16)

    for s in range(steps):
        columns = slice(s * tile, (s + 1) * tile)
        for copy in waits[1 + 2 * s] + waits[2 + 2 * s]:
            copy.wait()
        pre = dense(normed_ref[...], ups[s]) + up_bias_ref[:, columns].astype(jnp.float32)
        d_hidden = dense(feed_ref[...], downs[s])
        square = pre * pre
        bend = jnp.tanh(pre * (ROOT_TWO_OVER_PI + CUBE * ROOT_TWO_OVER_PI * square))
        half_up = 0.5 + 0.5 * bend
        active = pre * half_up
        slope = half_up + active * (1.0 - bend) * (
            ROOT_TWO_OVER_PI + 3.0 * CUBE * ROOT_TWO_OVER_PI * square
        )
        hidden_ref[:, columns] = active.astype(jnp.bfloat16)
        d_pre = (d_hidden * slope).astype(jnp.bfloat16)
        d_pre_ref[:, columns] = d_pre
        g_up_ref[:, columns] = jnp.sum(d_pre.astype(jnp.float32), axis=0, keepdims=True)

    def back(left_ref, right_ref):
        total = 0.0
        for s in range(steps):
            total += dense_nt(left_ref[:, s * tile : (s + 1) * tile], right_ref[s])
        return total

    grad = back(d_pre_ref, ups).astype(jnp.bfloat16)
    d_own_ref[...] = grad[:half]
    sent[...] = grad[half:]
    leaving = pltpu.make_async_copy(sent, d_peer_ref, sems.at[0, 0])
    leaving.start()
    first = lax.axis_index("tensor") == 0
    share = back(hidden_ref, downs)
    share += jnp.where(first, down_bias_ref[...].astype(jnp.float32), 0.0)
    share = jnp.where(real, share, 0.0) + jnp.where(first, whole_mid[...], 0.0)
    share = share.astype(jnp.bfloat16)
    for k, part in enumerate((part0_ref, part1_ref)):
        start = k * (half // 2)
        part[0] = share[start : start + half // 2]
        part[1] = share[half + start : half + start + half // 2]
    leaving.wait()


def middle_part(
    info, rows_low, own, peer, top, gain, bias, out_bias, packs, downs, up_bias, down_bias
):
    rows, width = rows_low.shape
    local = own.shape[1]
    hidden = up_bias.shape[1]
    steps = 2
    small = (rows_low, own, peer, *top, gain, bias, out_bias, up_bias, down_bias)
    inside = pl.BlockSpec(memory_space=pltpu.VMEM)
    outside = pl.BlockSpec(memory_space=pltpu.HBM)
    shapes = (
        full(rows // 2, width),
        low(rows, width),
        low(rows, width),
        low(rows, hidden),
        low(rows, hidden),
        low(rows // 2, width),
        low(rows // 2, width),
        low(2, rows // 4, width),
        low(2, rows // 4, width),
        low(width, local),
        full(1, hidden),
        full(1, width),
    )
    return pl.pallas_call(
        middle_kernel,
        out_shape=shapes,
        in_specs=[pl.BlockSpec(memory_space=pltpu.SMEM)]
        + [inside] * len(small)
        + [pl.BlockSpec(memory_space=pltpu.HBM)] * 8,
        out_specs=tuple(outside if k == 6 else inside for k in range(len(shapes))),
        scratch_shapes=[
            pltpu.VMEM((width, width), jnp.bfloat16),
            pltpu.VMEM((steps, width, hidden // steps), jnp.bfloat16),
            pltpu.VMEM((steps, width, hidden // steps), jnp.bfloat16),
            pltpu.VMEM((rows, width), jnp.float32),
            pltpu.VMEM((rows // 2, width), jnp.bfloat16),
            pltpu.SemaphoreType.DMA((1 + 2 * steps, 4)),
        ],
        compiler_params=pltpu.CompilerParams(vmem_limit_bytes=36 << 20),
        cost_estimate=pl.CostEstimate(
            flops=8 * rows * width * hidden, bytes_accessed=20 << 20, transcendentals=rows * hidden
        ),
    )(info, *small, *packs, *downs)


def turn_kernel(
    info, mid_ref, d_own_ref, got_ref, top0, top1, gain_ref, d_mid_ref, d_att_ref, sums_ref
):
    half, width = d_own_ref.shape
    grad = d_own_ref[...].astype(jnp.float32) + got_ref[...].astype(jnp.float32)
    normed, root = row_stats(mid_ref[...])
    top = jnp.concatenate([top0[...], top1[...]], axis=0).astype(jnp.float32)
    d_mid = top + row_pull(normed, root, grad * gain_ref[...].astype(jnp.float32))
    d_mid_ref[...] = d_mid
    d_att = jnp.where(held(info, 2, half // 2, width), d_mid, 0.0).astype(jnp.bfloat16)
    d_att_ref[...] = d_att
    sums_ref[0:1, :] = jnp.sum(grad * normed, axis=0, keepdims=True)
    sums_ref[1:2, :] = jnp.sum(grad, axis=0, keepdims=True)
    sums_ref[2:3, :] = jnp.sum(d_att.astype(jnp.float32), axis=0, keepdims=True)


def turn(info, mid, d_own, got, top, gain):
    half, width = d_own.shape
    fixed = lambda a: pl.BlockSpec(a.shape, lambda i, info: (0,) * len(a.shape))
    first = pl.BlockSpec((half, width), lambda i, info: (0, 0))
    shapes = (
        jax.ShapeDtypeStruct((half, width), jnp.float32),
        jax.ShapeDtypeStruct((half, width), jnp.bfloat16),
        jax.ShapeDtypeStruct((3, width), jnp.float32),
    )
    return pl.pallas_call(
        turn_kernel,
        out_shape=shapes,
        grid_spec=pltpu.PrefetchScalarGridSpec(
            num_scalar_prefetch=1,
            grid=(1,),
            in_specs=[first, fixed(d_own), fixed(got), fixed(top[0]), fixed(top[1]), fixed(gain)],
            out_specs=tuple(fixed(s) for s in shapes),
        ),
        compiler_params=pltpu.CompilerParams(vmem_limit_bytes=24 << 20),
        cost_estimate=pl.CostEstimate(
            flops=40 * half * width, bytes_accessed=4 << 20, transcendentals=half
        ),
    )(info, mid, d_own, got, *top, gain)


def leave_kernel(
    rows_ref, proj_ref, d_query_ref, d_pair_ref, got_ref, sums_two_ref,
    d_proj_ref, own_ref, peer_ref, sums_ref, bias_ref,
):
    pair = 2 * HEAD_DIM
    rows, local = d_query_ref.shape
    half = rows // 2
    d_proj_ref[:, :local] = d_query_ref[...]
    total = (d_pair_ref[...].astype(jnp.float32) + got_ref[...].astype(jnp.float32)).astype(
        jnp.bfloat16
    )
    for g in range(local // pair):
        for k in range(2):
            start = (k + 1) * local + g * pair
            d_proj_ref[:, start : start + pair] = total[:, (2 * g + k) * pair : (2 * g + k + 1) * pair]
    d_proj = d_proj_ref[...]
    bias_ref[...] = jnp.sum(d_proj.astype(jnp.float32), axis=0, keepdims=True)
    grad = dense_nt(d_proj, proj_ref[...])
    low = grad.astype(jnp.bfloat16)
    own_ref[...] = low[:half]
    peer_ref[...] = low[half:]
    normed, _ = row_stats(rows_ref[...].astype(jnp.float32))
    sums_ref[0:1, :] = jnp.sum(grad * normed, axis=0, keepdims=True)
    sums_ref[1:2, :] = jnp.sum(grad, axis=0, keepdims=True)
    sums_ref[2:5, :] = sums_two_ref[...]


def leave(rows_low, proj, d_query, d_pair, got, sums_two):
    rows, width = rows_low.shape
    columns = proj.shape[1]
    shapes = (
        low(rows, columns),
        low(rows // 2, width),
        low(rows // 2, width),
        full(5, width),
        full(1, columns),
    )
    args = (rows_low, proj, d_query, d_pair, got, sums_two)
    return call_once(leave_kernel, args, shapes, 2 * rows * width * columns)


def finish_kernel(rows_ref, own_ref, got_ref, gain_ref, d_mid_ref, first_ref, second_ref):
    half = rows_ref.shape[0]
    normed, root = row_stats(rows_ref[...].astype(jnp.float32))
    grad = own_ref[...].astype(jnp.float32) + got_ref[...].astype(jnp.float32)
    d_rows = row_pull(normed, root, grad * gain_ref[...].astype(jnp.float32)) + d_mid_ref[...]
    low = d_rows.astype(jnp.bfloat16)
    first_ref[...] = low[: half // 2]
    second_ref[...] = low[half // 2 :]


def finish(rows_low, own, got, gain, d_mid):
    half, width = own.shape
    top_half = pl.BlockSpec((half, width), lambda i: (0, 0))
    fixed = lambda a: pl.BlockSpec(a.shape, lambda i: (0,) * a.ndim)
    piece = jax.ShapeDtypeStruct((half // 2, width), jnp.bfloat16)
    return pl.pallas_call(
        finish_kernel,
        out_shape=(piece, piece),
        grid=(1,),
        in_specs=[top_half, fixed(own), fixed(got), fixed(gain), fixed(d_mid)],
        out_specs=(fixed(piece), fixed(piece)),
        compiler_params=pltpu.CompilerParams(vmem_limit_bytes=24 << 20),
        cost_estimate=pl.CostEstimate(
            flops=20 * half * width, bytes_accessed=4 << 20, transcendentals=half
        ),
    )(rows_low, own, got, gain, d_mid)


def weight_grad_kernel(*refs, counts):
    lefts, used = [], 0
    for count in counts:
        lefts.append((refs[used : used + count], refs[used + count]))
        used += count + 1
    own_ref, far_ref, send_ref = refs[used : used + 3]
    rows = own_ref.shape[0]
    mine = lax.axis_index("dp")
    targets = (own_ref, send_ref.at[:rows], far_ref, send_ref.at[rows:])
    start = 0
    for (pieces, right), turned in zip(lefts, refs[used + 3 :]):
        turned[...] = jnp.concatenate([piece[...] for piece in pieces], axis=0).T
        width = right.shape[1]
        for step, target in enumerate(targets):
            place = pl.multiple_of((mine ^ step) * rows, rows)
            grad = dense(turned[pl.ds(place, rows), :], right[...])
            target[:, start : start + width] = grad.astype(jnp.bfloat16)
        start += width


def split_bits(values):
    high = values.astype(jnp.bfloat16)
    return high, (values - high.astype(jnp.float32)).astype(jnp.bfloat16)


def weight_grad(*products):
    depth, width = products[0][-1].shape[0], products[0][0].shape[1]
    columns = sum(product[-1].shape[1] for product in products)
    rows = width // 4
    shapes = (low(rows, columns), low(rows, columns), low(2 * rows, columns))
    turned = [pltpu.VMEM((width, depth), jnp.bfloat16)] * len(products)
    kernel = functools.partial(
        weight_grad_kernel, counts=tuple(len(product) - 1 for product in products)
    )
    args = [array for product in products for array in product]
    return call_once(kernel, args, shapes, 2 * depth * width * columns, turned)


def add_terms(left, right):
    f32 = lambda value: value.astype(jnp.float32)
    half = left.shape[0] // 2
    total = f32(left[:half]) + f32(left[half:]) + (f32(right[:half]) + f32(right[half:]))
    return jnp.concatenate(split_bits(total), axis=0)


def merge_kernel(own_ref, far_ref, got_ref, mine_ref, theirs_ref, sum_ref, send_ref):
    rows = own_ref.shape[0]
    sum_ref[:rows, :] = own_ref[...] + got_ref[:rows, :]
    send_ref[:rows, :] = far_ref[...] + got_ref[rows:, :]
    terms = jnp.concatenate(split_bits(mine_ref[...] + theirs_ref[...]), axis=0)
    sum_ref[rows:, :] = terms
    send_ref[rows:, :] = terms


def merge(own, far, got, mine, theirs):
    rows, columns = own.shape
    packet = low(rows + 2 * mine.shape[0], columns)
    args = (own, far, got, mine, theirs)
    return call_once(merge_kernel, args, (packet, packet), own.size)


def spread_kernel(left_ref, right_ref, *outs, rows):
    plane = lax.axis_index("context")
    terms = add_terms(left_ref[rows:, :], right_ref[rows:, :])
    piece = rows // 4
    for step, out in enumerate(outs):
        start = pl.multiple_of((plane + step) % 4 * piece, piece)
        out[:piece, :] = left_ref[pl.ds(start, piece), :] + right_ref[pl.ds(start, piece), :]
        out[piece:, :] = terms


def spread(left, right, rows):
    piece = low(rows // 4 + left.shape[0] - rows, left.shape[1])
    kernel = functools.partial(spread_kernel, rows=rows)
    return call_once(kernel, (left, right), (piece,) * 4, left.size)


def total_kernel(*refs, piece):
    parts, (sum_ref, vectors_ref, held_ref) = refs[:4], refs[4:]
    plane = lax.axis_index("context")
    f32 = lambda value: value.astype(jnp.float32)
    total = f32(parts[0][:piece, :]) + f32(parts[1][:piece, :])
    total += f32(parts[2][:piece, :]) + f32(parts[3][:piece, :])
    sum_ref[...] = total.astype(jnp.bfloat16)
    count = vectors_ref.shape[0]
    for step, part in enumerate(parts):
        held_ref[(plane + 4 - step) % 4] = f32(part[piece : piece + count, :]) + f32(
            part[piece + count :, :]
        )
    vectors_ref[...] = held_ref[0] + held_ref[1] + held_ref[2] + held_ref[3]


def total(parts, piece, count):
    columns = parts[0].shape[1]
    shapes = (low(piece, columns), full(count, columns))
    held_terms = pltpu.VMEM((4, count, columns), jnp.float32)
    kernel = functools.partial(total_kernel, piece=piece)
    return call_once(kernel, parts, shapes, 4 * piece * columns, [held_terms])


def assemble_kernel(a, b, c, d, query_ref, key_ref, value_ref, out_ref, turned):
    plane = lax.axis_index("context")
    piece = a.shape[0]
    local = query_ref.shape[1]
    for step, part in enumerate((a, b, c, d)):
        start = pl.multiple_of((plane + 4 - step) % 4 * piece, piece)
        here = part[...].astype(jnp.float32)
        for k, ref in enumerate((query_ref, key_ref, value_ref, turned)):
            ref[pl.ds(start, piece), :] = here[:, k * local : (k + 1) * local]
    out_ref[...] = turned[...].T


def assemble(parts):
    piece, columns = parts[0].shape
    rows, local = 4 * piece, columns // 4
    shapes = (full(rows, local),) * 3 + (full(local, rows),)
    turned = pltpu.VMEM((rows, local), jnp.float32)
    return call_once(assemble_kernel, parts, shapes, 4 * piece * columns, [turned])


def vectors_kernel(up_ref, down_ref, proj_ref, mine_ref, theirs_ref, out_ref):
    width = down_ref.shape[1]
    sides = mine_ref[...] + theirs_ref[...]
    out_ref[...] = jnp.zeros_like(out_ref)
    out_ref[0:1, :] = up_ref[...]
    for k in range(2):
        out_ref[1 + k : 2 + k, :width] = sides[2 * k : 2 * k + 1]
        out_ref[1 + k : 2 + k, width:] = sides[2 * k + 1 : 2 * k + 2]
    out_ref[3:4, :width] = sides[4:5]
    out_ref[3:4, width:] = down_ref[...]
    out_ref[4:5, : proj_ref.shape[1]] = proj_ref[...]


def gather_vectors(up, down, proj, mine, theirs):
    args = (up, down, proj, mine, theirs)
    return call_once(vectors_kernel, args, (full(8, up.shape[1]),), up.size)[0]


def part_of(ref, index, count):
    start = index * count
    return ref[pl.ds(start if isinstance(start, int) else pl.multiple_of(start, count), count), :]


def cut_kernel(*refs, bits):
    plane = lax.axis_index("context")
    outs = refs[2 * len(bits) :]
    for k, bit in enumerate(bits):
        left, right = refs[2 * k], refs[2 * k + 1]
        index = plane % 2 if bit == 1 else plane // 2
        count = left.shape[0] // 2
        for out, half in ((outs[2 * k], index), (outs[2 * k + 1], 1 - index)):
            out[...] = part_of(left, half, count) + part_of(right, half, count)


def cut_sums(*pairs):
    args = [array for left, right, _ in pairs for array in (left, right)]
    shapes = [low(left.shape[0] // 2, left.shape[1]) for left, _, _ in pairs for _ in range(2)]
    kernel = functools.partial(cut_kernel, bits=tuple(bit for _, _, bit in pairs))
    return call_once(kernel, args, shapes, sum(a.size for a in args))


def glue_kernel(mine_ref, theirs_ref, left_ref, right_ref, glued_ref, sum_ref):
    second = lax.axis_index("context") // 2
    count = mine_ref.shape[0]
    for ref, index in ((mine_ref, second), (theirs_ref, 1 - second)):
        glued_ref[pl.ds(pl.multiple_of(index * count, count), count), :] = ref[...]
    sum_ref[...] = left_ref[...] + right_ref[...]


def glue_and_add(mine, theirs, left, right):
    shapes = (low(2 * mine.shape[0], mine.shape[1]), low(*left.shape))
    return call_once(glue_kernel, (mine, theirs, left, right), shapes, left.size)


def add_cut_kernel(a_ref, b_ref, left_ref, right_ref, sum_ref, keep_ref, send_ref):
    sum_ref[...] = a_ref[...] + b_ref[...]
    cut_kernel(left_ref, right_ref, keep_ref, send_ref, bits=(2,))


def add_and_cut(a, b, left, right):
    part = low(left.shape[0] // 2, left.shape[1])
    shapes = (low(*a.shape), part, part)
    return call_once(add_cut_kernel, (a, b, left, right), shapes, 2 * a.size)


def exchange(value, bit):
    size = lax.axis_size("dp")
    return lax.ppermute(value, "dp", [(i, i ^ bit) for i in range(size)])


def swap_tensor(value):
    return lax.ppermute(value, "tensor", [(0, 1), (1, 0)])


def together(*values):
    return lax.optimization_barrier(values)


def route(value, step, inward):
    pairs = []
    for far in range(2):
        for near in range(2):
            for plane in range(4):
                home = (2 * far + near) * 4 + plane
                away = (2 * far + plane // 2) * 4 + 2 * near + (step ^ (plane % 2))
                pairs.append((away, home) if inward else (home, away))
    return lax.ppermute(value, ("dp", "context"), pairs)


def pick_in(array, odd, upper):
    mine = jnp.where(upper, array[:, 1], array[:, 0])
    return [jnp.where(odd, mine[1 - step], mine[step]) for step in range(2)]


def join_out(near, far, odd, upper):
    arranged = [jnp.where(odd, jnp.stack(v[::-1]), jnp.stack(v)) for v in (near, far)]
    own, peer = arranged
    return jnp.where(upper, jnp.stack([peer, own], axis=1), jnp.stack([own, peer], axis=1))


def join_shares(mine, theirs, odd, upper):
    total = lambda a, b: a.astype(jnp.float32) + b[::-1].astype(jnp.float32)
    values = [total(a, b).astype(jnp.bfloat16) for a, b in zip(mine, theirs)]
    arranged = jnp.where(odd, jnp.stack(values[::-1]), jnp.stack(values))
    return jnp.where(upper, arranged[:, ::-1], arranged)


def gathered(shard, far_shard):
    return (shard, exchange(shard, 1), far_shard, exchange(far_shard, 1))


def turn_planes(value, step):
    return lax.ppermute(value, "context", [(i, (i + step) % 4) for i in range(4)])


def swap_planes(value, bit):
    return lax.ppermute(value, "context", [(i, i ^ bit) for i in range(4)])


def stack_rows(mine, theirs, second):
    return jnp.where(
        second, jnp.concatenate([theirs, mine], axis=0), jnp.concatenate([mine, theirs], axis=0)
    )


def per_device_planes(
    tokens,
    lengths,
    ln1_gain,
    ln1_bias,
    w_query,
    b_query,
    w_key,
    w_value,
    b_value,
    w_out,
    b_out,
    ln2_gain,
    ln2_bias,
    w_up,
    b_up,
    w_down,
    b_down,
    cotangent,
):
    block, width = tokens.shape[1:]
    half = block // 2
    local_width = w_query.shape[1]
    member = lax.axis_index("dp")
    near = member % 2
    plane = lax.axis_index("context")
    side = lax.axis_index("tensor")
    odd = plane % 2 == 1
    upper = side == 1
    upper_half = plane >= 2
    row = lambda vector: vector.reshape(1, -1)

    by_half = (2, 2, half, width)
    groups = local_width // (2 * HEAD_DIM)
    picked = pick_in(tokens.reshape(by_half), odd, upper)
    *picked, w_query, w_key, w_value = together(*picked, w_query, w_key, w_value)
    rows_parts = [route(picked[step], step, True) for step in range(2)]
    proj_own = jnp.concatenate([w_query, w_key, w_value], axis=1)
    proj_far = exchange(proj_own, 2)
    proj_near = exchange(proj_own, 1)
    out_own = w_out.T
    out_peer = swap_tensor(out_own)
    lengths_other = exchange(lengths, 1)
    down_own = w_down.T
    *rows_parts, proj_far, proj_near, out_peer, lengths_other, down_own, cotangent = together(
        *rows_parts, proj_far, proj_near, out_peer, lengths_other, down_own, cotangent
    )

    rows_parts += [swap_tensor(v) for v in rows_parts]
    proj_last = exchange(proj_far, 1)
    down_far = exchange(down_own, 2)
    pack_own = jnp.concatenate([w_up, out_own, out_peer], axis=1)
    top_picked = pick_in(cotangent.reshape(by_half), odd, upper)
    top_parts = [route(top_picked[step], step, True) for step in range(2)]
    *rows_parts, proj_last, down_far, pack_own, top_0, top_1 = together(
        *rows_parts, proj_last, down_far, pack_own, *top_parts
    )

    pack_far = exchange(pack_own, 2)
    top_parts = [top_0, top_1, swap_tensor(top_0), swap_tensor(top_1)]
    proj_blocks = (proj_own, proj_near, proj_far, proj_last)
    lengths_near = jnp.where(plane // 2 == near, lengths, lengths_other)
    length = jnp.where(odd, lengths_near[1], lengths_near[0])
    index = jnp.arange(9, dtype=jnp.int32)
    quarter = index % 4
    core = jnp.where(index < 4, near, 1 - near)
    piece = jnp.where(quarter < 2, side, 1 - side)
    starts = (2 * core + (quarter % 2 ^ plane % 2)) * block + piece * half
    info = jnp.where(index < 8, starts, length)
    rows_low, normed_low, queries, pair_own, proj = enter(
        rows_parts, row(ln1_gain), row(ln1_bias), row(b_query), row(b_value), proj_blocks
    )
    pair_other = exchange(pair_own, 1)
    mixed, logs = attend(info, queries, pair_own, pair_other)

    mixed, down_own, down_far, pack_own, *top_parts = together(
        mixed, down_own, down_far, pack_own, *top_parts
    )
    mixed_peer = swap_tensor(mixed)
    down_blocks = gathered(down_own, down_far)
    pack_near = exchange(pack_own, 1)
    mixed_peer, pack_near, pack_far, *down_blocks = together(
        mixed_peer, pack_near, pack_far, *down_blocks
    )
    pack_blocks = (pack_own, pack_near, pack_far, exchange(pack_far, 1))
    (
        middle,
        normed_two,
        d_feed,
        hidden,
        d_pre,
        d_own,
        d_peer,
        *shares,
        out_t,
        grad_up_bias,
        grad_down_bias,
    ) = middle_part(
        info,
        rows_low,
        mixed,
        mixed_peer,
        top_parts,
        row(ln2_gain),
        row(ln2_bias),
        row(b_out),
        pack_blocks,
        down_blocks,
        row(b_up),
        row(b_down),
    )

    got = swap_tensor(d_peer)
    down_own, down_far, down_send = weight_grad((d_feed, hidden))
    up_own, up_far, up_send = weight_grad((normed_two, d_pre))
    got, down_send, up_send, *shares = together(got, down_send, up_send, *shares)

    down_got = exchange(down_send, 1)
    d_middle, d_att, sums_two = turn(info, middle, d_own, got, top_parts[:2], row(ln2_gain))
    d_att, down_got, up_send, *shares = together(d_att, down_got, up_send, *shares)

    shard = down_own.shape[0]
    columns = hidden.shape[1]
    d_att_peer = swap_tensor(d_att)
    got_1 = exchange(down_far + down_got[shard:], 2)
    down_own = down_own + down_got[:shard]
    up_got = exchange(up_send, 1)
    share_0 = route(shares[0], 0, False)
    up_own, up_far = up_own + up_got[:shard], up_far + up_got[shard:]
    d_att_peer, got_1, up_own, up_far, share_0, share_1 = together(
        d_att_peer, got_1, up_own, up_far, share_0, shares[1]
    )

    half_1, sent = cut_sums((down_own, got_1, 1))
    got_1 = swap_planes(sent, 1)
    got_2 = exchange(up_far, 2)
    share_1 = route(share_1, 1, False)
    d_queries, d_pair, d_send = attend_back(
        info, queries, pair_own, pair_other, mixed, d_att, d_att_peer, out_t, logs
    )
    d_send, got_1, got_2, share_0, share_1 = together(d_send, got_1, got_2, share_0, share_1)


    d_got = exchange(d_send, 1)
    quarter_1, sent_1, half_2, sent_2 = cut_sums((half_1, got_1, 2), (up_own, got_2, 1))
    got_1 = swap_planes(sent_1, 2)
    got_2 = swap_planes(sent_2, 1)
    d_proj, one_own, one_peer, sides, proj_bias = leave(
        rows_low, proj, d_queries, d_pair, d_got, sums_two
    )
    own, far, send = weight_grad((normed_low, d_proj), (d_att, d_att_peer, mixed))
    share_got = [swap_tensor(share_0)]
    one_peer, sides, send, got_1, got_2, *share_got = together(
        one_peer, sides, send, got_1, got_2, *share_got
    )

    quarter_1, quarter_2, sent = add_and_cut(quarter_1, got_1, half_2, got_2)
    got_1 = swap_planes(quarter_1, 2)
    got_2 = swap_planes(sent, 2)
    sides_got = swap_tensor(sides)
    one_got = swap_tensor(one_peer)
    send_got = exchange(send, 1)
    send_got, one_got, got_1, got_2, sides_got = together(
        send_got, one_got, got_1, got_2, sides_got
    )

    vectors = gather_vectors(grad_up_bias, grad_down_bias, proj_bias, sides, sides_got)
    vectors_got = exchange(vectors, 1)
    input_rows = finish(rows_low, one_own, one_got, row(ln1_gain), d_middle)
    *input_rows, vectors_got, share_1 = together(*input_rows, vectors_got, share_1)

    packet, packet_far = merge(own, far, send_got, vectors, vectors_got)
    packet_got = exchange(packet_far, 2)
    share_got.append(swap_tensor(share_1))
    in_near = [route(input_rows[step], step, False) for step in range(2)]
    half_1, quarter_2 = glue_and_add(quarter_1, got_1, quarter_2, got_2)
    got_1 = swap_planes(half_1, 1)
    got_2 = swap_planes(quarter_2, 2)
    packet_got, got_1, got_2, *pieces = together(packet_got, got_1, got_2, *in_near, *share_got)
    in_near, share_got = pieces[:2], pieces[2:]

    quarters = spread(packet, packet_got, shard)
    arrived = [turn_planes(quarters[step], step) for step in range(1, 4)]
    in_far = [swap_tensor(v) for v in in_near]
    half_2 = stack_rows(quarter_2, got_2, upper_half)
    got_2 = swap_planes(half_2, 1)
    grad_down = stack_rows(half_1, got_1, odd).astype(jnp.float32).T
    output = join_shares((share_0, share_1), share_got, odd, upper)
    *pieces, got_2 = together(quarters[0], *arrived, *in_far, got_2)

    in_far = pieces[4:]
    quarter, vectors = total(pieces[:4], shard // 4, vectors.shape[0])
    quarters = [quarter] + [turn_planes(quarter, step) for step in range(1, 4)]
    input_grad = join_out(in_near, in_far, odd, upper)
    grad_up = stack_rows(half_2, got_2, odd).astype(jnp.float32)
    grad_query, grad_key, grad_value, grad_out = assemble(quarters)
    return (
        output.reshape(tokens.shape),
        input_grad.reshape(tokens.shape),
        vectors[1, :width],
        vectors[1, width:],
        grad_query,
        vectors[4, :local_width],
        grad_key,
        grad_value,
        vectors[4, 2 * local_width : 3 * local_width],
        grad_out,
        vectors[3, :width],
        vectors[2, :width],
        vectors[2, width:],
        grad_up,
        vectors[0],
        grad_down,
        vectors[3, width:],
    )


def pick(mesh):
    sizes = mesh.shape
    planes = sizes["dp"] == 4 and sizes["context"] == 4 and sizes["tensor"] == 2
    return per_device_planes if planes else per_device_general


def solution(mesh):
    return jax.shard_map(
        pick(mesh),
        mesh=mesh,
        in_specs=(
            P("dp", "context", None),
            P("dp"),
            P(),
            P(),
            P("dp", "tensor"),
            P("tensor"),
            P("dp", "tensor"),
            P("dp", "tensor"),
            P("tensor"),
            P("tensor", "dp"),
            P(),
            P(),
            P(),
            P("dp", "tensor"),
            P("tensor"),
            P("tensor", "dp"),
            P(),
            P("dp", "context", None),
        ),
        out_specs=(
            P("dp", "context", None),
            P("dp", "context", None),
            P(),
            P(),
            P("dp", "tensor"),
            P("tensor"),
            P("dp", "tensor"),
            P("dp", "tensor"),
            P("tensor"),
            P("tensor", "dp"),
            P(),
            P(),
            P(),
            P("dp", "tensor"),
            P("tensor"),
            P("tensor", "dp"),
            P(),
        ),
        check_vma=False,
    )
```

```python
import functools

import jax
import jax.numpy as jnp
from jax import lax
from jax.experimental import pallas as pl
from jax.experimental.pallas import tpu as pltpu
from jax.sharding import PartitionSpec as P

HEAD_DIM = 64


epsilon = 1e-06
masked_value = -1e30


def norm_rows(values, gain_vec, bias_vec):
    average = jnp.mean(values, axis=-1, keepdims=True)
    centred = values - average
    spread = jnp.mean(centred * centred, axis=-1, keepdims=True)
    return centred * lax.rsqrt(spread + epsilon) * gain_vec + bias_vec


def gelu_tanh(values):
    return jax.nn.gelu(values, approximate=True)


def dense(left, right):
    return jnp.dot(left, right, preferred_element_type=jnp.float32)


def dense_tn(left, right):
    return lax.dot_general(
        left, right, (((0,), (0,)), ((), ())), preferred_element_type=jnp.float32
    )


def dense_nt(left, right):
    return lax.dot_general(
        left, right, (((1,), (1,)), ((), ())), preferred_element_type=jnp.float32
    )


def per_device_general(
    tokens,
    lengths,
    ln1_gain,
    ln1_bias,
    w_query,
    b_query,
    w_key,
    w_value,
    b_value,
    w_out,
    b_out,
    ln2_gain,
    ln2_bias,
    w_up,
    b_up,
    w_down,
    b_down,
    cotangent,
):
    seq_count, shard_rows, width = tokens.shape
    full_len = shard_rows * lax.axis_size("context")
    local_width = w_query.shape[1]
    local_heads = local_width // HEAD_DIM
    scale = HEAD_DIM ** (-0.5)
    row_count = seq_count * shard_rows
    query_weight, key_weight, value_weight, up_weight, out_weight, down_weight = (
        lax.all_gather(w_query, "dp", axis=0, tiled=True),
        lax.all_gather(w_key, "dp", axis=0, tiled=True),
        lax.all_gather(w_value, "dp", axis=0, tiled=True),
        lax.all_gather(w_up, "dp", axis=0, tiled=True),
        lax.all_gather(w_out, "dp", axis=1, tiled=True),
        lax.all_gather(w_down, "dp", axis=1, tiled=True),
    )
    gain_one = ln1_gain.astype(jnp.float32)
    bias_one = ln1_bias.astype(jnp.float32)
    query_bias = b_query.astype(jnp.float32)
    value_bias = b_value.astype(jnp.float32)
    out_bias = b_out.astype(jnp.float32)
    gain_two = ln2_gain.astype(jnp.float32)
    bias_two = ln2_bias.astype(jnp.float32)
    up_bias = b_up.astype(jnp.float32)
    down_bias = b_down.astype(jnp.float32)
    places = lax.axis_index("context") * shard_rows + jnp.arange(shard_rows, dtype=jnp.int32)
    keep = (places[None, :] < lengths[:, None]).astype(jnp.float32).reshape(row_count, 1)
    key_places = jnp.arange(full_len, dtype=jnp.int32)
    rows_in = tokens.reshape(row_count, width).astype(jnp.float32)
    normed_one, pull_one = jax.vjp(norm_rows, rows_in, gain_one, bias_one)
    normed_low = normed_one.astype(jnp.bfloat16)
    queries = (dense(normed_low, query_weight) + query_bias).astype(jnp.bfloat16)
    keys_own = dense(normed_low, key_weight).astype(jnp.bfloat16)
    values_own = (dense(normed_low, value_weight) + value_bias).astype(jnp.bfloat16)
    keys_whole, values_whole = (
        lax.all_gather(
            keys_own.reshape(seq_count, shard_rows, local_width), "context", axis=1, tiled=True
        ),
        lax.all_gather(
            values_own.reshape(seq_count, shard_rows, local_width), "context", axis=1, tiled=True
        ),
    )
    query_heads = queries.reshape(seq_count, shard_rows, local_heads, HEAD_DIM)
    head_outs = []
    log_sums = []
    for member in range(seq_count):
        key_heads = keys_whole[member].reshape(full_len, local_heads, HEAD_DIM)
        value_heads = values_whole[member].reshape(full_len, local_heads, HEAD_DIM)
        raw_scores = (
            jnp.einsum(
                "qhd,khd->hqk", query_heads[member], key_heads, preferred_element_type=jnp.float32
            )
            * scale
        )
        live = (key_places < lengths[member])[None, None, :]
        masked = jnp.where(live, raw_scores, masked_value)
        largest = jnp.max(masked, axis=-1, keepdims=True)
        log_total = largest + jnp.log(jnp.sum(jnp.exp(masked - largest), axis=-1, keepdims=True))
        probs_low = jnp.exp(masked - log_total).astype(jnp.bfloat16)
        mixed_heads = jnp.einsum(
            "hqk,khd->qhd", probs_low, value_heads, preferred_element_type=jnp.float32
        )
        head_outs.append(mixed_heads.reshape(shard_rows, local_width))
        log_sums.append(log_total)
    context_low = jnp.concatenate(head_outs, axis=0).astype(jnp.bfloat16)
    attention = (
        lax.psum(dense(context_low, out_weight).astype(jnp.bfloat16), "tensor").astype(jnp.float32)
        + out_bias
    )
    middle = rows_in + keep * attention
    normed_two, pull_two = jax.vjp(norm_rows, middle, gain_two, bias_two)
    normed_two_low = normed_two.astype(jnp.bfloat16)
    hidden_pre = dense(normed_two_low, up_weight) + up_bias
    hidden, pull_gelu = jax.vjp(gelu_tanh, hidden_pre)
    hidden_low = hidden.astype(jnp.bfloat16)
    feed = (
        lax.psum(dense(hidden_low, down_weight).astype(jnp.bfloat16), "tensor").astype(jnp.float32)
        + down_bias
    )
    output = (middle + keep * feed).astype(jnp.bfloat16).reshape(tokens.shape)
    grad_top = cotangent.reshape(row_count, width).astype(jnp.float32)
    d_feed = (keep * grad_top).astype(jnp.bfloat16)
    grad_down_bias = jnp.sum(d_feed.astype(jnp.float32), axis=0)
    grad_down = dense_tn(hidden_low, d_feed)
    d_hidden = dense_nt(d_feed, down_weight)
    d_pre = pull_gelu(d_hidden)[0].astype(jnp.bfloat16)
    grad_up_bias = jnp.sum(d_pre.astype(jnp.float32), axis=0)
    grad_up = dense_tn(normed_two_low, d_pre)
    d_normed_two = lax.psum(dense_nt(d_pre, up_weight).astype(jnp.bfloat16), "tensor").astype(
        jnp.float32
    )
    d_middle, grad_gain_two, grad_bias_two = pull_two(d_normed_two)
    d_middle = d_middle + grad_top
    d_attention = (keep * d_middle).astype(jnp.bfloat16)
    grad_out_bias = jnp.sum(d_attention.astype(jnp.float32), axis=0)
    grad_out = dense_tn(context_low, d_attention)
    d_context = dense_nt(d_attention, out_weight).astype(jnp.bfloat16)
    back_keys, back_values = (keys_whole, values_whole)
    d_context_heads = d_context.reshape(seq_count, shard_rows, local_heads, HEAD_DIM)
    query_grads = []
    own_grads = []
    inner_rows = []
    for member in range(seq_count):
        key_heads = back_keys[member].reshape(full_len, local_heads, HEAD_DIM)
        value_heads = back_values[member].reshape(full_len, local_heads, HEAD_DIM)
        raw_scores = (
            jnp.einsum(
                "qhd,khd->hqk", query_heads[member], key_heads, preferred_element_type=jnp.float32
            )
            * scale
        )
        live = (key_places < lengths[member])[None, None, :]
        probs = jnp.where(live, jnp.exp(raw_scores - log_sums[member]), 0.0)
        d_probs = jnp.einsum(
            "qhd,khd->hqk", d_context_heads[member], value_heads, preferred_element_type=jnp.float32
        )
        inner = jnp.sum(probs * d_probs, axis=-1, keepdims=True)
        d_scores = (probs * (d_probs - inner)).astype(jnp.bfloat16)
        d_query = (
            jnp.einsum("hqk,khd->qhd", d_scores, key_heads, preferred_element_type=jnp.float32)
            * scale
        )
        query_grads.append(d_query.reshape(shard_rows, local_width))
        inner_rows.append(inner[:, :, 0])
        d_keys = (
            jnp.einsum(
                "hqk,qhd->khd", d_scores, query_heads[member], preferred_element_type=jnp.float32
            )
            * scale
        )
        d_values = jnp.einsum(
            "hqk,qhd->khd",
            probs.astype(jnp.bfloat16),
            d_context_heads[member],
            preferred_element_type=jnp.float32,
        )
        key_term = jnp.concatenate(
            [d_keys.reshape(full_len, local_width), d_values.reshape(full_len, local_width)], axis=1
        )
        own_grads.append(
            lax.psum_scatter(
                key_term.astype(jnp.bfloat16), "context", scatter_dimension=0, tiled=True
            ).astype(jnp.float32)
        )
    d_query_low = jnp.concatenate(query_grads, axis=0).astype(jnp.bfloat16)
    key_value_grads = jnp.concatenate(own_grads, axis=0)
    d_keys_low = key_value_grads[:, :local_width].astype(jnp.bfloat16)
    d_values_low = key_value_grads[:, local_width:].astype(jnp.bfloat16)
    grad_query = dense_tn(normed_low, d_query_low)
    grad_query_bias = jnp.sum(d_query_low.astype(jnp.float32), axis=0)
    grad_key = dense_tn(normed_low, d_keys_low)
    grad_value = dense_tn(normed_low, d_values_low)
    grad_value_bias = jnp.sum(d_values_low.astype(jnp.float32), axis=0)
    d_normed_one = lax.psum(
        (
            dense_nt(d_query_low, query_weight)
            + dense_nt(d_keys_low, key_weight)
            + dense_nt(d_values_low, value_weight)
        ).astype(jnp.bfloat16),
        "tensor",
    ).astype(jnp.float32)
    d_rows, grad_gain_one, grad_bias_one = pull_one(d_normed_one)
    input_grad = (d_rows + d_middle).astype(jnp.bfloat16).reshape(tokens.shape)
    data_sums = (
        lax.psum_scatter(
            grad_query.astype(jnp.bfloat16), "dp", scatter_dimension=0, tiled=True
        ).astype(jnp.float32),
        lax.psum_scatter(
            grad_key.astype(jnp.bfloat16), "dp", scatter_dimension=0, tiled=True
        ).astype(jnp.float32),
        lax.psum_scatter(
            grad_value.astype(jnp.bfloat16), "dp", scatter_dimension=0, tiled=True
        ).astype(jnp.float32),
        lax.psum_scatter(
            grad_up.astype(jnp.bfloat16), "dp", scatter_dimension=0, tiled=True
        ).astype(jnp.float32),
        lax.psum_scatter(
            grad_out.astype(jnp.bfloat16), "dp", scatter_dimension=1, tiled=True
        ).astype(jnp.float32),
        lax.psum_scatter(
            grad_down.astype(jnp.bfloat16), "dp", scatter_dimension=1, tiled=True
        ).astype(jnp.float32),
    )
    owned_sums = (
        lax.psum(data_sums[0].astype(jnp.bfloat16), "context").astype(jnp.float32),
        lax.psum(data_sums[1].astype(jnp.bfloat16), "context").astype(jnp.float32),
        lax.psum(data_sums[2].astype(jnp.bfloat16), "context").astype(jnp.float32),
        lax.psum(data_sums[3].astype(jnp.bfloat16), "context").astype(jnp.float32),
        lax.psum(data_sums[4].astype(jnp.bfloat16), "context").astype(jnp.float32),
        lax.psum(data_sums[5].astype(jnp.bfloat16), "context").astype(jnp.float32),
    )
    small_sums = lax.psum(
        (
            grad_gain_one,
            grad_bias_one,
            grad_query_bias,
            grad_value_bias,
            grad_out_bias,
            grad_gain_two,
            grad_bias_two,
            grad_up_bias,
            grad_down_bias,
        ),
        ("dp", "context"),
    )
    return (
        output,
        input_grad,
        small_sums[0],
        small_sums[1],
        owned_sums[0],
        small_sums[2],
        owned_sums[1],
        owned_sums[2],
        small_sums[3],
        owned_sums[4],
        small_sums[4],
        small_sums[5],
        small_sums[6],
        owned_sums[3],
        small_sums[7],
        owned_sums[5],
        small_sums[8],
    )


def live_bias(info, count):
    places = lax.broadcasted_iota(jnp.int32, (count, 2 * HEAD_DIM), 0)
    return jnp.concatenate(
        [jnp.where(info[k] + places < info[8], 0.0, masked_value) for k in range(8)], axis=0
    ).astype(jnp.bfloat16)


def split_pair(array, extra):
    lane = lax.broadcasted_iota(jnp.int32, array.shape, 1)
    zero = jnp.zeros((), jnp.bfloat16)
    left = jnp.where(lane < HEAD_DIM, array, jnp.where(lane == HEAD_DIM, extra, zero))
    right = jnp.where(lane >= HEAD_DIM, array, jnp.where(lane == 0, extra, zero))
    return left, right


LOG_SCALE = HEAD_DIM ** (-0.5) * 1.4426950408889634


def attend_kernel(info, query_ref, own_ref, other_ref, out_ref, log_ref):
    pair = 2 * HEAD_DIM
    count = query_ref.shape[0] // 4
    keys = jnp.concatenate([own_ref[:, :pair], other_ref[:, :pair]], axis=0)
    values = jnp.concatenate([own_ref[:, pair:], other_ref[:, pair:]], axis=0)
    values_t = values.T
    key_heads = split_pair(keys, live_bias(info, count))
    query_heads = split_pair(query_ref[...], jnp.ones((), jnp.bfloat16))
    mixed = []
    for head in range(2):
        scores = dense_nt(key_heads[head], query_heads[head])
        largest = jnp.max(scores, axis=0, keepdims=True)
        weights = jnp.exp2((scores - largest) * LOG_SCALE)
        total = jnp.sum(weights, axis=0, keepdims=True)
        dims = slice(head * HEAD_DIM, (head + 1) * HEAD_DIM)
        mixed.append(dense(values_t[dims], weights.astype(jnp.bfloat16)) / total)
        log_ref[0, head : head + 1, :] = largest * LOG_SCALE + jnp.log2(total)
    out_ref[...] = jnp.concatenate(mixed, axis=0).T.astype(jnp.bfloat16)


def attend(info, queries, pair_own, pair_other):
    rows, width = queries.shape
    pair = 2 * HEAD_DIM
    groups = width // pair
    work = 4 * rows * 2 * rows * width
    return pl.pallas_call(
        attend_kernel,
        out_shape=(
            jax.ShapeDtypeStruct((rows, width), jnp.bfloat16),
            jax.ShapeDtypeStruct((groups, 2, rows), jnp.float32),
        ),
        grid_spec=pltpu.PrefetchScalarGridSpec(
            num_scalar_prefetch=1,
            grid=(groups,),
            in_specs=[
                pl.BlockSpec((rows, pair), lambda g, info: (0, g)),
                pl.BlockSpec((rows, 2 * pair), lambda g, info: (0, g)),
                pl.BlockSpec((rows, 2 * pair), lambda g, info: (0, g)),
            ],
            out_specs=(
                pl.BlockSpec((rows, pair), lambda g, info: (0, g)),
                pl.BlockSpec((1, 2, rows), lambda g, info: (g, 0, 0)),
            ),
        ),
        compiler_params=pltpu.CompilerParams(vmem_limit_bytes=32 << 20),
        cost_estimate=pl.CostEstimate(
            flops=4 * work, bytes_accessed=12 * rows * width, transcendentals=work // (2 * HEAD_DIM)
        ),
    )(info, queries, pair_own, pair_other)


def attend_back_kernel(
    info,
    query_ref,
    own_ref,
    other_ref,
    out_ref,
    d_own_ref,
    d_peer_ref,
    proj_ref,
    log_ref,
    d_query_ref,
    d_pair_ref,
    d_other_ref,
):
    pair = 2 * HEAD_DIM
    rows = query_ref.shape[0]
    scale = HEAD_DIM ** (-0.5)
    keys = jnp.concatenate([own_ref[:, :pair], other_ref[:, :pair]], axis=0)
    values = jnp.concatenate([own_ref[:, pair:], other_ref[:, pair:]], axis=0)
    keys_t = keys.T
    key_heads = split_pair(keys, live_bias(info, rows // 4))
    value_heads = split_pair(values, jnp.zeros((), jnp.bfloat16))
    query = query_ref[...]
    query_heads = split_pair(query, jnp.ones((), jnp.bfloat16))
    d_att = jnp.concatenate([d_own_ref[...], d_peer_ref[...]], axis=0)
    grad = dense(d_att, proj_ref[...]).astype(jnp.bfloat16)
    inner_t = (grad.astype(jnp.float32) * out_ref[...].astype(jnp.float32)).T
    d_query, d_keys, d_values = [], [], []
    for head in range(2):
        dims = slice(head * HEAD_DIM, (head + 1) * HEAD_DIM)
        inner = jnp.sum(inner_t[dims], axis=0, keepdims=True)
        scores = dense_nt(key_heads[head], query_heads[head])
        probs = jnp.exp2(scores * LOG_SCALE - log_ref[0, head : head + 1, :])
        d_probs = dense_nt(value_heads[head], grad)
        d_scores = (probs * (d_probs - inner)).astype(jnp.bfloat16)
        d_query.append(dense(keys_t[dims], d_scores))
        d_keys.append(dense(d_scores, query))
        d_values.append(dense(probs.astype(jnp.bfloat16), grad))
    d_query_ref[...] = (jnp.concatenate(d_query, axis=0).T * scale).astype(jnp.bfloat16)
    left = lax.broadcasted_iota(jnp.int32, d_keys[0].shape, 1) < HEAD_DIM
    d_key = (jnp.where(left, d_keys[0], d_keys[1]) * scale).astype(jnp.bfloat16)
    d_value = jnp.where(left, d_values[0], d_values[1]).astype(jnp.bfloat16)
    d_pair_ref[:, :pair] = d_key[:rows]
    d_pair_ref[:, pair:] = d_value[:rows]
    d_other_ref[:, :pair] = d_key[rows:]
    d_other_ref[:, pair:] = d_value[rows:]


def attend_back(info, queries, pair_own, pair_other, mixed, d_own, d_peer, out_t, logs):
    rows, local = queries.shape
    width = out_t.shape[0]
    pair = 2 * HEAD_DIM
    work = 4 * rows * 2 * rows * local
    narrow = pl.BlockSpec((rows, pair), lambda g, info: (0, g))
    wide = pl.BlockSpec((rows, 2 * pair), lambda g, info: (0, g))
    halves = pl.BlockSpec((rows // 2, width), lambda g, info: (0, 0))
    return pl.pallas_call(
        attend_back_kernel,
        out_shape=tuple(
            jax.ShapeDtypeStruct((rows, columns), jnp.bfloat16)
            for columns in (local, 2 * local, 2 * local)
        ),
        grid_spec=pltpu.PrefetchScalarGridSpec(
            num_scalar_prefetch=1,
            grid=(local // pair,),
            in_specs=[
                narrow,
                wide,
                wide,
                narrow,
                halves,
                halves,
                pl.BlockSpec((width, pair), lambda g, info: (0, g)),
                pl.BlockSpec((1, 2, rows), lambda g, info: (g, 0, 0)),
            ],
            out_specs=(narrow, wide, wide),
        ),
        compiler_params=pltpu.CompilerParams(vmem_limit_bytes=32 << 20),
        cost_estimate=pl.CostEstimate(
            flops=10 * work, bytes_accessed=24 * rows * local, transcendentals=work // (2 * HEAD_DIM)
        ),
    )(info, queries, pair_own, pair_other, mixed, d_own, d_peer, out_t, logs)


def held(info, quarters, count, width):
    places = lax.broadcasted_iota(jnp.int32, (count, width), 0)
    return jnp.concatenate([info[k] + places < info[8] for k in range(quarters)], axis=0)


def fixed(array):
    return pl.BlockSpec(array.shape, lambda i: (0,) * len(array.shape))


def call_once(kernel, args, shapes, flops, scratch=()):
    moved = sum(a.size * a.dtype.itemsize for a in (*args, *shapes))
    return pl.pallas_call(
        kernel,
        out_shape=tuple(shapes),
        grid=(1,),
        in_specs=[fixed(a) for a in args],
        out_specs=tuple(fixed(s) for s in shapes),
        scratch_shapes=list(scratch),
        compiler_params=pltpu.CompilerParams(vmem_limit_bytes=24 << 20),
        cost_estimate=pl.CostEstimate(flops=flops, bytes_accessed=moved, transcendentals=0),
    )(*args)


def low(*shape):
    return jax.ShapeDtypeStruct(shape, jnp.bfloat16)


def full(*shape):
    return jax.ShapeDtypeStruct(shape, jnp.float32)


def row_stats(values):
    centred = values - jnp.mean(values, axis=-1, keepdims=True)
    spread = jnp.mean(centred * centred, axis=-1, keepdims=True)
    root = lax.rsqrt(spread + epsilon)
    return centred * root, root


def row_pull(normed, root, grad):
    return root * (
        grad
        - jnp.mean(grad, axis=-1, keepdims=True)
        - normed * jnp.mean(grad * normed, axis=-1, keepdims=True)
    )


def settle(parts, out_ref):
    rows = parts[0].shape[0]
    mine = lax.axis_index("dp")
    for step, part in enumerate(parts):
        start = pl.multiple_of((mine ^ step) * rows, rows)
        out_ref[pl.ds(start, rows), :] = part[...]


def enter_kernel(
    own0, own1, peer0, peer1, gain_ref, bias_ref, q_bias_ref, v_bias_ref, a, b, c, d,
    rows_ref, normed_ref, query_ref, pair_ref, proj_ref,
):
    pair = 2 * HEAD_DIM
    settle((a, b, c, d), proj_ref)
    rows = jnp.concatenate([own0[...], own1[...], peer0[...], peer1[...]], axis=0)
    rows_ref[...] = rows
    normed, _ = row_stats(rows.astype(jnp.float32))
    normed = normed * gain_ref[...].astype(jnp.float32) + bias_ref[...].astype(jnp.float32)
    normed = normed.astype(jnp.bfloat16)
    normed_ref[...] = normed
    local = query_ref.shape[1]
    mixed = dense(normed, proj_ref[...])
    query_ref[...] = (mixed[:, :local] + q_bias_ref[...].astype(jnp.float32)).astype(jnp.bfloat16)
    for g in range(local // pair):
        cols = slice(g * pair, (g + 1) * pair)
        key = mixed[:, local + g * pair : local + (g + 1) * pair]
        value = mixed[:, 2 * local + g * pair : 2 * local + (g + 1) * pair]
        value = value + v_bias_ref[:, cols].astype(jnp.float32)
        pair_ref[:, 2 * g * pair : (2 * g + 1) * pair] = key.astype(jnp.bfloat16)
        pair_ref[:, (2 * g + 1) * pair : (2 * g + 2) * pair] = value.astype(jnp.bfloat16)


def enter(pieces, gain, bias, q_bias, v_bias, blocks):
    half, width = pieces[0].shape
    rows = 4 * half
    local = q_bias.shape[1]
    shapes = (
        low(rows, width),
        low(rows, width),
        low(rows, local),
        low(rows, 2 * local),
        low(width, 3 * local),
    )
    args = (*pieces, gain, bias, q_bias, v_bias, *blocks)
    return call_once(enter_kernel, args, shapes, 6 * rows * width * local)


ROOT_TWO_OVER_PI = 0.7978845608028654
CUBE = 0.044715


def fetch(parts, columns, out_ref, sems):
    rows = parts[0].shape[0]
    mine = lax.axis_index("dp")
    copies = []
    for step, part in enumerate(parts):
        start = pl.multiple_of((mine ^ step) * rows, rows)
        copy = pltpu.make_async_copy(
            part.at[:, columns], out_ref.at[pl.ds(start, rows)], sems.at[step]
        )
        copy.start()
        copies.append(copy)
    return copies


def middle_kernel(
    info, rows_ref, own_ref, peer_ref, top0, top1, top2, top3, gain_ref, bias_ref, out_bias_ref,
    up_bias_ref, down_bias_ref, pa, pb, pc, pd, da, db, dc, dd,
    mid_ref, normed_ref, feed_ref, hidden_ref, d_pre_ref, d_own_ref, d_peer_ref,
    part0_ref, part1_ref, out_ref, g_up_ref, g_down_ref,
    outs, ups, downs, whole_mid, sent, sems,
):
    rows, width = rows_ref.shape
    half = rows // 2
    local = own_ref.shape[1]
    hidden_width = up_bias_ref.shape[1]
    steps = ups.shape[0]
    tile = hidden_width // steps
    packs, lasts = (pa, pb, pc, pd), (da, db, dc, dd)
    waits = [fetch(packs, pl.ds(hidden_width, width), outs, sems.at[0])]
    for s in range(steps):
        columns = pl.ds(s * tile, tile)
        waits.append(fetch(packs, columns, ups.at[s], sems.at[1 + 2 * s]))
        waits.append(fetch(lasts, columns, downs.at[s], sems.at[2 + 2 * s]))

    real = held(info, 4, rows // 4, width)
    top = jnp.concatenate([top0[...], top1[...], top2[...], top3[...]], axis=0)
    feed = jnp.where(real, top.astype(jnp.float32), 0.0)
    feed_ref[...] = feed.astype(jnp.bfloat16)
    g_down_ref[...] = jnp.sum(feed, axis=0, keepdims=True)
    peer = jnp.concatenate([peer_ref[half:, :], peer_ref[:half, :]], axis=0)
    for copy in waits[0]:
        copy.wait()
    out_ref[...] = outs[:, :local]
    attention = (
        dense_nt(own_ref[...], outs[:, :local])
        + dense_nt(peer, outs[:, local:])
        + out_bias_ref[...].astype(jnp.float32)
    )
    mid = rows_ref[...].astype(jnp.float32) + jnp.where(real, attention, 0.0)
    mid_ref[...] = mid[:half]
    whole_mid[...] = mid
    normed, _ = row_stats(mid)
    normed = normed * gain_ref[...].astype(jnp.float32) + bias_ref[...].astype(jnp.float32)
    normed_ref[...] = normed.astype(jnp.bfloat16)

    for s in range(steps):
        columns = slice(s * tile, (s + 1) * tile)
        for copy in waits[1 + 2 * s] + waits[2 + 2 * s]:
            copy.wait()
        pre = dense(normed_ref[...], ups[s]) + up_bias_ref[:, columns].astype(jnp.float32)
        d_hidden = dense(feed_ref[...], downs[s])
        square = pre * pre
        bend = jnp.tanh(pre * (ROOT_TWO_OVER_PI + CUBE * ROOT_TWO_OVER_PI * square))
        half_up = 0.5 + 0.5 * bend
        active = pre * half_up
        slope = half_up + active * (1.0 - bend) * (
            ROOT_TWO_OVER_PI + 3.0 * CUBE * ROOT_TWO_OVER_PI * square
        )
        hidden_ref[:, columns] = active.astype(jnp.bfloat16)
        d_pre = (d_hidden * slope).astype(jnp.bfloat16)
        d_pre_ref[:, columns] = d_pre
        g_up_ref[:, columns] = jnp.sum(d_pre.astype(jnp.float32), axis=0, keepdims=True)

    def back(left_ref, right_ref):
        total = 0.0
        for s in range(steps):
            total += dense_nt(left_ref[:, s * tile : (s + 1) * tile], right_ref[s])
        return total

    grad = back(d_pre_ref, ups).astype(jnp.bfloat16)
    d_own_ref[...] = grad[:half]
    sent[...] = grad[half:]
    leaving = pltpu.make_async_copy(sent, d_peer_ref, sems.at[0, 0])
    leaving.start()
    first = lax.axis_index("tensor") == 0
    share = back(hidden_ref, downs)
    share += jnp.where(first, down_bias_ref[...].astype(jnp.float32), 0.0)
    share = jnp.where(real, share, 0.0) + jnp.where(first, whole_mid[...], 0.0)
    share = share.astype(jnp.bfloat16)
    for k, part in enumerate((part0_ref, part1_ref)):
        start = k * (half // 2)
        part[0] = share[start : start + half // 2]
        part[1] = share[half + start : half + start + half // 2]
    leaving.wait()


def middle_part(
    info, rows_low, own, peer, top, gain, bias, out_bias, packs, downs, up_bias, down_bias
):
    rows, width = rows_low.shape
    local = own.shape[1]
    hidden = up_bias.shape[1]
    steps = 2
    small = (rows_low, own, peer, *top, gain, bias, out_bias, up_bias, down_bias)
    inside = pl.BlockSpec(memory_space=pltpu.VMEM)
    outside = pl.BlockSpec(memory_space=pltpu.HBM)
    shapes = (
        full(rows // 2, width),
        low(rows, width),
        low(rows, width),
        low(rows, hidden),
        low(rows, hidden),
        low(rows // 2, width),
        low(rows // 2, width),
        low(2, rows // 4, width),
        low(2, rows // 4, width),
        low(width, local),
        full(1, hidden),
        full(1, width),
    )
    return pl.pallas_call(
        middle_kernel,
        out_shape=shapes,
        in_specs=[pl.BlockSpec(memory_space=pltpu.SMEM)]
        + [inside] * len(small)
        + [pl.BlockSpec(memory_space=pltpu.HBM)] * 8,
        out_specs=tuple(outside if k == 6 else inside for k in range(len(shapes))),
        scratch_shapes=[
            pltpu.VMEM((width, width), jnp.bfloat16),
            pltpu.VMEM((steps, width, hidden // steps), jnp.bfloat16),
            pltpu.VMEM((steps, width, hidden // steps), jnp.bfloat16),
            pltpu.VMEM((rows, width), jnp.float32),
            pltpu.VMEM((rows // 2, width), jnp.bfloat16),
            pltpu.SemaphoreType.DMA((1 + 2 * steps, 4)),
        ],
        compiler_params=pltpu.CompilerParams(vmem_limit_bytes=36 << 20),
        cost_estimate=pl.CostEstimate(
            flops=8 * rows * width * hidden, bytes_accessed=20 << 20, transcendentals=rows * hidden
        ),
    )(info, *small, *packs, *downs)


def turn_kernel(
    info, mid_ref, d_own_ref, got_ref, top0, top1, gain_ref, d_mid_ref, d_att_ref, sums_ref
):
    half, width = d_own_ref.shape
    grad = d_own_ref[...].astype(jnp.float32) + got_ref[...].astype(jnp.float32)
    normed, root = row_stats(mid_ref[...])
    top = jnp.concatenate([top0[...], top1[...]], axis=0).astype(jnp.float32)
    d_mid = top + row_pull(normed, root, grad * gain_ref[...].astype(jnp.float32))
    d_mid_ref[...] = d_mid
    d_att = jnp.where(held(info, 2, half // 2, width), d_mid, 0.0).astype(jnp.bfloat16)
    d_att_ref[...] = d_att
    sums_ref[0:1, :] = jnp.sum(grad * normed, axis=0, keepdims=True)
    sums_ref[1:2, :] = jnp.sum(grad, axis=0, keepdims=True)
    sums_ref[2:3, :] = jnp.sum(d_att.astype(jnp.float32), axis=0, keepdims=True)


def turn(info, mid, d_own, got, top, gain):
    half, width = d_own.shape
    fixed = lambda a: pl.BlockSpec(a.shape, lambda i, info: (0,) * len(a.shape))
    first = pl.BlockSpec((half, width), lambda i, info: (0, 0))
    shapes = (
        jax.ShapeDtypeStruct((half, width), jnp.float32),
        jax.ShapeDtypeStruct((half, width), jnp.bfloat16),
        jax.ShapeDtypeStruct((3, width), jnp.float32),
    )
    return pl.pallas_call(
        turn_kernel,
        out_shape=shapes,
        grid_spec=pltpu.PrefetchScalarGridSpec(
            num_scalar_prefetch=1,
            grid=(1,),
            in_specs=[first, fixed(d_own), fixed(got), fixed(top[0]), fixed(top[1]), fixed(gain)],
            out_specs=tuple(fixed(s) for s in shapes),
        ),
        compiler_params=pltpu.CompilerParams(vmem_limit_bytes=24 << 20),
        cost_estimate=pl.CostEstimate(
            flops=40 * half * width, bytes_accessed=4 << 20, transcendentals=half
        ),
    )(info, mid, d_own, got, *top, gain)


def leave_kernel(
    rows_ref, proj_ref, d_query_ref, d_pair_ref, got_ref, sums_two_ref,
    d_proj_ref, own_ref, peer_ref, sums_ref, bias_ref,
):
    pair = 2 * HEAD_DIM
    rows, local = d_query_ref.shape
    half = rows // 2
    d_proj_ref[:, :local] = d_query_ref[...]
    total = (d_pair_ref[...].astype(jnp.float32) + got_ref[...].astype(jnp.float32)).astype(
        jnp.bfloat16
    )
    for g in range(local // pair):
        for k in range(2):
            start = (k + 1) * local + g * pair
            d_proj_ref[:, start : start + pair] = total[:, (2 * g + k) * pair : (2 * g + k + 1) * pair]
    d_proj = d_proj_ref[...]
    bias_ref[...] = jnp.sum(d_proj.astype(jnp.float32), axis=0, keepdims=True)
    grad = dense_nt(d_proj, proj_ref[...])
    low = grad.astype(jnp.bfloat16)
    own_ref[...] = low[:half]
    peer_ref[...] = low[half:]
    normed, _ = row_stats(rows_ref[...].astype(jnp.float32))
    sums_ref[0:1, :] = jnp.sum(grad * normed, axis=0, keepdims=True)
    sums_ref[1:2, :] = jnp.sum(grad, axis=0, keepdims=True)
    sums_ref[2:5, :] = sums_two_ref[...]


def leave(rows_low, proj, d_query, d_pair, got, sums_two):
    rows, width = rows_low.shape
    columns = proj.shape[1]
    shapes = (
        low(rows, columns),
        low(rows // 2, width),
        low(rows // 2, width),
        full(5, width),
        full(1, columns),
    )
    args = (rows_low, proj, d_query, d_pair, got, sums_two)
    return call_once(leave_kernel, args, shapes, 2 * rows * width * columns)


def finish_kernel(rows_ref, own_ref, got_ref, gain_ref, d_mid_ref, first_ref, second_ref):
    half = rows_ref.shape[0]
    normed, root = row_stats(rows_ref[...].astype(jnp.float32))
    grad = own_ref[...].astype(jnp.float32) + got_ref[...].astype(jnp.float32)
    d_rows = row_pull(normed, root, grad * gain_ref[...].astype(jnp.float32)) + d_mid_ref[...]
    low = d_rows.astype(jnp.bfloat16)
    first_ref[...] = low[: half // 2]
    second_ref[...] = low[half // 2 :]


def finish(rows_low, own, got, gain, d_mid):
    half, width = own.shape
    top_half = pl.BlockSpec((half, width), lambda i: (0, 0))
    fixed = lambda a: pl.BlockSpec(a.shape, lambda i: (0,) * a.ndim)
    piece = jax.ShapeDtypeStruct((half // 2, width), jnp.bfloat16)
    return pl.pallas_call(
        finish_kernel,
        out_shape=(piece, piece),
        grid=(1,),
        in_specs=[top_half, fixed(own), fixed(got), fixed(gain), fixed(d_mid)],
        out_specs=(fixed(piece), fixed(piece)),
        compiler_params=pltpu.CompilerParams(vmem_limit_bytes=24 << 20),
        cost_estimate=pl.CostEstimate(
            flops=20 * half * width, bytes_accessed=4 << 20, transcendentals=half
        ),
    )(rows_low, own, got, gain, d_mid)


def weight_grad_kernel(*refs, counts):
    lefts, used = [], 0
    for count in counts:
        lefts.append((refs[used : used + count], refs[used + count]))
        used += count + 1
    own_ref, far_ref, send_ref = refs[used : used + 3]
    rows = own_ref.shape[0]
    mine = lax.axis_index("dp")
    targets = (own_ref, send_ref.at[:rows], far_ref, send_ref.at[rows:])
    start = 0
    for (pieces, right), turned in zip(lefts, refs[used + 3 :]):
        turned[...] = jnp.concatenate([piece[...] for piece in pieces], axis=0).T
        width = right.shape[1]
        for step, target in enumerate(targets):
            place = pl.multiple_of((mine ^ step) * rows, rows)
            grad = dense(turned[pl.ds(place, rows), :], right[...])
            target[:, start : start + width] = grad.astype(jnp.bfloat16)
        start += width


def split_bits(values):
    high = values.astype(jnp.bfloat16)
    return high, (values - high.astype(jnp.float32)).astype(jnp.bfloat16)


def weight_grad(*products):
    depth, width = products[0][-1].shape[0], products[0][0].shape[1]
    columns = sum(product[-1].shape[1] for product in products)
    rows = width // 4
    shapes = (low(rows, columns), low(rows, columns), low(2 * rows, columns))
    turned = [pltpu.VMEM((width, depth), jnp.bfloat16)] * len(products)
    kernel = functools.partial(
        weight_grad_kernel, counts=tuple(len(product) - 1 for product in products)
    )
    args = [array for product in products for array in product]
    return call_once(kernel, args, shapes, 2 * depth * width * columns, turned)


def add_terms(left, right):
    f32 = lambda value: value.astype(jnp.float32)
    half = left.shape[0] // 2
    total = f32(left[:half]) + f32(left[half:]) + (f32(right[:half]) + f32(right[half:]))
    return jnp.concatenate(split_bits(total), axis=0)


def merge_kernel(own_ref, far_ref, got_ref, mine_ref, theirs_ref, sum_ref, send_ref):
    rows = own_ref.shape[0]
    sum_ref[:rows, :] = own_ref[...] + got_ref[:rows, :]
    send_ref[:rows, :] = far_ref[...] + got_ref[rows:, :]
    terms = jnp.concatenate(split_bits(mine_ref[...] + theirs_ref[...]), axis=0)
    sum_ref[rows:, :] = terms
    send_ref[rows:, :] = terms


def merge(own, far, got, mine, theirs):
    rows, columns = own.shape
    packet = low(rows + 2 * mine.shape[0], columns)
    args = (own, far, got, mine, theirs)
    return call_once(merge_kernel, args, (packet, packet), own.size)


def spread_kernel(left_ref, right_ref, *outs, rows):
    plane = lax.axis_index("context")
    terms = add_terms(left_ref[rows:, :], right_ref[rows:, :])
    piece = rows // 4
    for step, out in enumerate(outs):
        start = pl.multiple_of((plane + step) % 4 * piece, piece)
        out[:piece, :] = left_ref[pl.ds(start, piece), :] + right_ref[pl.ds(start, piece), :]
        out[piece:, :] = terms


def spread(left, right, rows):
    piece = low(rows // 4 + left.shape[0] - rows, left.shape[1])
    kernel = functools.partial(spread_kernel, rows=rows)
    return call_once(kernel, (left, right), (piece,) * 4, left.size)


def total_kernel(*refs, piece):
    parts, (sum_ref, vectors_ref, held_ref) = refs[:4], refs[4:]
    plane = lax.axis_index("context")
    f32 = lambda value: value.astype(jnp.float32)
    total = f32(parts[0][:piece, :]) + f32(parts[1][:piece, :])
    total += f32(parts[2][:piece, :]) + f32(parts[3][:piece, :])
    sum_ref[...] = total.astype(jnp.bfloat16)
    count = vectors_ref.shape[0]
    for step, part in enumerate(parts):
        held_ref[(plane + 4 - step) % 4] = f32(part[piece : piece + count, :]) + f32(
            part[piece + count :, :]
        )
    vectors_ref[...] = held_ref[0] + held_ref[1] + held_ref[2] + held_ref[3]


def total(parts, piece, count):
    columns = parts[0].shape[1]
    shapes = (low(piece, columns), full(count, columns))
    held_terms = pltpu.VMEM((4, count, columns), jnp.float32)
    kernel = functools.partial(total_kernel, piece=piece)
    return call_once(kernel, parts, shapes, 4 * piece * columns, [held_terms])


def assemble_kernel(a, b, c, d, query_ref, key_ref, value_ref, out_ref, turned):
    plane = lax.axis_index("context")
    piece = a.shape[0]
    local = query_ref.shape[1]
    for step, part in enumerate((a, b, c, d)):
        start = pl.multiple_of((plane + 4 - step) % 4 * piece, piece)
        here = part[...].astype(jnp.float32)
        for k, ref in enumerate((query_ref, key_ref, value_ref, turned)):
            ref[pl.ds(start, piece), :] = here[:, k * local : (k + 1) * local]
    out_ref[...] = turned[...].T


def assemble(parts):
    piece, columns = parts[0].shape
    rows, local = 4 * piece, columns // 4
    shapes = (full(rows, local),) * 3 + (full(local, rows),)
    turned = pltpu.VMEM((rows, local), jnp.float32)
    return call_once(assemble_kernel, parts, shapes, 4 * piece * columns, [turned])


def vectors_kernel(up_ref, down_ref, proj_ref, mine_ref, theirs_ref, out_ref):
    width = down_ref.shape[1]
    sides = mine_ref[...] + theirs_ref[...]
    out_ref[...] = jnp.zeros_like(out_ref)
    out_ref[0:1, :] = up_ref[...]
    for k in range(2):
        out_ref[1 + k : 2 + k, :width] = sides[2 * k : 2 * k + 1]
        out_ref[1 + k : 2 + k, width:] = sides[2 * k + 1 : 2 * k + 2]
    out_ref[3:4, :width] = sides[4:5]
    out_ref[3:4, width:] = down_ref[...]
    out_ref[4:5, : proj_ref.shape[1]] = proj_ref[...]


def gather_vectors(up, down, proj, mine, theirs):
    args = (up, down, proj, mine, theirs)
    return call_once(vectors_kernel, args, (full(8, up.shape[1]),), up.size)[0]


def part_of(ref, index, count):
    start = index * count
    return ref[pl.ds(start if isinstance(start, int) else pl.multiple_of(start, count), count), :]


def cut_kernel(*refs, bits):
    plane = lax.axis_index("context")
    outs = refs[2 * len(bits) :]
    for k, bit in enumerate(bits):
        left, right = refs[2 * k], refs[2 * k + 1]
        index = plane % 2 if bit == 1 else plane // 2
        count = left.shape[0] // 2
        for out, half in ((outs[2 * k], index), (outs[2 * k + 1], 1 - index)):
            out[...] = part_of(left, half, count) + part_of(right, half, count)


def cut_sums(*pairs):
    args = [array for left, right, _ in pairs for array in (left, right)]
    shapes = [low(left.shape[0] // 2, left.shape[1]) for left, _, _ in pairs for _ in range(2)]
    kernel = functools.partial(cut_kernel, bits=tuple(bit for _, _, bit in pairs))
    return call_once(kernel, args, shapes, sum(a.size for a in args))


def glue_kernel(mine_ref, theirs_ref, left_ref, right_ref, glued_ref, sum_ref):
    second = lax.axis_index("context") // 2
    count = mine_ref.shape[0]
    for ref, index in ((mine_ref, second), (theirs_ref, 1 - second)):
        glued_ref[pl.ds(pl.multiple_of(index * count, count), count), :] = ref[...]
    sum_ref[...] = left_ref[...] + right_ref[...]


def glue_and_add(mine, theirs, left, right):
    shapes = (low(2 * mine.shape[0], mine.shape[1]), low(*left.shape))
    return call_once(glue_kernel, (mine, theirs, left, right), shapes, left.size)


def add_cut_kernel(a_ref, b_ref, left_ref, right_ref, sum_ref, keep_ref, send_ref):
    sum_ref[...] = a_ref[...] + b_ref[...]
    cut_kernel(left_ref, right_ref, keep_ref, send_ref, bits=(2,))


def add_and_cut(a, b, left, right):
    part = low(left.shape[0] // 2, left.shape[1])
    shapes = (low(*a.shape), part, part)
    return call_once(add_cut_kernel, (a, b, left, right), shapes, 2 * a.size)


def exchange(value, bit):
    size = lax.axis_size("dp")
    return lax.ppermute(value, "dp", [(i, i ^ bit) for i in range(size)])


def swap_tensor(value):
    return lax.ppermute(value, "tensor", [(0, 1), (1, 0)])


def together(*values):
    return lax.optimization_barrier(values)


def route(value, step, inward):
    pairs = []
    for far in range(2):
        for near in range(2):
            for plane in range(4):
                home = (2 * far + near) * 4 + plane
                away = (2 * far + plane // 2) * 4 + 2 * near + (step ^ (plane % 2))
                pairs.append((away, home) if inward else (home, away))
    return lax.ppermute(value, ("dp", "context"), pairs)


def pick_in(array, odd, upper):
    mine = jnp.where(upper, array[:, 1], array[:, 0])
    return [jnp.where(odd, mine[1 - step], mine[step]) for step in range(2)]


def join_out(near, far, odd, upper):
    arranged = [jnp.where(odd, jnp.stack(v[::-1]), jnp.stack(v)) for v in (near, far)]
    own, peer = arranged
    return jnp.where(upper, jnp.stack([peer, own], axis=1), jnp.stack([own, peer], axis=1))


def join_shares(mine, theirs, odd, upper):
    total = lambda a, b: a.astype(jnp.float32) + b[::-1].astype(jnp.float32)
    values = [total(a, b).astype(jnp.bfloat16) for a, b in zip(mine, theirs)]
    arranged = jnp.where(odd, jnp.stack(values[::-1]), jnp.stack(values))
    return jnp.where(upper, arranged[:, ::-1], arranged)


def gathered(shard, far_shard):
    return (shard, exchange(shard, 1), far_shard, exchange(far_shard, 1))


def turn_planes(value, step):
    return lax.ppermute(value, "context", [(i, (i + step) % 4) for i in range(4)])


def swap_planes(value, bit):
    return lax.ppermute(value, "context", [(i, i ^ bit) for i in range(4)])


def stack_rows(mine, theirs, second):
    return jnp.where(
        second, jnp.concatenate([theirs, mine], axis=0), jnp.concatenate([mine, theirs], axis=0)
    )


def per_device_planes(
    tokens,
    lengths,
    ln1_gain,
    ln1_bias,
    w_query,
    b_query,
    w_key,
    w_value,
    b_value,
    w_out,
    b_out,
    ln2_gain,
    ln2_bias,
    w_up,
    b_up,
    w_down,
    b_down,
    cotangent,
):
    block, width = tokens.shape[1:]
    half = block // 2
    local_width = w_query.shape[1]
    member = lax.axis_index("dp")
    near = member % 2
    plane = lax.axis_index("context")
    side = lax.axis_index("tensor")
    odd = plane % 2 == 1
    upper = side == 1
    upper_half = plane >= 2
    row = lambda vector: vector.reshape(1, -1)

    by_half = (2, 2, half, width)
    groups = local_width // (2 * HEAD_DIM)
    picked = pick_in(tokens.reshape(by_half), odd, upper)
    *picked, w_query, w_key, w_value = together(*picked, w_query, w_key, w_value)
    rows_parts = [route(picked[step], step, True) for step in range(2)]
    proj_own = jnp.concatenate([w_query, w_key, w_value], axis=1)
    proj_far = exchange(proj_own, 2)
    proj_near = exchange(proj_own, 1)
    out_own = w_out.T
    out_peer = swap_tensor(out_own)
    lengths_other = exchange(lengths, 1)
    down_own = w_down.T
    *rows_parts, proj_far, proj_near, out_peer, lengths_other, down_own, cotangent = together(
        *rows_parts, proj_far, proj_near, out_peer, lengths_other, down_own, cotangent
    )

    rows_parts += [swap_tensor(v) for v in rows_parts]
    proj_last = exchange(proj_far, 1)
    down_far = exchange(down_own, 2)
    pack_own = jnp.concatenate([w_up, out_own, out_peer], axis=1)
    top_picked = pick_in(cotangent.reshape(by_half), odd, upper)
    top_parts = [route(top_picked[step], step, True) for step in range(2)]
    *rows_parts, proj_last, down_far, pack_own, top_0, top_1 = together(
        *rows_parts, proj_last, down_far, pack_own, *top_parts
    )

    pack_far = exchange(pack_own, 2)
    top_parts = [top_0, top_1, swap_tensor(top_0), swap_tensor(top_1)]
    proj_blocks = (proj_own, proj_near, proj_far, proj_last)
    lengths_near = jnp.where(plane // 2 == near, lengths, lengths_other)
    length = jnp.where(odd, lengths_near[1], lengths_near[0])
    index = jnp.arange(9, dtype=jnp.int32)
    quarter = index % 4
    core = jnp.where(index < 4, near, 1 - near)
    piece = jnp.where(quarter < 2, side, 1 - side)
    starts = (2 * core + (quarter % 2 ^ plane % 2)) * block + piece * half
    info = jnp.where(index < 8, starts, length)
    rows_low, normed_low, queries, pair_own, proj = enter(
        rows_parts, row(ln1_gain), row(ln1_bias), row(b_query), row(b_value), proj_blocks
    )
    pair_other = exchange(pair_own, 1)
    mixed, logs = attend(info, queries, pair_own, pair_other)

    mixed, down_own, down_far, pack_own, *top_parts = together(
        mixed, down_own, down_far, pack_own, *top_parts
    )
    mixed_peer = swap_tensor(mixed)
    down_blocks = gathered(down_own, down_far)
    pack_near = exchange(pack_own, 1)
    mixed_peer, pack_near, pack_far, *down_blocks = together(
        mixed_peer, pack_near, pack_far, *down_blocks
    )
    pack_blocks = (pack_own, pack_near, pack_far, exchange(pack_far, 1))
    (
        middle,
        normed_two,
        d_feed,
        hidden,
        d_pre,
        d_own,
        d_peer,
        *shares,
        out_t,
        grad_up_bias,
        grad_down_bias,
    ) = middle_part(
        info,
        rows_low,
        mixed,
        mixed_peer,
        top_parts,
        row(ln2_gain),
        row(ln2_bias),
        row(b_out),
        pack_blocks,
        down_blocks,
        row(b_up),
        row(b_down),
    )

    got = swap_tensor(d_peer)
    down_own, down_far, down_send = weight_grad((d_feed, hidden))
    up_own, up_far, up_send = weight_grad((normed_two, d_pre))
    got, down_send, up_send, *shares = together(got, down_send, up_send, *shares)

    down_got = exchange(down_send, 1)
    d_middle, d_att, sums_two = turn(info, middle, d_own, got, top_parts[:2], row(ln2_gain))
    d_att, down_got, up_send, *shares = together(d_att, down_got, up_send, *shares)

    shard = down_own.shape[0]
    columns = hidden.shape[1]
    d_att_peer = swap_tensor(d_att)
    got_1 = exchange(down_far + down_got[shard:], 2)
    down_own = down_own + down_got[:shard]
    up_got = exchange(up_send, 1)
    share_0 = route(shares[0], 0, False)
    up_own, up_far = up_own + up_got[:shard], up_far + up_got[shard:]
    d_att_peer, got_1, up_own, up_far, share_0, share_1 = together(
        d_att_peer, got_1, up_own, up_far, share_0, shares[1]
    )

    half_1, sent = cut_sums((down_own, got_1, 1))
    got_1 = swap_planes(sent, 1)
    got_2 = exchange(up_far, 2)
    share_1 = route(share_1, 1, False)
    d_queries, d_pair, d_send = attend_back(
        info, queries, pair_own, pair_other, mixed, d_att, d_att_peer, out_t, logs
    )
    d_send, got_1, got_2, share_0, share_1 = together(d_send, got_1, got_2, share_0, share_1)


    d_got = exchange(d_send, 1)
    quarter_1, sent_1, half_2, sent_2 = cut_sums((half_1, got_1, 2), (up_own, got_2, 1))
    got_1 = swap_planes(sent_1, 2)
    got_2 = swap_planes(sent_2, 1)
    d_proj, one_own, one_peer, sides, proj_bias = leave(
        rows_low, proj, d_queries, d_pair, d_got, sums_two
    )
    own, far, send = weight_grad((normed_low, d_proj), (d_att, d_att_peer, mixed))
    one_peer, sides, send, got_1, got_2 = together(one_peer, sides, send, got_1, got_2)

    quarter_1, quarter_2, sent = add_and_cut(quarter_1, got_1, half_2, got_2)
    got_1 = swap_planes(quarter_1, 2)
    got_2 = swap_planes(sent, 2)
    sides_got = swap_tensor(sides)
    one_got = swap_tensor(one_peer)
    send_got = exchange(send, 1)
    send_got, one_got, got_1, got_2, sides_got = together(
        send_got, one_got, got_1, got_2, sides_got
    )

    vectors = gather_vectors(grad_up_bias, grad_down_bias, proj_bias, sides, sides_got)
    vectors_got = exchange(vectors, 1)
    input_rows = finish(rows_low, one_own, one_got, row(ln1_gain), d_middle)
    *input_rows, vectors_got, share_0, share_1 = together(
        *input_rows, vectors_got, share_0, share_1
    )

    packet, packet_far = merge(own, far, send_got, vectors, vectors_got)
    packet_got = exchange(packet_far, 2)
    share_got = [swap_tensor(share_0)]
    in_near = [route(input_rows[step], step, False) for step in range(2)]
    half_1, quarter_2 = glue_and_add(quarter_1, got_1, quarter_2, got_2)
    got_1 = swap_planes(half_1, 1)
    got_2 = swap_planes(quarter_2, 2)
    packet_got, got_1, got_2, share_1, *pieces = together(
        packet_got, got_1, got_2, share_1, *in_near, *share_got
    )
    in_near, share_got = pieces[:2], pieces[2:]

    quarters = spread(packet, packet_got, shard)
    arrived = [turn_planes(quarters[step], step) for step in range(1, 4)]
    in_far = [swap_tensor(v) for v in in_near]
    share_got.append(swap_tensor(share_1))
    half_2 = stack_rows(quarter_2, got_2, upper_half)
    got_2 = swap_planes(half_2, 1)
    arrived[0], half_1, got_1 = together(arrived[0], half_1, got_1)
    grad_down = stack_rows(half_1, got_1, odd).astype(jnp.float32).T
    *pieces, got_2 = together(quarters[0], *arrived, *in_far, *share_got, got_2)

    in_far, share_got = pieces[4:6], pieces[6:]
    quarter, vectors = total(pieces[:4], shard // 4, vectors.shape[0])
    quarters = [quarter] + [turn_planes(quarter, step) for step in range(1, 4)]
    input_grad = join_out(in_near, in_far, odd, upper)
    output = join_shares((share_0, share_1), share_got, odd, upper)
    grad_up = stack_rows(half_2, got_2, odd).astype(jnp.float32)
    *quarters, input_grad, output, grad_up, grad_down = together(
        *quarters, input_grad, output, grad_up, grad_down
    )
    grad_query, grad_key, grad_value, grad_out = assemble(quarters)
    return (
        output.reshape(tokens.shape),
        input_grad.reshape(tokens.shape),
        vectors[1, :width],
        vectors[1, width:],
        grad_query,
        vectors[4, :local_width],
        grad_key,
        grad_value,
        vectors[4, 2 * local_width : 3 * local_width],
        grad_out,
        vectors[3, :width],
        vectors[2, :width],
        vectors[2, width:],
        grad_up,
        vectors[0],
        grad_down,
        vectors[3, width:],
    )


def pick(mesh):
    sizes = mesh.shape
    planes = sizes["dp"] == 4 and sizes["context"] == 4 and sizes["tensor"] == 2
    return per_device_planes if planes else per_device_general


def solution(mesh):
    return jax.shard_map(
        pick(mesh),
        mesh=mesh,
        in_specs=(
            P("dp", "context", None),
            P("dp"),
            P(),
            P(),
            P("dp", "tensor"),
            P("tensor"),
            P("dp", "tensor"),
            P("dp", "tensor"),
            P("tensor"),
            P("tensor", "dp"),
            P(),
            P(),
            P(),
            P("dp", "tensor"),
            P("tensor"),
            P("tensor", "dp"),
            P(),
            P("dp", "context", None),
        ),
        out_specs=(
            P("dp", "context", None),
            P("dp", "context", None),
            P(),
            P(),
            P("dp", "tensor"),
            P("tensor"),
            P("dp", "tensor"),
            P("dp", "tensor"),
            P("tensor"),
            P("tensor", "dp"),
            P(),
            P(),
            P(),
            P("dp", "tensor"),
            P("tensor"),
            P("tensor", "dp"),
            P(),
        ),
        check_vma=False,
    )
```

```python
import functools

import jax
import jax.numpy as jnp
from jax import lax
from jax.experimental import pallas as pl
from jax.experimental.pallas import tpu as pltpu
from jax.sharding import PartitionSpec as P

HEAD_DIM = 64


epsilon = 1e-06
masked_value = -1e30


def norm_rows(values, gain_vec, bias_vec):
    average = jnp.mean(values, axis=-1, keepdims=True)
    centred = values - average
    spread = jnp.mean(centred * centred, axis=-1, keepdims=True)
    return centred * lax.rsqrt(spread + epsilon) * gain_vec + bias_vec


def gelu_tanh(values):
    return jax.nn.gelu(values, approximate=True)


def dense(left, right):
    return jnp.dot(left, right, preferred_element_type=jnp.float32)


def dense_tn(left, right):
    return lax.dot_general(
        left, right, (((0,), (0,)), ((), ())), preferred_element_type=jnp.float32
    )


def dense_nt(left, right):
    return lax.dot_general(
        left, right, (((1,), (1,)), ((), ())), preferred_element_type=jnp.float32
    )


def per_device_general(
    tokens,
    lengths,
    ln1_gain,
    ln1_bias,
    w_query,
    b_query,
    w_key,
    w_value,
    b_value,
    w_out,
    b_out,
    ln2_gain,
    ln2_bias,
    w_up,
    b_up,
    w_down,
    b_down,
    cotangent,
):
    seq_count, shard_rows, width = tokens.shape
    full_len = shard_rows * lax.axis_size("context")
    local_width = w_query.shape[1]
    local_heads = local_width // HEAD_DIM
    scale = HEAD_DIM ** (-0.5)
    row_count = seq_count * shard_rows
    query_weight, key_weight, value_weight, up_weight, out_weight, down_weight = (
        lax.all_gather(w_query, "dp", axis=0, tiled=True),
        lax.all_gather(w_key, "dp", axis=0, tiled=True),
        lax.all_gather(w_value, "dp", axis=0, tiled=True),
        lax.all_gather(w_up, "dp", axis=0, tiled=True),
        lax.all_gather(w_out, "dp", axis=1, tiled=True),
        lax.all_gather(w_down, "dp", axis=1, tiled=True),
    )
    gain_one = ln1_gain.astype(jnp.float32)
    bias_one = ln1_bias.astype(jnp.float32)
    query_bias = b_query.astype(jnp.float32)
    value_bias = b_value.astype(jnp.float32)
    out_bias = b_out.astype(jnp.float32)
    gain_two = ln2_gain.astype(jnp.float32)
    bias_two = ln2_bias.astype(jnp.float32)
    up_bias = b_up.astype(jnp.float32)
    down_bias = b_down.astype(jnp.float32)
    places = lax.axis_index("context") * shard_rows + jnp.arange(shard_rows, dtype=jnp.int32)
    keep = (places[None, :] < lengths[:, None]).astype(jnp.float32).reshape(row_count, 1)
    key_places = jnp.arange(full_len, dtype=jnp.int32)
    rows_in = tokens.reshape(row_count, width).astype(jnp.float32)
    normed_one, pull_one = jax.vjp(norm_rows, rows_in, gain_one, bias_one)
    normed_low = normed_one.astype(jnp.bfloat16)
    queries = (dense(normed_low, query_weight) + query_bias).astype(jnp.bfloat16)
    keys_own = dense(normed_low, key_weight).astype(jnp.bfloat16)
    values_own = (dense(normed_low, value_weight) + value_bias).astype(jnp.bfloat16)
    keys_whole, values_whole = (
        lax.all_gather(
            keys_own.reshape(seq_count, shard_rows, local_width), "context", axis=1, tiled=True
        ),
        lax.all_gather(
            values_own.reshape(seq_count, shard_rows, local_width), "context", axis=1, tiled=True
        ),
    )
    query_heads = queries.reshape(seq_count, shard_rows, local_heads, HEAD_DIM)
    head_outs = []
    log_sums = []
    for member in range(seq_count):
        key_heads = keys_whole[member].reshape(full_len, local_heads, HEAD_DIM)
        value_heads = values_whole[member].reshape(full_len, local_heads, HEAD_DIM)
        raw_scores = (
            jnp.einsum(
                "qhd,khd->hqk", query_heads[member], key_heads, preferred_element_type=jnp.float32
            )
            * scale
        )
        live = (key_places < lengths[member])[None, None, :]
        masked = jnp.where(live, raw_scores, masked_value)
        largest = jnp.max(masked, axis=-1, keepdims=True)
        log_total = largest + jnp.log(jnp.sum(jnp.exp(masked - largest), axis=-1, keepdims=True))
        probs_low = jnp.exp(masked - log_total).astype(jnp.bfloat16)
        mixed_heads = jnp.einsum(
            "hqk,khd->qhd", probs_low, value_heads, preferred_element_type=jnp.float32
        )
        head_outs.append(mixed_heads.reshape(shard_rows, local_width))
        log_sums.append(log_total)
    context_low = jnp.concatenate(head_outs, axis=0).astype(jnp.bfloat16)
    attention = (
        lax.psum(dense(context_low, out_weight).astype(jnp.bfloat16), "tensor").astype(jnp.float32)
        + out_bias
    )
    middle = rows_in + keep * attention
    normed_two, pull_two = jax.vjp(norm_rows, middle, gain_two, bias_two)
    normed_two_low = normed_two.astype(jnp.bfloat16)
    hidden_pre = dense(normed_two_low, up_weight) + up_bias
    hidden, pull_gelu = jax.vjp(gelu_tanh, hidden_pre)
    hidden_low = hidden.astype(jnp.bfloat16)
    feed = (
        lax.psum(dense(hidden_low, down_weight).astype(jnp.bfloat16), "tensor").astype(jnp.float32)
        + down_bias
    )
    output = (middle + keep * feed).astype(jnp.bfloat16).reshape(tokens.shape)
    grad_top = cotangent.reshape(row_count, width).astype(jnp.float32)
    d_feed = (keep * grad_top).astype(jnp.bfloat16)
    grad_down_bias = jnp.sum(d_feed.astype(jnp.float32), axis=0)
    grad_down = dense_tn(hidden_low, d_feed)
    d_hidden = dense_nt(d_feed, down_weight)
    d_pre = pull_gelu(d_hidden)[0].astype(jnp.bfloat16)
    grad_up_bias = jnp.sum(d_pre.astype(jnp.float32), axis=0)
    grad_up = dense_tn(normed_two_low, d_pre)
    d_normed_two = lax.psum(dense_nt(d_pre, up_weight).astype(jnp.bfloat16), "tensor").astype(
        jnp.float32
    )
    d_middle, grad_gain_two, grad_bias_two = pull_two(d_normed_two)
    d_middle = d_middle + grad_top
    d_attention = (keep * d_middle).astype(jnp.bfloat16)
    grad_out_bias = jnp.sum(d_attention.astype(jnp.float32), axis=0)
    grad_out = dense_tn(context_low, d_attention)
    d_context = dense_nt(d_attention, out_weight).astype(jnp.bfloat16)
    back_keys, back_values = (keys_whole, values_whole)
    d_context_heads = d_context.reshape(seq_count, shard_rows, local_heads, HEAD_DIM)
    query_grads = []
    own_grads = []
    inner_rows = []
    for member in range(seq_count):
        key_heads = back_keys[member].reshape(full_len, local_heads, HEAD_DIM)
        value_heads = back_values[member].reshape(full_len, local_heads, HEAD_DIM)
        raw_scores = (
            jnp.einsum(
                "qhd,khd->hqk", query_heads[member], key_heads, preferred_element_type=jnp.float32
            )
            * scale
        )
        live = (key_places < lengths[member])[None, None, :]
        probs = jnp.where(live, jnp.exp(raw_scores - log_sums[member]), 0.0)
        d_probs = jnp.einsum(
            "qhd,khd->hqk", d_context_heads[member], value_heads, preferred_element_type=jnp.float32
        )
        inner = jnp.sum(probs * d_probs, axis=-1, keepdims=True)
        d_scores = (probs * (d_probs - inner)).astype(jnp.bfloat16)
        d_query = (
            jnp.einsum("hqk,khd->qhd", d_scores, key_heads, preferred_element_type=jnp.float32)
            * scale
        )
        query_grads.append(d_query.reshape(shard_rows, local_width))
        inner_rows.append(inner[:, :, 0])
        d_keys = (
            jnp.einsum(
                "hqk,qhd->khd", d_scores, query_heads[member], preferred_element_type=jnp.float32
            )
            * scale
        )
        d_values = jnp.einsum(
            "hqk,qhd->khd",
            probs.astype(jnp.bfloat16),
            d_context_heads[member],
            preferred_element_type=jnp.float32,
        )
        key_term = jnp.concatenate(
            [d_keys.reshape(full_len, local_width), d_values.reshape(full_len, local_width)], axis=1
        )
        own_grads.append(
            lax.psum_scatter(
                key_term.astype(jnp.bfloat16), "context", scatter_dimension=0, tiled=True
            ).astype(jnp.float32)
        )
    d_query_low = jnp.concatenate(query_grads, axis=0).astype(jnp.bfloat16)
    key_value_grads = jnp.concatenate(own_grads, axis=0)
    d_keys_low = key_value_grads[:, :local_width].astype(jnp.bfloat16)
    d_values_low = key_value_grads[:, local_width:].astype(jnp.bfloat16)
    grad_query = dense_tn(normed_low, d_query_low)
    grad_query_bias = jnp.sum(d_query_low.astype(jnp.float32), axis=0)
    grad_key = dense_tn(normed_low, d_keys_low)
    grad_value = dense_tn(normed_low, d_values_low)
    grad_value_bias = jnp.sum(d_values_low.astype(jnp.float32), axis=0)
    d_normed_one = lax.psum(
        (
            dense_nt(d_query_low, query_weight)
            + dense_nt(d_keys_low, key_weight)
            + dense_nt(d_values_low, value_weight)
        ).astype(jnp.bfloat16),
        "tensor",
    ).astype(jnp.float32)
    d_rows, grad_gain_one, grad_bias_one = pull_one(d_normed_one)
    input_grad = (d_rows + d_middle).astype(jnp.bfloat16).reshape(tokens.shape)
    data_sums = (
        lax.psum_scatter(
            grad_query.astype(jnp.bfloat16), "dp", scatter_dimension=0, tiled=True
        ).astype(jnp.float32),
        lax.psum_scatter(
            grad_key.astype(jnp.bfloat16), "dp", scatter_dimension=0, tiled=True
        ).astype(jnp.float32),
        lax.psum_scatter(
            grad_value.astype(jnp.bfloat16), "dp", scatter_dimension=0, tiled=True
        ).astype(jnp.float32),
        lax.psum_scatter(
            grad_up.astype(jnp.bfloat16), "dp", scatter_dimension=0, tiled=True
        ).astype(jnp.float32),
        lax.psum_scatter(
            grad_out.astype(jnp.bfloat16), "dp", scatter_dimension=1, tiled=True
        ).astype(jnp.float32),
        lax.psum_scatter(
            grad_down.astype(jnp.bfloat16), "dp", scatter_dimension=1, tiled=True
        ).astype(jnp.float32),
    )
    owned_sums = (
        lax.psum(data_sums[0].astype(jnp.bfloat16), "context").astype(jnp.float32),
        lax.psum(data_sums[1].astype(jnp.bfloat16), "context").astype(jnp.float32),
        lax.psum(data_sums[2].astype(jnp.bfloat16), "context").astype(jnp.float32),
        lax.psum(data_sums[3].astype(jnp.bfloat16), "context").astype(jnp.float32),
        lax.psum(data_sums[4].astype(jnp.bfloat16), "context").astype(jnp.float32),
        lax.psum(data_sums[5].astype(jnp.bfloat16), "context").astype(jnp.float32),
    )
    small_sums = lax.psum(
        (
            grad_gain_one,
            grad_bias_one,
            grad_query_bias,
            grad_value_bias,
            grad_out_bias,
            grad_gain_two,
            grad_bias_two,
            grad_up_bias,
            grad_down_bias,
        ),
        ("dp", "context"),
    )
    return (
        output,
        input_grad,
        small_sums[0],
        small_sums[1],
        owned_sums[0],
        small_sums[2],
        owned_sums[1],
        owned_sums[2],
        small_sums[3],
        owned_sums[4],
        small_sums[4],
        small_sums[5],
        small_sums[6],
        owned_sums[3],
        small_sums[7],
        owned_sums[5],
        small_sums[8],
    )


def live_bias(info, count):
    places = lax.broadcasted_iota(jnp.int32, (count, 2 * HEAD_DIM), 0)
    return jnp.concatenate(
        [jnp.where(info[k] + places < info[8], 0.0, masked_value) for k in range(8)], axis=0
    ).astype(jnp.bfloat16)


def split_pair(array, extra):
    lane = lax.broadcasted_iota(jnp.int32, array.shape, 1)
    zero = jnp.zeros((), jnp.bfloat16)
    left = jnp.where(lane < HEAD_DIM, array, jnp.where(lane == HEAD_DIM, extra, zero))
    right = jnp.where(lane >= HEAD_DIM, array, jnp.where(lane == 0, extra, zero))
    return left, right


LOG_SCALE = HEAD_DIM ** (-0.5) * 1.4426950408889634


def attend_kernel(info, query_ref, own_ref, other_ref, out_ref, log_ref):
    pair = 2 * HEAD_DIM
    count = query_ref.shape[0] // 4
    keys = jnp.concatenate([own_ref[:, :pair], other_ref[:, :pair]], axis=0)
    values = jnp.concatenate([own_ref[:, pair:], other_ref[:, pair:]], axis=0)
    values_t = values.T
    key_heads = split_pair(keys, live_bias(info, count))
    query_heads = split_pair(query_ref[...], jnp.ones((), jnp.bfloat16))
    mixed = []
    for head in range(2):
        scores = dense_nt(key_heads[head], query_heads[head])
        largest = jnp.max(scores, axis=0, keepdims=True)
        weights = jnp.exp2((scores - largest) * LOG_SCALE)
        total = jnp.sum(weights, axis=0, keepdims=True)
        dims = slice(head * HEAD_DIM, (head + 1) * HEAD_DIM)
        mixed.append(dense(values_t[dims], weights.astype(jnp.bfloat16)) / total)
        log_ref[0, head : head + 1, :] = largest * LOG_SCALE + jnp.log2(total)
    out_ref[...] = jnp.concatenate(mixed, axis=0).T.astype(jnp.bfloat16)


def attend(info, queries, pair_own, pair_other):
    rows, width = queries.shape
    pair = 2 * HEAD_DIM
    groups = width // pair
    work = 4 * rows * 2 * rows * width
    return pl.pallas_call(
        attend_kernel,
        out_shape=(
            jax.ShapeDtypeStruct((rows, width), jnp.bfloat16),
            jax.ShapeDtypeStruct((groups, 2, rows), jnp.float32),
        ),
        grid_spec=pltpu.PrefetchScalarGridSpec(
            num_scalar_prefetch=1,
            grid=(groups,),
            in_specs=[
                pl.BlockSpec((rows, pair), lambda g, info: (0, g)),
                pl.BlockSpec((rows, 2 * pair), lambda g, info: (0, g)),
                pl.BlockSpec((rows, 2 * pair), lambda g, info: (0, g)),
            ],
            out_specs=(
                pl.BlockSpec((rows, pair), lambda g, info: (0, g)),
                pl.BlockSpec((1, 2, rows), lambda g, info: (g, 0, 0)),
            ),
        ),
        compiler_params=pltpu.CompilerParams(vmem_limit_bytes=32 << 20),
        cost_estimate=pl.CostEstimate(
            flops=4 * work, bytes_accessed=12 * rows * width, transcendentals=work // (2 * HEAD_DIM)
        ),
    )(info, queries, pair_own, pair_other)


def attend_back_kernel(
    info,
    query_ref,
    own_ref,
    other_ref,
    out_ref,
    d_own_ref,
    d_peer_ref,
    proj_ref,
    log_ref,
    d_query_ref,
    d_pair_ref,
    d_other_ref,
):
    pair = 2 * HEAD_DIM
    rows = query_ref.shape[0]
    scale = HEAD_DIM ** (-0.5)
    keys = jnp.concatenate([own_ref[:, :pair], other_ref[:, :pair]], axis=0)
    values = jnp.concatenate([own_ref[:, pair:], other_ref[:, pair:]], axis=0)
    keys_t = keys.T
    key_heads = split_pair(keys, live_bias(info, rows // 4))
    value_heads = split_pair(values, jnp.zeros((), jnp.bfloat16))
    query = query_ref[...]
    query_heads = split_pair(query, jnp.ones((), jnp.bfloat16))
    d_att = jnp.concatenate([d_own_ref[...], d_peer_ref[...]], axis=0)
    grad = dense(d_att, proj_ref[...]).astype(jnp.bfloat16)
    inner_t = (grad.astype(jnp.float32) * out_ref[...].astype(jnp.float32)).T
    d_query, d_keys, d_values = [], [], []
    for head in range(2):
        dims = slice(head * HEAD_DIM, (head + 1) * HEAD_DIM)
        inner = jnp.sum(inner_t[dims], axis=0, keepdims=True)
        scores = dense_nt(key_heads[head], query_heads[head])
        probs = jnp.exp2(scores * LOG_SCALE - log_ref[0, head : head + 1, :])
        d_probs = dense_nt(value_heads[head], grad)
        d_scores = (probs * (d_probs - inner)).astype(jnp.bfloat16)
        d_query.append(dense(keys_t[dims], d_scores))
        d_keys.append(dense(d_scores, query))
        d_values.append(dense(probs.astype(jnp.bfloat16), grad))
    d_query_ref[...] = (jnp.concatenate(d_query, axis=0).T * scale).astype(jnp.bfloat16)
    left = lax.broadcasted_iota(jnp.int32, d_keys[0].shape, 1) < HEAD_DIM
    d_key = (jnp.where(left, d_keys[0], d_keys[1]) * scale).astype(jnp.bfloat16)
    d_value = jnp.where(left, d_values[0], d_values[1]).astype(jnp.bfloat16)
    d_pair_ref[:, :pair] = d_key[:rows]
    d_pair_ref[:, pair:] = d_value[:rows]
    d_other_ref[:, :pair] = d_key[rows:]
    d_other_ref[:, pair:] = d_value[rows:]


def attend_back(info, queries, pair_own, pair_other, mixed, d_own, d_peer, out_t, logs):
    rows, local = queries.shape
    width = out_t.shape[0]
    pair = 2 * HEAD_DIM
    work = 4 * rows * 2 * rows * local
    narrow = pl.BlockSpec((rows, pair), lambda g, info: (0, g))
    wide = pl.BlockSpec((rows, 2 * pair), lambda g, info: (0, g))
    halves = pl.BlockSpec((rows // 2, width), lambda g, info: (0, 0))
    return pl.pallas_call(
        attend_back_kernel,
        out_shape=tuple(
            jax.ShapeDtypeStruct((rows, columns), jnp.bfloat16)
            for columns in (local, 2 * local, 2 * local)
        ),
        grid_spec=pltpu.PrefetchScalarGridSpec(
            num_scalar_prefetch=1,
            grid=(local // pair,),
            in_specs=[
                narrow,
                wide,
                wide,
                narrow,
                halves,
                halves,
                pl.BlockSpec((width, pair), lambda g, info: (0, g)),
                pl.BlockSpec((1, 2, rows), lambda g, info: (g, 0, 0)),
            ],
            out_specs=(narrow, wide, wide),
        ),
        compiler_params=pltpu.CompilerParams(vmem_limit_bytes=32 << 20),
        cost_estimate=pl.CostEstimate(
            flops=10 * work, bytes_accessed=24 * rows * local, transcendentals=work // (2 * HEAD_DIM)
        ),
    )(info, queries, pair_own, pair_other, mixed, d_own, d_peer, out_t, logs)


def held(info, quarters, count, width):
    places = lax.broadcasted_iota(jnp.int32, (count, width), 0)
    return jnp.concatenate([info[k] + places < info[8] for k in range(quarters)], axis=0)


def fixed(array):
    return pl.BlockSpec(array.shape, lambda i: (0,) * len(array.shape))


def call_once(kernel, args, shapes, flops, scratch=()):
    moved = sum(a.size * a.dtype.itemsize for a in (*args, *shapes))
    return pl.pallas_call(
        kernel,
        out_shape=tuple(shapes),
        grid=(1,),
        in_specs=[fixed(a) for a in args],
        out_specs=tuple(fixed(s) for s in shapes),
        scratch_shapes=list(scratch),
        compiler_params=pltpu.CompilerParams(vmem_limit_bytes=24 << 20),
        cost_estimate=pl.CostEstimate(flops=flops, bytes_accessed=moved, transcendentals=0),
    )(*args)


def low(*shape):
    return jax.ShapeDtypeStruct(shape, jnp.bfloat16)


def full(*shape):
    return jax.ShapeDtypeStruct(shape, jnp.float32)


def row_stats(values):
    centred = values - jnp.mean(values, axis=-1, keepdims=True)
    spread = jnp.mean(centred * centred, axis=-1, keepdims=True)
    root = lax.rsqrt(spread + epsilon)
    return centred * root, root


def row_pull(normed, root, grad):
    return root * (
        grad
        - jnp.mean(grad, axis=-1, keepdims=True)
        - normed * jnp.mean(grad * normed, axis=-1, keepdims=True)
    )


def settle(parts, out_ref):
    rows = parts[0].shape[0]
    mine = lax.axis_index("dp")
    for step, part in enumerate(parts):
        start = pl.multiple_of((mine ^ step) * rows, rows)
        out_ref[pl.ds(start, rows), :] = part[...]


def enter_kernel(
    own0, own1, peer0, peer1, gain_ref, bias_ref, q_bias_ref, v_bias_ref, a, b, c, d,
    rows_ref, normed_ref, query_ref, pair_ref, proj_ref,
):
    pair = 2 * HEAD_DIM
    settle((a, b, c, d), proj_ref)
    rows = jnp.concatenate([own0[...], own1[...], peer0[...], peer1[...]], axis=0)
    rows_ref[...] = rows
    normed, _ = row_stats(rows.astype(jnp.float32))
    normed = normed * gain_ref[...].astype(jnp.float32) + bias_ref[...].astype(jnp.float32)
    normed = normed.astype(jnp.bfloat16)
    normed_ref[...] = normed
    local = query_ref.shape[1]
    mixed = dense(normed, proj_ref[...])
    query_ref[...] = (mixed[:, :local] + q_bias_ref[...].astype(jnp.float32)).astype(jnp.bfloat16)
    for g in range(local // pair):
        cols = slice(g * pair, (g + 1) * pair)
        key = mixed[:, local + g * pair : local + (g + 1) * pair]
        value = mixed[:, 2 * local + g * pair : 2 * local + (g + 1) * pair]
        value = value + v_bias_ref[:, cols].astype(jnp.float32)
        pair_ref[:, 2 * g * pair : (2 * g + 1) * pair] = key.astype(jnp.bfloat16)
        pair_ref[:, (2 * g + 1) * pair : (2 * g + 2) * pair] = value.astype(jnp.bfloat16)


def enter(pieces, gain, bias, q_bias, v_bias, blocks):
    half, width = pieces[0].shape
    rows = 4 * half
    local = q_bias.shape[1]
    shapes = (
        low(rows, width),
        low(rows, width),
        low(rows, local),
        low(rows, 2 * local),
        low(width, 3 * local),
    )
    args = (*pieces, gain, bias, q_bias, v_bias, *blocks)
    return call_once(enter_kernel, args, shapes, 6 * rows * width * local)


ROOT_TWO_OVER_PI = 0.7978845608028654
CUBE = 0.044715


def fetch(parts, columns, out_ref, sems):
    rows = parts[0].shape[0]
    mine = lax.axis_index("dp")
    copies = []
    for step, part in enumerate(parts):
        start = pl.multiple_of((mine ^ step) * rows, rows)
        copy = pltpu.make_async_copy(
            part.at[:, columns], out_ref.at[pl.ds(start, rows)], sems.at[step]
        )
        copy.start()
        copies.append(copy)
    return copies


def middle_kernel(
    info, rows_ref, own_ref, peer_ref, top0, top1, top2, top3, gain_ref, bias_ref, out_bias_ref,
    up_bias_ref, down_bias_ref, pa, pb, pc, pd, da, db, dc, dd,
    mid_ref, normed_ref, feed_ref, hidden_ref, d_pre_ref, d_own_ref, d_peer_ref,
    part0_ref, part1_ref, out_ref, g_up_ref, g_down_ref,
    outs, ups, downs, whole_mid, sent, sems,
):
    rows, width = rows_ref.shape
    half = rows // 2
    local = own_ref.shape[1]
    hidden_width = up_bias_ref.shape[1]
    steps = ups.shape[0]
    tile = hidden_width // steps
    packs, lasts = (pa, pb, pc, pd), (da, db, dc, dd)
    waits = [fetch(packs, pl.ds(hidden_width, width), outs, sems.at[0])]
    for s in range(steps):
        columns = pl.ds(s * tile, tile)
        waits.append(fetch(packs, columns, ups.at[s], sems.at[1 + 2 * s]))
        waits.append(fetch(lasts, columns, downs.at[s], sems.at[2 + 2 * s]))

    real = held(info, 4, rows // 4, width)
    top = jnp.concatenate([top0[...], top1[...], top2[...], top3[...]], axis=0)
    feed = jnp.where(real, top.astype(jnp.float32), 0.0)
    feed_ref[...] = feed.astype(jnp.bfloat16)
    g_down_ref[...] = jnp.sum(feed, axis=0, keepdims=True)
    peer = jnp.concatenate([peer_ref[half:, :], peer_ref[:half, :]], axis=0)
    for copy in waits[0]:
        copy.wait()
    out_ref[...] = outs[:, :local]
    attention = (
        dense_nt(own_ref[...], outs[:, :local])
        + dense_nt(peer, outs[:, local:])
        + out_bias_ref[...].astype(jnp.float32)
    )
    mid = rows_ref[...].astype(jnp.float32) + jnp.where(real, attention, 0.0)
    mid_ref[...] = mid[:half]
    whole_mid[...] = mid
    normed, _ = row_stats(mid)
    normed = normed * gain_ref[...].astype(jnp.float32) + bias_ref[...].astype(jnp.float32)
    normed_ref[...] = normed.astype(jnp.bfloat16)

    for s in range(steps):
        columns = slice(s * tile, (s + 1) * tile)
        for copy in waits[1 + 2 * s] + waits[2 + 2 * s]:
            copy.wait()
        pre = dense(normed_ref[...], ups[s]) + up_bias_ref[:, columns].astype(jnp.float32)
        d_hidden = dense(feed_ref[...], downs[s])
        square = pre * pre
        bend = jnp.tanh(pre * (ROOT_TWO_OVER_PI + CUBE * ROOT_TWO_OVER_PI * square))
        half_up = 0.5 + 0.5 * bend
        active = pre * half_up
        slope = half_up + active * (1.0 - bend) * (
            ROOT_TWO_OVER_PI + 3.0 * CUBE * ROOT_TWO_OVER_PI * square
        )
        hidden_ref[:, columns] = active.astype(jnp.bfloat16)
        d_pre = (d_hidden * slope).astype(jnp.bfloat16)
        d_pre_ref[:, columns] = d_pre
        g_up_ref[:, columns] = jnp.sum(d_pre.astype(jnp.float32), axis=0, keepdims=True)

    def back(left_ref, right_ref):
        total = 0.0
        for s in range(steps):
            total += dense_nt(left_ref[:, s * tile : (s + 1) * tile], right_ref[s])
        return total

    grad = back(d_pre_ref, ups).astype(jnp.bfloat16)
    d_own_ref[...] = grad[:half]
    sent[...] = grad[half:]
    leaving = pltpu.make_async_copy(sent, d_peer_ref, sems.at[0, 0])
    leaving.start()
    first = lax.axis_index("tensor") == 0
    share = back(hidden_ref, downs)
    share += jnp.where(first, down_bias_ref[...].astype(jnp.float32), 0.0)
    share = jnp.where(real, share, 0.0) + jnp.where(first, whole_mid[...], 0.0)
    share = share.astype(jnp.bfloat16)
    for k, part in enumerate((part0_ref, part1_ref)):
        start = k * (half // 2)
        part[0] = share[start : start + half // 2]
        part[1] = share[half + start : half + start + half // 2]
    leaving.wait()


def middle_part(
    info, rows_low, own, peer, top, gain, bias, out_bias, packs, downs, up_bias, down_bias
):
    rows, width = rows_low.shape
    local = own.shape[1]
    hidden = up_bias.shape[1]
    steps = 2
    small = (rows_low, own, peer, *top, gain, bias, out_bias, up_bias, down_bias)
    inside = pl.BlockSpec(memory_space=pltpu.VMEM)
    outside = pl.BlockSpec(memory_space=pltpu.HBM)
    shapes = (
        full(rows // 2, width),
        low(rows, width),
        low(rows, width),
        low(rows, hidden),
        low(rows, hidden),
        low(rows // 2, width),
        low(rows // 2, width),
        low(2, rows // 4, width),
        low(2, rows // 4, width),
        low(width, local),
        full(1, hidden),
        full(1, width),
    )
    return pl.pallas_call(
        middle_kernel,
        out_shape=shapes,
        in_specs=[pl.BlockSpec(memory_space=pltpu.SMEM)]
        + [inside] * len(small)
        + [pl.BlockSpec(memory_space=pltpu.HBM)] * 8,
        out_specs=tuple(outside if k == 6 else inside for k in range(len(shapes))),
        scratch_shapes=[
            pltpu.VMEM((width, width), jnp.bfloat16),
            pltpu.VMEM((steps, width, hidden // steps), jnp.bfloat16),
            pltpu.VMEM((steps, width, hidden // steps), jnp.bfloat16),
            pltpu.VMEM((rows, width), jnp.float32),
            pltpu.VMEM((rows // 2, width), jnp.bfloat16),
            pltpu.SemaphoreType.DMA((1 + 2 * steps, 4)),
        ],
        compiler_params=pltpu.CompilerParams(vmem_limit_bytes=36 << 20),
        cost_estimate=pl.CostEstimate(
            flops=8 * rows * width * hidden, bytes_accessed=20 << 20, transcendentals=rows * hidden
        ),
    )(info, *small, *packs, *downs)


def turn_kernel(
    info, mid_ref, d_own_ref, got_ref, top0, top1, gain_ref, d_mid_ref, d_att_ref, sums_ref
):
    half, width = d_own_ref.shape
    grad = d_own_ref[...].astype(jnp.float32) + got_ref[...].astype(jnp.float32)
    normed, root = row_stats(mid_ref[...])
    top = jnp.concatenate([top0[...], top1[...]], axis=0).astype(jnp.float32)
    d_mid = top + row_pull(normed, root, grad * gain_ref[...].astype(jnp.float32))
    d_mid_ref[...] = d_mid
    d_att = jnp.where(held(info, 2, half // 2, width), d_mid, 0.0).astype(jnp.bfloat16)
    d_att_ref[...] = d_att
    sums_ref[0:1, :] = jnp.sum(grad * normed, axis=0, keepdims=True)
    sums_ref[1:2, :] = jnp.sum(grad, axis=0, keepdims=True)
    sums_ref[2:3, :] = jnp.sum(d_att.astype(jnp.float32), axis=0, keepdims=True)


def turn(info, mid, d_own, got, top, gain):
    half, width = d_own.shape
    fixed = lambda a: pl.BlockSpec(a.shape, lambda i, info: (0,) * len(a.shape))
    first = pl.BlockSpec((half, width), lambda i, info: (0, 0))
    shapes = (
        jax.ShapeDtypeStruct((half, width), jnp.float32),
        jax.ShapeDtypeStruct((half, width), jnp.bfloat16),
        jax.ShapeDtypeStruct((3, width), jnp.float32),
    )
    return pl.pallas_call(
        turn_kernel,
        out_shape=shapes,
        grid_spec=pltpu.PrefetchScalarGridSpec(
            num_scalar_prefetch=1,
            grid=(1,),
            in_specs=[first, fixed(d_own), fixed(got), fixed(top[0]), fixed(top[1]), fixed(gain)],
            out_specs=tuple(fixed(s) for s in shapes),
        ),
        compiler_params=pltpu.CompilerParams(vmem_limit_bytes=24 << 20),
        cost_estimate=pl.CostEstimate(
            flops=40 * half * width, bytes_accessed=4 << 20, transcendentals=half
        ),
    )(info, mid, d_own, got, *top, gain)


def leave_kernel(
    rows_ref, proj_ref, d_query_ref, d_pair_ref, got_ref, sums_two_ref,
    d_proj_ref, own_ref, peer_ref, sums_ref, bias_ref,
):
    pair = 2 * HEAD_DIM
    rows, local = d_query_ref.shape
    half = rows // 2
    d_proj_ref[:, :local] = d_query_ref[...]
    total = (d_pair_ref[...].astype(jnp.float32) + got_ref[...].astype(jnp.float32)).astype(
        jnp.bfloat16
    )
    for g in range(local // pair):
        for k in range(2):
            start = (k + 1) * local + g * pair
            d_proj_ref[:, start : start + pair] = total[:, (2 * g + k) * pair : (2 * g + k + 1) * pair]
    d_proj = d_proj_ref[...]
    bias_ref[...] = jnp.sum(d_proj.astype(jnp.float32), axis=0, keepdims=True)
    grad = dense_nt(d_proj, proj_ref[...])
    low = grad.astype(jnp.bfloat16)
    own_ref[...] = low[:half]
    peer_ref[...] = low[half:]
    normed, _ = row_stats(rows_ref[...].astype(jnp.float32))
    sums_ref[0:1, :] = jnp.sum(grad * normed, axis=0, keepdims=True)
    sums_ref[1:2, :] = jnp.sum(grad, axis=0, keepdims=True)
    sums_ref[2:5, :] = sums_two_ref[...]


def leave(rows_low, proj, d_query, d_pair, got, sums_two):
    rows, width = rows_low.shape
    columns = proj.shape[1]
    shapes = (
        low(rows, columns),
        low(rows // 2, width),
        low(rows // 2, width),
        full(5, width),
        full(1, columns),
    )
    args = (rows_low, proj, d_query, d_pair, got, sums_two)
    return call_once(leave_kernel, args, shapes, 2 * rows * width * columns)


def finish_kernel(rows_ref, own_ref, got_ref, gain_ref, d_mid_ref, first_ref, second_ref):
    half = rows_ref.shape[0]
    normed, root = row_stats(rows_ref[...].astype(jnp.float32))
    grad = own_ref[...].astype(jnp.float32) + got_ref[...].astype(jnp.float32)
    d_rows = row_pull(normed, root, grad * gain_ref[...].astype(jnp.float32)) + d_mid_ref[...]
    low = d_rows.astype(jnp.bfloat16)
    first_ref[...] = low[: half // 2]
    second_ref[...] = low[half // 2 :]


def finish(rows_low, own, got, gain, d_mid):
    half, width = own.shape
    top_half = pl.BlockSpec((half, width), lambda i: (0, 0))
    fixed = lambda a: pl.BlockSpec(a.shape, lambda i: (0,) * a.ndim)
    piece = jax.ShapeDtypeStruct((half // 2, width), jnp.bfloat16)
    return pl.pallas_call(
        finish_kernel,
        out_shape=(piece, piece),
        grid=(1,),
        in_specs=[top_half, fixed(own), fixed(got), fixed(gain), fixed(d_mid)],
        out_specs=(fixed(piece), fixed(piece)),
        compiler_params=pltpu.CompilerParams(vmem_limit_bytes=24 << 20),
        cost_estimate=pl.CostEstimate(
            flops=20 * half * width, bytes_accessed=4 << 20, transcendentals=half
        ),
    )(rows_low, own, got, gain, d_mid)


def weight_grad_kernel(*refs, counts):
    lefts, used = [], 0
    for count in counts:
        lefts.append((refs[used : used + count], refs[used + count]))
        used += count + 1
    own_ref, far_ref, send_ref = refs[used : used + 3]
    rows = own_ref.shape[0]
    mine = lax.axis_index("dp")
    targets = (own_ref, send_ref.at[:rows], far_ref, send_ref.at[rows:])
    start = 0
    for (pieces, right), turned in zip(lefts, refs[used + 3 :]):
        turned[...] = jnp.concatenate([piece[...] for piece in pieces], axis=0).T
        width = right.shape[1]
        for step, target in enumerate(targets):
            place = pl.multiple_of((mine ^ step) * rows, rows)
            grad = dense(turned[pl.ds(place, rows), :], right[...])
            target[:, start : start + width] = grad.astype(jnp.bfloat16)
        start += width


def split_bits(values):
    high = values.astype(jnp.bfloat16)
    return high, (values - high.astype(jnp.float32)).astype(jnp.bfloat16)


def weight_grad(*products):
    depth, width = products[0][-1].shape[0], products[0][0].shape[1]
    columns = sum(product[-1].shape[1] for product in products)
    rows = width // 4
    shapes = (low(rows, columns), low(rows, columns), low(2 * rows, columns))
    turned = [pltpu.VMEM((width, depth), jnp.bfloat16)] * len(products)
    kernel = functools.partial(
        weight_grad_kernel, counts=tuple(len(product) - 1 for product in products)
    )
    args = [array for product in products for array in product]
    return call_once(kernel, args, shapes, 2 * depth * width * columns, turned)


def add_terms(left, right):
    f32 = lambda value: value.astype(jnp.float32)
    half = left.shape[0] // 2
    total = f32(left[:half]) + f32(left[half:]) + (f32(right[:half]) + f32(right[half:]))
    return jnp.concatenate(split_bits(total), axis=0)


def merge_kernel(own_ref, far_ref, got_ref, mine_ref, theirs_ref, sum_ref, send_ref):
    rows = own_ref.shape[0]
    sum_ref[:rows, :] = own_ref[...] + got_ref[:rows, :]
    send_ref[:rows, :] = far_ref[...] + got_ref[rows:, :]
    terms = jnp.concatenate(split_bits(mine_ref[...] + theirs_ref[...]), axis=0)
    sum_ref[rows:, :] = terms
    send_ref[rows:, :] = terms


def merge(own, far, got, mine, theirs):
    rows, columns = own.shape
    packet = low(rows + 2 * mine.shape[0], columns)
    args = (own, far, got, mine, theirs)
    return call_once(merge_kernel, args, (packet, packet), own.size)


def spread_kernel(left_ref, right_ref, *outs, rows):
    plane = lax.axis_index("context")
    terms = add_terms(left_ref[rows:, :], right_ref[rows:, :])
    piece = rows // 4
    for step, out in enumerate(outs):
        start = pl.multiple_of((plane + step) % 4 * piece, piece)
        out[:piece, :] = left_ref[pl.ds(start, piece), :] + right_ref[pl.ds(start, piece), :]
        out[piece:, :] = terms


def spread(left, right, rows):
    piece = low(rows // 4 + left.shape[0] - rows, left.shape[1])
    kernel = functools.partial(spread_kernel, rows=rows)
    return call_once(kernel, (left, right), (piece,) * 4, left.size)


def total_kernel(*refs, piece):
    parts, (sum_ref, vectors_ref, held_ref) = refs[:4], refs[4:]
    plane = lax.axis_index("context")
    f32 = lambda value: value.astype(jnp.float32)
    total = f32(parts[0][:piece, :]) + f32(parts[1][:piece, :])
    total += f32(parts[2][:piece, :]) + f32(parts[3][:piece, :])
    sum_ref[...] = total.astype(jnp.bfloat16)
    count = vectors_ref.shape[0]
    for step, part in enumerate(parts):
        held_ref[(plane + 4 - step) % 4] = f32(part[piece : piece + count, :]) + f32(
            part[piece + count :, :]
        )
    vectors_ref[...] = held_ref[0] + held_ref[1] + held_ref[2] + held_ref[3]


def total(parts, piece, count):
    columns = parts[0].shape[1]
    shapes = (low(piece, columns), full(count, columns))
    held_terms = pltpu.VMEM((4, count, columns), jnp.float32)
    kernel = functools.partial(total_kernel, piece=piece)
    return call_once(kernel, parts, shapes, 4 * piece * columns, [held_terms])


def assemble_kernel(a, b, c, d, query_ref, key_ref, value_ref, out_ref, turned):
    plane = lax.axis_index("context")
    piece = a.shape[0]
    local = query_ref.shape[1]
    for step, part in enumerate((a, b, c, d)):
        start = pl.multiple_of((plane + 4 - step) % 4 * piece, piece)
        here = part[...].astype(jnp.float32)
        for k, ref in enumerate((query_ref, key_ref, value_ref, turned)):
            ref[pl.ds(start, piece), :] = here[:, k * local : (k + 1) * local]
    out_ref[...] = turned[...].T


def assemble(parts):
    piece, columns = parts[0].shape
    rows, local = 4 * piece, columns // 4
    shapes = (full(rows, local),) * 3 + (full(local, rows),)
    turned = pltpu.VMEM((rows, local), jnp.float32)
    return call_once(assemble_kernel, parts, shapes, 4 * piece * columns, [turned])


def vectors_kernel(up_ref, down_ref, proj_ref, mine_ref, theirs_ref, out_ref):
    width = down_ref.shape[1]
    sides = mine_ref[...] + theirs_ref[...]
    out_ref[...] = jnp.zeros_like(out_ref)
    out_ref[0:1, :] = up_ref[...]
    for k in range(2):
        out_ref[1 + k : 2 + k, :width] = sides[2 * k : 2 * k + 1]
        out_ref[1 + k : 2 + k, width:] = sides[2 * k + 1 : 2 * k + 2]
    out_ref[3:4, :width] = sides[4:5]
    out_ref[3:4, width:] = down_ref[...]
    out_ref[4:5, : proj_ref.shape[1]] = proj_ref[...]


def gather_vectors(up, down, proj, mine, theirs):
    args = (up, down, proj, mine, theirs)
    return call_once(vectors_kernel, args, (full(8, up.shape[1]),), up.size)[0]


def part_of(ref, index, count):
    start = index * count
    return ref[pl.ds(start if isinstance(start, int) else pl.multiple_of(start, count), count), :]


def cut_kernel(*refs, bits):
    plane = lax.axis_index("context")
    outs = refs[2 * len(bits) :]
    for k, bit in enumerate(bits):
        left, right = refs[2 * k], refs[2 * k + 1]
        index = plane % 2 if bit == 1 else plane // 2
        count = left.shape[0] // 2
        for out, half in ((outs[2 * k], index), (outs[2 * k + 1], 1 - index)):
            out[...] = part_of(left, half, count) + part_of(right, half, count)


def cut_sums(*pairs):
    args = [array for left, right, _ in pairs for array in (left, right)]
    shapes = [low(left.shape[0] // 2, left.shape[1]) for left, _, _ in pairs for _ in range(2)]
    kernel = functools.partial(cut_kernel, bits=tuple(bit for _, _, bit in pairs))
    return call_once(kernel, args, shapes, sum(a.size for a in args))


def glue_kernel(mine_ref, theirs_ref, left_ref, right_ref, glued_ref, sum_ref):
    second = lax.axis_index("context") // 2
    count = mine_ref.shape[0]
    for ref, index in ((mine_ref, second), (theirs_ref, 1 - second)):
        glued_ref[pl.ds(pl.multiple_of(index * count, count), count), :] = ref[...]
    sum_ref[...] = left_ref[...] + right_ref[...]


def glue_and_add(mine, theirs, left, right):
    shapes = (low(2 * mine.shape[0], mine.shape[1]), low(*left.shape))
    return call_once(glue_kernel, (mine, theirs, left, right), shapes, left.size)


def add_cut_kernel(a_ref, b_ref, left_ref, right_ref, sum_ref, keep_ref, send_ref):
    sum_ref[...] = a_ref[...] + b_ref[...]
    cut_kernel(left_ref, right_ref, keep_ref, send_ref, bits=(2,))


def add_and_cut(a, b, left, right):
    part = low(left.shape[0] // 2, left.shape[1])
    shapes = (low(*a.shape), part, part)
    return call_once(add_cut_kernel, (a, b, left, right), shapes, 2 * a.size)


def exchange(value, bit):
    size = lax.axis_size("dp")
    return lax.ppermute(value, "dp", [(i, i ^ bit) for i in range(size)])


def swap_tensor(value):
    return lax.ppermute(value, "tensor", [(0, 1), (1, 0)])


def together(*values):
    return lax.optimization_barrier(values)


def route(value, step, inward):
    pairs = []
    for far in range(2):
        for near in range(2):
            for plane in range(4):
                home = (2 * far + near) * 4 + plane
                away = (2 * far + plane // 2) * 4 + 2 * near + (step ^ (plane % 2))
                pairs.append((away, home) if inward else (home, away))
    return lax.ppermute(value, ("dp", "context"), pairs)


def pick_in(array, odd, upper):
    mine = jnp.where(upper, array[:, 1], array[:, 0])
    return [jnp.where(odd, mine[1 - step], mine[step]) for step in range(2)]


def join_out(near, far, odd, upper):
    arranged = [jnp.where(odd, jnp.stack(v[::-1]), jnp.stack(v)) for v in (near, far)]
    own, peer = arranged
    return jnp.where(upper, jnp.stack([peer, own], axis=1), jnp.stack([own, peer], axis=1))


def join_shares(mine, theirs, odd, upper):
    total = lambda a, b: a.astype(jnp.float32) + b[::-1].astype(jnp.float32)
    values = [total(a, b).astype(jnp.bfloat16) for a, b in zip(mine, theirs)]
    arranged = jnp.where(odd, jnp.stack(values[::-1]), jnp.stack(values))
    return jnp.where(upper, arranged[:, ::-1], arranged)


def gathered(shard, far_shard):
    return (shard, exchange(shard, 1), far_shard, exchange(far_shard, 1))


def turn_planes(value, step):
    return lax.ppermute(value, "context", [(i, (i + step) % 4) for i in range(4)])


def swap_planes(value, bit):
    return lax.ppermute(value, "context", [(i, i ^ bit) for i in range(4)])


def stack_rows(mine, theirs, second):
    return jnp.where(
        second, jnp.concatenate([theirs, mine], axis=0), jnp.concatenate([mine, theirs], axis=0)
    )


def per_device_planes(
    tokens,
    lengths,
    ln1_gain,
    ln1_bias,
    w_query,
    b_query,
    w_key,
    w_value,
    b_value,
    w_out,
    b_out,
    ln2_gain,
    ln2_bias,
    w_up,
    b_up,
    w_down,
    b_down,
    cotangent,
):
    block, width = tokens.shape[1:]
    half = block // 2
    local_width = w_query.shape[1]
    member = lax.axis_index("dp")
    near = member % 2
    plane = lax.axis_index("context")
    side = lax.axis_index("tensor")
    odd = plane % 2 == 1
    upper = side == 1
    upper_half = plane >= 2
    row = lambda vector: vector.reshape(1, -1)

    by_half = (2, 2, half, width)
    groups = local_width // (2 * HEAD_DIM)
    picked = pick_in(tokens.reshape(by_half), odd, upper)
    *picked, w_query, w_key, w_value = together(*picked, w_query, w_key, w_value)
    rows_parts = [route(picked[step], step, True) for step in range(2)]
    proj_own = jnp.concatenate([w_query, w_key, w_value], axis=1)
    proj_far = exchange(proj_own, 2)
    proj_near = exchange(proj_own, 1)
    out_own = w_out.T
    out_peer = swap_tensor(out_own)
    lengths_other = exchange(lengths, 1)
    down_own = w_down.T
    *rows_parts, proj_far, proj_near, out_peer, lengths_other, down_own, cotangent = together(
        *rows_parts, proj_far, proj_near, out_peer, lengths_other, down_own, cotangent
    )

    rows_parts += [swap_tensor(v) for v in rows_parts]
    rows_parts[2], lengths, lengths_other = together(rows_parts[2], lengths, lengths_other)
    lengths_near = jnp.where(plane // 2 == near, lengths, lengths_other)
    length = jnp.where(odd, lengths_near[1], lengths_near[0])
    index = jnp.arange(9, dtype=jnp.int32)
    quarter = index % 4
    core = jnp.where(index < 4, near, 1 - near)
    piece = jnp.where(quarter < 2, side, 1 - side)
    starts = (2 * core + (quarter % 2 ^ plane % 2)) * block + piece * half
    info = jnp.where(index < 8, starts, length)
    proj_last = exchange(proj_far, 1)
    down_far = exchange(down_own, 2)
    pack_own = jnp.concatenate([w_up, out_own, out_peer], axis=1)
    top_picked = pick_in(cotangent.reshape(by_half), odd, upper)
    top_parts = [route(top_picked[step], step, True) for step in range(2)]
    *rows_parts, proj_last, down_far, pack_own, info, top_0, top_1 = together(
        *rows_parts, proj_last, down_far, pack_own, info, *top_parts
    )

    pack_far = exchange(pack_own, 2)
    top_parts = [top_0, top_1, swap_tensor(top_0), swap_tensor(top_1)]
    proj_blocks = (proj_own, proj_near, proj_far, proj_last)
    rows_low, normed_low, queries, pair_own, proj = enter(
        rows_parts, row(ln1_gain), row(ln1_bias), row(b_query), row(b_value), proj_blocks
    )
    pair_other = exchange(pair_own, 1)
    mixed, logs = attend(info, queries, pair_own, pair_other)

    mixed, down_own, down_far, pack_own, *top_parts = together(
        mixed, down_own, down_far, pack_own, *top_parts
    )
    mixed_peer = swap_tensor(mixed)
    down_blocks = gathered(down_own, down_far)
    pack_near = exchange(pack_own, 1)
    mixed_peer, pack_near, pack_far, *down_blocks = together(
        mixed_peer, pack_near, pack_far, *down_blocks
    )
    pack_blocks = (pack_own, pack_near, pack_far, exchange(pack_far, 1))
    (
        middle,
        normed_two,
        d_feed,
        hidden,
        d_pre,
        d_own,
        d_peer,
        *shares,
        out_t,
        grad_up_bias,
        grad_down_bias,
    ) = middle_part(
        info,
        rows_low,
        mixed,
        mixed_peer,
        top_parts,
        row(ln2_gain),
        row(ln2_bias),
        row(b_out),
        pack_blocks,
        down_blocks,
        row(b_up),
        row(b_down),
    )

    got = swap_tensor(d_peer)
    down_own, down_far, down_send = weight_grad((d_feed, hidden))
    up_own, up_far, up_send = weight_grad((normed_two, d_pre))
    got, down_send, up_send, *shares = together(got, down_send, up_send, *shares)

    down_got = exchange(down_send, 1)
    d_middle, d_att, sums_two = turn(info, middle, d_own, got, top_parts[:2], row(ln2_gain))
    d_att, down_got, up_send, *shares = together(d_att, down_got, up_send, *shares)

    shard = down_own.shape[0]
    columns = hidden.shape[1]
    d_att_peer = swap_tensor(d_att)
    got_1 = exchange(down_far + down_got[shard:], 2)
    down_own = down_own + down_got[:shard]
    up_got = exchange(up_send, 1)
    share_0 = route(shares[0], 0, False)
    up_own, up_far = up_own + up_got[:shard], up_far + up_got[shard:]
    d_att_peer, got_1, up_own, up_far, share_0, share_1 = together(
        d_att_peer, got_1, up_own, up_far, share_0, shares[1]
    )

    half_1, sent = cut_sums((down_own, got_1, 1))
    got_1 = swap_planes(sent, 1)
    got_2 = exchange(up_far, 2)
    share_1 = route(share_1, 1, False)
    d_queries, d_pair, d_send = attend_back(
        info, queries, pair_own, pair_other, mixed, d_att, d_att_peer, out_t, logs
    )
    d_send, got_1, got_2, share_0, share_1 = together(d_send, got_1, got_2, share_0, share_1)


    d_got = exchange(d_send, 1)
    quarter_1, sent_1, half_2, sent_2 = cut_sums((half_1, got_1, 2), (up_own, got_2, 1))
    got_1 = swap_planes(sent_1, 2)
    got_2 = swap_planes(sent_2, 1)
    d_proj, one_own, one_peer, sides, proj_bias = leave(
        rows_low, proj, d_queries, d_pair, d_got, sums_two
    )
    own, far, send = weight_grad((normed_low, d_proj), (d_att, d_att_peer, mixed))
    one_peer, sides, send, got_1, got_2 = together(one_peer, sides, send, got_1, got_2)

    quarter_1, quarter_2, sent = add_and_cut(quarter_1, got_1, half_2, got_2)
    got_1 = swap_planes(quarter_1, 2)
    got_2 = swap_planes(sent, 2)
    sides_got = swap_tensor(sides)
    one_got = swap_tensor(one_peer)
    send_got = exchange(send, 1)
    send_got, one_got, got_1, got_2, sides_got = together(
        send_got, one_got, got_1, got_2, sides_got
    )

    vectors = gather_vectors(grad_up_bias, grad_down_bias, proj_bias, sides, sides_got)
    vectors_got = exchange(vectors, 1)
    input_rows = finish(rows_low, one_own, one_got, row(ln1_gain), d_middle)
    *input_rows, vectors_got, share_0, share_1 = together(
        *input_rows, vectors_got, share_0, share_1
    )

    packet, packet_far = merge(own, far, send_got, vectors, vectors_got)
    packet_got = exchange(packet_far, 2)
    share_got = [swap_tensor(share_0)]
    in_near = [route(input_rows[step], step, False) for step in range(2)]
    half_1, quarter_2 = glue_and_add(quarter_1, got_1, quarter_2, got_2)
    got_1 = swap_planes(half_1, 1)
    got_2 = swap_planes(quarter_2, 2)
    packet_got, got_1, got_2, share_1, *pieces = together(
        packet_got, got_1, got_2, share_1, *in_near, *share_got
    )
    in_near, share_got = pieces[:2], pieces[2:]

    quarters = spread(packet, packet_got, shard)
    arrived = [turn_planes(quarters[step], step) for step in range(1, 4)]
    in_far = [swap_tensor(v) for v in in_near]
    share_got.append(swap_tensor(share_1))
    half_2 = stack_rows(quarter_2, got_2, upper_half)
    got_2 = swap_planes(half_2, 1)
    arrived[0], half_1, got_1 = together(arrived[0], half_1, got_1)
    grad_down = stack_rows(half_1, got_1, odd).astype(jnp.float32).T
    *pieces, got_2 = together(quarters[0], *arrived, *in_far, *share_got, got_2)

    in_far, share_got = pieces[4:6], pieces[6:]
    quarter, vectors = total(pieces[:4], shard // 4, vectors.shape[0])
    quarters = [quarter] + [turn_planes(quarter, step) for step in range(1, 4)]
    input_grad = join_out(in_near, in_far, odd, upper)
    output = join_shares((share_0, share_1), share_got, odd, upper)
    grad_up = stack_rows(half_2, got_2, odd).astype(jnp.float32)
    *quarters, input_grad, output, grad_up, grad_down = together(
        *quarters, input_grad, output, grad_up, grad_down
    )
    grad_query, grad_key, grad_value, grad_out = assemble(quarters)
    return (
        output.reshape(tokens.shape),
        input_grad.reshape(tokens.shape),
        vectors[1, :width],
        vectors[1, width:],
        grad_query,
        vectors[4, :local_width],
        grad_key,
        grad_value,
        vectors[4, 2 * local_width : 3 * local_width],
        grad_out,
        vectors[3, :width],
        vectors[2, :width],
        vectors[2, width:],
        grad_up,
        vectors[0],
        grad_down,
        vectors[3, width:],
    )


def pick(mesh):
    sizes = mesh.shape
    planes = sizes["dp"] == 4 and sizes["context"] == 4 and sizes["tensor"] == 2
    return per_device_planes if planes else per_device_general


def solution(mesh):
    return jax.shard_map(
        pick(mesh),
        mesh=mesh,
        in_specs=(
            P("dp", "context", None),
            P("dp"),
            P(),
            P(),
            P("dp", "tensor"),
            P("tensor"),
            P("dp", "tensor"),
            P("dp", "tensor"),
            P("tensor"),
            P("tensor", "dp"),
            P(),
            P(),
            P(),
            P("dp", "tensor"),
            P("tensor"),
            P("tensor", "dp"),
            P(),
            P("dp", "context", None),
        ),
        out_specs=(
            P("dp", "context", None),
            P("dp", "context", None),
            P(),
            P(),
            P("dp", "tensor"),
            P("tensor"),
            P("dp", "tensor"),
            P("dp", "tensor"),
            P("tensor"),
            P("tensor", "dp"),
            P(),
            P(),
            P(),
            P("dp", "tensor"),
            P("tensor"),
            P("tensor", "dp"),
            P(),
        ),
        check_vma=False,
    )
```
